256 devices in a mesh: dp: 32 (over z, x_lo, core), chan: 8 (over y, x_hi).
Axes of the slice: x: 4 (x_hi: 2, x_lo: 2; x = x_hi * 2 + x_lo), y: 4, z: 8, core: 2. Of those that a mesh axis runs over, the one named last changes fastest.
Arguments:
- inputs: bfloat16 [32, 2048, 1152], P('dp', 'chan'), may hold values from -6 to 6
- weight: bfloat16 [2048, 9, 256], P('chan'), may hold values from -0.046875 to 0.046875
- cotangent: bfloat16 [32, 256, 1152], P('dp', 'chan'), may hold values from -6 to 6
Outputs:
- result: bfloat16 [32, 256, 1152], P('dp', 'chan')
- input_grad: bfloat16 [32, 2048, 1152], P('dp', 'chan')
- weight_grad: float32 [2048, 9, 256], P('chan')
The draws below stay inside these ranges and needn't reach their ends.
All inputs are finite; a program needn't handle non-finite values.
Results may differ from the reference program's by a relative error of at most 0.001.
Values may be sent and summed in bfloat16 or wider, within the bound.
A program may use at most 64 MiB of HBM per device.

```python
import jax
import jax.numpy as jnp
from jax import lax

CIN = 2048
COUT = 256
DILATION_RATE = 12
KERNEL_TAPS = 9
MAP_HEIGHT = 16
MAP_WIDTH = 72
HW = 1152
BATCH = 32


def levels(own_key, shape, shards, low, largest):
    def one(dim, blocks):
        draws = jax.random.uniform(jax.random.fold_in(jax.random.fold_in(own_key, 6), dim), (blocks,), jnp.float32, low / len(shards), largest / len(shards))
        return jnp.repeat(jnp.exp(draws), shape[dim] // blocks).reshape((-1,) + (1,) * (len(shape) - dim - 1))

    gain = one(*shards[0])
    for cut in shards[1:]:
        gain = gain * one(*cut)
    return gain


def centred(stream_key, dims, scale, reach, pieces=(), dtype=jnp.bfloat16):
    entries = scale * jax.random.normal(stream_key, dims, jnp.float32)
    if pieces:
        entries = entries * levels(stream_key, dims, pieces, -0.22, 0.18)
    return jnp.clip(entries, -reach, reach).astype(dtype)


def setup_inputs(seed: int = 0) -> dict:
    key_list = jax.random.split(jax.random.key(seed), 4)
    inputs = centred(key_list[0], (BATCH, CIN, HW), 1.0, 6.0, ((0, 32), (1, 8)))
    weight = centred(key_list[1], (CIN, KERNEL_TAPS, COUT), (CIN * KERNEL_TAPS) ** -0.5, 0.046875, ((0, 8),))
    cotangent = centred(key_list[2], (BATCH, COUT, HW), 1.0, 6.0, ((0, 32), (1, 8)))
    return {"inputs": inputs, "weight": weight, "cotangent": cotangent}


def translated_input(receptive_field, row_shift, column_shift):
    bordered_input = jnp.pad(receptive_field, ((0, 0), (DILATION_RATE, DILATION_RATE), (DILATION_RATE, DILATION_RATE)))
    return bordered_input[:, DILATION_RATE + row_shift:DILATION_RATE + row_shift + MAP_HEIGHT, DILATION_RATE + column_shift:DILATION_RATE + column_shift + MAP_WIDTH]


def reference(inputs, weight, cotangent):
    tap_shifts = [(DILATION_RATE * (tap_index // 3 - 1), DILATION_RATE * (tap_index % 3 - 1)) for tap_index in range(KERNEL_TAPS)]

    def one_sample(carry, sample):
        feature_flat, grads_flat = sample
        feature_map = feature_flat.reshape(CIN, MAP_HEIGHT, MAP_WIDTH)
        grads = grads_flat.reshape(COUT, MAP_HEIGHT, MAP_WIDTH)
        out_sum = jnp.zeros((COUT, MAP_HEIGHT * MAP_WIDTH), jnp.float32)
        back_sum = jnp.zeros((CIN, MAP_HEIGHT * MAP_WIDTH), jnp.float32)
        tap_grads = []
        for tap_index in range(KERNEL_TAPS):
            row_shift, column_shift = tap_shifts[tap_index]
            displaced_input = translated_input(feature_map, row_shift, column_shift).reshape(CIN, MAP_HEIGHT * MAP_WIDTH)
            out_sum = out_sum + jnp.dot(weight[:, tap_index, :].T, displaced_input, preferred_element_type=jnp.float32)
            displaced_gradient = translated_input(grads, -row_shift, -column_shift).reshape(COUT, MAP_HEIGHT * MAP_WIDTH)
            back_sum = back_sum + jnp.dot(weight[:, tap_index, :], displaced_gradient, preferred_element_type=jnp.float32)
            tap_grads.append(jnp.dot(displaced_input, grads_flat.T, preferred_element_type=jnp.float32))
        carry = carry + jnp.stack(tap_grads, axis=1)
        return carry, (out_sum.astype(jnp.bfloat16), back_sum.astype(jnp.bfloat16))

    start = jnp.zeros((CIN, KERNEL_TAPS, COUT), jnp.float32)
    total, (outs, backs) = lax.scan(one_sample, start, (inputs, cotangent))
    return (outs, backs, total / jnp.float32(BATCH))
```

```python
import functools

import jax
import jax.numpy as jnp
from jax import lax
from jax.experimental import pallas as pl
from jax.experimental.pallas import tpu as pltpu
from jax.sharding import PartitionSpec as P

DILATION_RATE = 12
MAP_HEIGHT = 16
MAP_WIDTH = 72


def translated_input(receptive_field, row_shift, column_shift, reach):
    height, width = (receptive_field.shape[1], receptive_field.shape[2])
    bordered_input = jnp.pad(receptive_field, ((0, 0), (reach, reach), (reach, reach)))
    return bordered_input[
        :,
        reach + row_shift : reach + row_shift + height,
        reach + column_shift : reach + column_shift + width,
    ]


def _allreduce_kernel(axis_names, nz, a_ref, o_ref, rc, s1, rx, s2, rp, rm, ap, am,
                      send_sems, recv_sems):
    rows, cols = a_ref.shape
    half = rows // 2
    quarter = half // 2
    chunk = quarter // nz
    lanes = cols // 2
    MESH = pl.DeviceIdType.MESH
    dp = lax.axis_index("dp")
    core = dp % 2
    xl = (dp // 2) % 2
    z = dp // 4
    nd = 4 * nz
    pc = dp + 1 - 2 * core
    px = dp + 2 - 4 * xl
    zr = (dp + 4) % nd
    zl = (dp + nd - 4) % nd

    def dev(p):
        return tuple(p if n == "dp" else lax.axis_index(n) for n in axis_names)

    barrier = pltpu.get_barrier_semaphore()
    for peer in (pc, px, zr, zl):
        pl.semaphore_signal(barrier, inc=1, device_id=dev(peer), device_id_type=MESH)
    pl.semaphore_wait(barrier, 4)

    sent = []
    counter = [0]

    def remote(src, dst, peer):
        k = counter[0]
        counter[0] += 1
        c = pltpu.make_async_remote_copy(
            src_ref=src, dst_ref=dst, send_sem=send_sems.at[k], recv_sem=recv_sems.at[k],
            device_id=dev(peer), device_id_type=MESH)
        c.start()
        sent.append(c)
        return c

    mine_c = pl.multiple_of(core * half, 8)
    other_c = pl.multiple_of((1 - core) * half, 8)
    c = remote(a_ref.at[pl.ds(other_c, half)], rc, pc)
    c.wait_recv()
    s1[...] = a_ref[pl.ds(mine_c, half), :] + rc[...]

    mine_x = pl.multiple_of(xl * quarter, 8)
    other_x = pl.multiple_of((1 - xl) * quarter, 8)
    c = remote(s1.at[pl.ds(other_x, quarter)], rx, px)
    c.wait_recv()
    s2[...] = s1[pl.ds(mine_x, quarter), :] + rx[...]

    def rows_of(j):
        return pl.ds(pl.multiple_of(j * chunk, 8), chunk)

    lo = pl.ds(0, lanes)
    hi = pl.ds(lanes, lanes)
    for s in range(nz - 1):
        jp = (z + 2 * nz - 1 - s) % nz
        jm = (z + 1 + s) % nz
        if s == 0:
            src_p = s2.at[rows_of(jp), lo]
            src_m = s2.at[rows_of(jm), hi]
        else:
            ap[s] = s2[rows_of(jp), lo] + rp[s - 1]
            am[s] = s2[rows_of(jm), hi] + rm[s - 1]
            src_p = ap.at[s]
            src_m = am.at[s]
        cp = remote(src_p, rp.at[s], zr)
        cm = remote(src_m, rm.at[s], zl)
        cp.wait_recv()
        cm.wait_recv()

    base = core * half + xl * quarter
    own = pl.ds(pl.multiple_of(base + z * chunk, 8), chunk)
    o_ref[own, lo] = s2[rows_of(z), lo] + rp[nz - 2]
    o_ref[own, hi] = s2[rows_of(z), hi] + rm[nz - 2]

    for s in range(nz - 1):
        jp = (z + nz - s) % nz
        jm = (z + s) % nz
        rp_rows = pl.ds(pl.multiple_of(base + jp * chunk, 8), chunk)
        rm_rows = pl.ds(pl.multiple_of(base + jm * chunk, 8), chunk)
        cp = remote(o_ref.at[rp_rows, lo], o_ref.at[rp_rows, lo], zr)
        cm = remote(o_ref.at[rm_rows, hi], o_ref.at[rm_rows, hi], zl)
        cp.wait_recv()
        cm.wait_recv()

    q_rows = pl.ds(pl.multiple_of(base, 8), quarter)
    c = remote(o_ref.at[q_rows], o_ref.at[q_rows], px)
    c.wait_recv()

    h_rows = pl.ds(pl.multiple_of(core * half, 8), half)
    c = remote(o_ref.at[h_rows], o_ref.at[h_rows], pc)
    c.wait_recv()

    for c in sent:
        c.wait_send()


def dp_allreduce(a, axis_names):
    rows, cols = a.shape
    nz = lax.axis_size("dp") // 4
    half = rows // 2
    quarter = half // 2
    chunk = quarter // nz
    lanes = cols // 2
    n_copies = 2 + 2 * (nz - 1) * 2 + 2
    vmem = pltpu.VMEM
    return pl.pallas_call(
        functools.partial(_allreduce_kernel, axis_names, nz),
        out_shape=jax.ShapeDtypeStruct((rows, cols), a.dtype),
        in_specs=[pl.BlockSpec(memory_space=vmem)],
        out_specs=pl.BlockSpec(memory_space=vmem),
        scratch_shapes=[
            vmem((half, cols), a.dtype),
            vmem((half, cols), a.dtype),
            vmem((quarter, cols), a.dtype),
            vmem((quarter, cols), a.dtype),
            vmem((nz - 1, chunk, lanes), a.dtype),
            vmem((nz - 1, chunk, lanes), a.dtype),
            vmem((nz - 1, chunk, lanes), a.dtype),
            vmem((nz - 1, chunk, lanes), a.dtype),
            pltpu.SemaphoreType.DMA((n_copies,)),
            pltpu.SemaphoreType.DMA((n_copies,)),
        ],
        compiler_params=pltpu.CompilerParams(
            collective_id=0, has_side_effects=True, vmem_limit_bytes=48 * 1024 * 1024
        ),
    )(a)


def on_device(axis_names, inputs, weight, cotangent):
    input_channels_local = inputs.shape[1]
    cout_local = cotangent.shape[1]
    tap_locations = MAP_HEIGHT * MAP_WIDTH
    feature_map = inputs[0].reshape(input_channels_local, MAP_HEIGHT, MAP_WIDTH)
    tap_list = weight.shape[1]
    output_channels_total = weight.shape[2]
    tap_shifts = [
        (DILATION_RATE * (tap_index // 3 - 1), DILATION_RATE * (tap_index % 3 - 1))
        for tap_index in range(tap_list)
    ]
    displaced_input = [
        translated_input(feature_map, first_operand, second_operand, DILATION_RATE).reshape(
            input_channels_local, tap_locations
        )
        for first_operand, second_operand in tap_shifts
    ]
    flat_grads = lax.all_gather(cotangent[0], "chan", axis=0, tiled=True)
    contract_cols = (((1,), (1,)), ((), ()))
    local_grad = jnp.stack(
        [
            lax.dot_general(
                displaced_input[tap_index],
                flat_grads,
                contract_cols,
                preferred_element_type=jnp.float32,
            )
            for tap_index in range(tap_list)
        ],
        axis=0,
    )
    summed = dp_allreduce(
        local_grad.reshape(tap_list * input_channels_local, output_channels_total), axis_names
    )
    summed_grad = jnp.transpose(
        summed.reshape(tap_list, input_channels_local, output_channels_total), (1, 0, 2)
    )
    weight_grad = summed_grad / jnp.float32(lax.axis_size("dp"))

    contract_rows = (((0,), (0,)), ((), ()))
    total = jnp.zeros((cout_local * lax.axis_size("chan"), tap_locations), jnp.float32)
    for tap_index in range(tap_list):
        columns = weight[:, tap_index, :]
        total = total + lax.dot_general(
            columns, displaced_input[tap_index], contract_rows, preferred_element_type=jnp.float32
        )
    owned = lax.psum_scatter(total, "chan", scatter_dimension=0, tiled=True)
    result = owned.astype(jnp.bfloat16).reshape(1, cout_local, tap_locations)
    collected_input = flat_grads.reshape(output_channels_total, MAP_HEIGHT, MAP_WIDTH)
    back_sum = jnp.zeros((input_channels_local, tap_locations), jnp.float32)
    for tap_index in range(tap_list):
        row_shift, column_shift = tap_shifts[tap_index]
        displaced_gradient = translated_input(
            collected_input, -row_shift, -column_shift, DILATION_RATE
        ).reshape(output_channels_total, tap_locations)
        back_sum = back_sum + jnp.dot(
            weight[:, tap_index, :], displaced_gradient, preferred_element_type=jnp.float32
        )
    input_grad = back_sum.astype(jnp.bfloat16).reshape(1, input_channels_local, tap_locations)
    return (result, input_grad, weight_grad)


def solution(mesh):
    placed = (P("dp", "chan", None), P("chan", None, None), P("dp", "chan", None))
    return jax.shard_map(
        functools.partial(on_device, tuple(mesh.axis_names)),
        mesh=mesh,
        in_specs=placed,
        out_specs=(P("dp", "chan", None), P("dp", "chan", None), P("chan", None, None)),
        check_vma=False,
    )
```

```python
import functools

import jax
import jax.numpy as jnp
from jax import lax
from jax.experimental import pallas as pl
from jax.experimental.pallas import tpu as pltpu
from jax.sharding import PartitionSpec as P

DILATION_RATE = 12
MAP_HEIGHT = 16
MAP_WIDTH = 72


def translated_input(receptive_field, row_shift, column_shift, reach):
    height, width = (receptive_field.shape[1], receptive_field.shape[2])
    bordered_input = jnp.pad(receptive_field, ((0, 0), (reach, reach), (reach, reach)))
    return bordered_input[
        :,
        reach + row_shift : reach + row_shift + height,
        reach + column_shift : reach + column_shift + width,
    ]


def _allreduce_kernel(axis_names, nz, a_ref, o_ref, rc, s1, rx, s2, rp, rm, ap, am,
                      send_sems, recv_sems):
    rows, cols = a_ref.shape
    half = rows // 2
    quarter = half // 2
    chunk = quarter // nz
    lanes = cols // 2
    MESH = pl.DeviceIdType.MESH
    dp = lax.axis_index("dp")
    core = dp % 2
    xl = (dp // 2) % 2
    z = dp // 4
    nd = 4 * nz
    pc = dp + 1 - 2 * core
    px = dp + 2 - 4 * xl
    zr = (dp + 4) % nd
    zl = (dp + nd - 4) % nd

    def dev(p):
        return tuple(p if n == "dp" else lax.axis_index(n) for n in axis_names)

    barrier = pltpu.get_barrier_semaphore()
    for peer in (pc, px, zr, zl):
        pl.semaphore_signal(barrier, inc=1, device_id=dev(peer), device_id_type=MESH)
    pl.semaphore_wait(barrier, 4)

    sent = []
    counter = [0]

    def remote(src, dst, peer):
        k = counter[0]
        counter[0] += 1
        c = pltpu.make_async_remote_copy(
            src_ref=src, dst_ref=dst, send_sem=send_sems.at[k], recv_sem=recv_sems.at[k],
            device_id=dev(peer), device_id_type=MESH)
        c.start()
        sent.append(c)
        return c

    mine_c = pl.multiple_of(core * half, 8)
    other_c = pl.multiple_of((1 - core) * half, 8)
    c = remote(a_ref.at[pl.ds(other_c, half)], rc, pc)
    c.wait_recv()
    s1[...] = a_ref[pl.ds(mine_c, half), :] + rc[...]

    mine_x = pl.multiple_of(xl * quarter, 8)
    other_x = pl.multiple_of((1 - xl) * quarter, 8)
    c = remote(s1.at[pl.ds(other_x, quarter)], rx, px)
    c.wait_recv()
    s2[...] = s1[pl.ds(mine_x, quarter), :] + rx[...]

    def rows_of(j):
        return pl.ds(pl.multiple_of(j * chunk, 8), chunk)

    lo = pl.ds(0, lanes)
    hi = pl.ds(lanes, lanes)
    for s in range(nz - 1):
        jp = (z + 2 * nz - 1 - s) % nz
        jm = (z + 1 + s) % nz
        if s == 0:
            src_p = s2.at[rows_of(jp), lo]
            src_m = s2.at[rows_of(jm), hi]
        else:
            ap[s] = s2[rows_of(jp), lo] + rp[s - 1]
            am[s] = s2[rows_of(jm), hi] + rm[s - 1]
            src_p = ap.at[s]
            src_m = am.at[s]
        cp = remote(src_p, rp.at[s], zr)
        cm = remote(src_m, rm.at[s], zl)
        cp.wait_recv()
        cm.wait_recv()

    base = core * half + xl * quarter
    own = pl.ds(pl.multiple_of(base + z * chunk, 8), chunk)
    o_ref[own, lo] = s2[rows_of(z), lo] + rp[nz - 2]
    o_ref[own, hi] = s2[rows_of(z), hi] + rm[nz - 2]

    for s in range(nz - 1):
        jp = (z + nz - s) % nz
        jm = (z + s) % nz
        rp_rows = pl.ds(pl.multiple_of(base + jp * chunk, 8), chunk)
        rm_rows = pl.ds(pl.multiple_of(base + jm * chunk, 8), chunk)
        cp = remote(o_ref.at[rp_rows, lo], o_ref.at[rp_rows, lo], zr)
        cm = remote(o_ref.at[rm_rows, hi], o_ref.at[rm_rows, hi], zl)
        cp.wait_recv()
        cm.wait_recv()

    q_rows = pl.ds(pl.multiple_of(base, 8), quarter)
    c = remote(o_ref.at[q_rows], o_ref.at[q_rows], px)
    c.wait_recv()

    h_rows = pl.ds(pl.multiple_of(core * half, 8), half)
    c = remote(o_ref.at[h_rows], o_ref.at[h_rows], pc)
    c.wait_recv()

    for c in sent:
        c.wait_send()


def dp_allreduce(a, axis_names):
    rows, cols = a.shape
    nz = lax.axis_size("dp") // 4
    half = rows // 2
    quarter = half // 2
    chunk = quarter // nz
    lanes = cols // 2
    n_copies = 2 + 2 * (nz - 1) * 2 + 2
    vmem = pltpu.VMEM
    return pl.pallas_call(
        functools.partial(_allreduce_kernel, axis_names, nz),
        out_shape=jax.ShapeDtypeStruct((rows, cols), a.dtype),
        in_specs=[pl.BlockSpec(memory_space=vmem)],
        out_specs=pl.BlockSpec(memory_space=vmem),
        scratch_shapes=[
            vmem((half, cols), a.dtype),
            vmem((half, cols), a.dtype),
            vmem((quarter, cols), a.dtype),
            vmem((quarter, cols), a.dtype),
            vmem((nz - 1, chunk, lanes), a.dtype),
            vmem((nz - 1, chunk, lanes), a.dtype),
            vmem((nz - 1, chunk, lanes), a.dtype),
            vmem((nz - 1, chunk, lanes), a.dtype),
            pltpu.SemaphoreType.DMA((n_copies,)),
            pltpu.SemaphoreType.DMA((n_copies,)),
        ],
        compiler_params=pltpu.CompilerParams(
            collective_id=0, has_side_effects=True, vmem_limit_bytes=48 * 1024 * 1024
        ),
    )(a)


def _allgather_kernel(axis_names, n, x_ref, o_ref, send_sems, recv_sems):
    rows = x_ref.shape[0]
    MESH = pl.DeviceIdType.MESH
    me = lax.axis_index("chan")

    def dev(p):
        return tuple(p if a == "chan" else lax.axis_index(a) for a in axis_names)

    barrier = pltpu.get_barrier_semaphore()
    for k in range(1, n):
        pl.semaphore_signal(barrier, inc=1, device_id=dev((me + k) % n), device_id_type=MESH)
    pl.semaphore_wait(barrier, n - 1)

    mine = pl.ds(pl.multiple_of(me * rows, 16), rows)
    copies = []
    for k in range(1, n):
        peer = (me + k) % n
        c = pltpu.make_async_remote_copy(
            src_ref=x_ref, dst_ref=o_ref.at[mine], send_sem=send_sems.at[k],
            recv_sem=recv_sems.at[k], device_id=dev(peer), device_id_type=MESH)
        c.start()
        copies.append(c)
    o_ref[mine, :] = x_ref[...]
    for k in range(1, n):
        src = (me + n - k) % n
        theirs = pl.ds(pl.multiple_of(src * rows, 16), rows)
        pltpu.make_async_remote_copy(
            src_ref=x_ref, dst_ref=o_ref.at[theirs], send_sem=send_sems.at[k],
            recv_sem=recv_sems.at[k], device_id=dev(src), device_id_type=MESH).wait_recv()
    for c in copies:
        c.wait_send()


def chan_allgather(x, axis_names):
    rows, cols = x.shape
    n = lax.axis_size("chan")
    vmem = pltpu.VMEM
    return pl.pallas_call(
        functools.partial(_allgather_kernel, axis_names, n),
        out_shape=jax.ShapeDtypeStruct((rows * n, cols), x.dtype),
        in_specs=[pl.BlockSpec(memory_space=vmem)],
        out_specs=pl.BlockSpec(memory_space=vmem),
        scratch_shapes=[pltpu.SemaphoreType.DMA((n,)), pltpu.SemaphoreType.DMA((n,))],
        compiler_params=pltpu.CompilerParams(collective_id=1, has_side_effects=True),
    )(x)


def on_device(axis_names, inputs, weight, cotangent):
    input_channels_local = inputs.shape[1]
    cout_local = cotangent.shape[1]
    tap_locations = MAP_HEIGHT * MAP_WIDTH
    feature_map = inputs[0].reshape(input_channels_local, MAP_HEIGHT, MAP_WIDTH)
    tap_list = weight.shape[1]
    output_channels_total = weight.shape[2]
    tap_shifts = [
        (DILATION_RATE * (tap_index // 3 - 1), DILATION_RATE * (tap_index % 3 - 1))
        for tap_index in range(tap_list)
    ]
    displaced_input = [
        translated_input(feature_map, first_operand, second_operand, DILATION_RATE).reshape(
            input_channels_local, tap_locations
        )
        for first_operand, second_operand in tap_shifts
    ]
    flat_grads = chan_allgather(cotangent[0], axis_names)
    contract_cols = (((1,), (1,)), ((), ()))
    local_grad = jnp.stack(
        [
            lax.dot_general(
                displaced_input[tap_index],
                flat_grads,
                contract_cols,
                preferred_element_type=jnp.float32,
            )
            for tap_index in range(tap_list)
        ],
        axis=0,
    )
    summed = dp_allreduce(
        local_grad.reshape(tap_list * input_channels_local, output_channels_total), axis_names
    )
    summed_grad = jnp.transpose(
        summed.reshape(tap_list, input_channels_local, output_channels_total), (1, 0, 2)
    )
    weight_grad = summed_grad / jnp.float32(lax.axis_size("dp"))

    contract_rows = (((0,), (0,)), ((), ()))
    total = jnp.zeros((cout_local * lax.axis_size("chan"), tap_locations), jnp.float32)
    for tap_index in range(tap_list):
        columns = weight[:, tap_index, :]
        total = total + lax.dot_general(
            columns, displaced_input[tap_index], contract_rows, preferred_element_type=jnp.float32
        )
    owned = lax.psum_scatter(total, "chan", scatter_dimension=0, tiled=True)
    result = owned.astype(jnp.bfloat16).reshape(1, cout_local, tap_locations)
    collected_input = flat_grads.reshape(output_channels_total, MAP_HEIGHT, MAP_WIDTH)
    back_sum = jnp.zeros((input_channels_local, tap_locations), jnp.float32)
    for tap_index in range(tap_list):
        row_shift, column_shift = tap_shifts[tap_index]
        displaced_gradient = translated_input(
            collected_input, -row_shift, -column_shift, DILATION_RATE
        ).reshape(output_channels_total, tap_locations)
        back_sum = back_sum + jnp.dot(
            weight[:, tap_index, :], displaced_gradient, preferred_element_type=jnp.float32
        )
    input_grad = back_sum.astype(jnp.bfloat16).reshape(1, input_channels_local, tap_locations)
    return (result, input_grad, weight_grad)


def solution(mesh):
    placed = (P("dp", "chan", None), P("chan", None, None), P("dp", "chan", None))
    return jax.shard_map(
        functools.partial(on_device, tuple(mesh.axis_names)),
        mesh=mesh,
        in_specs=placed,
        out_specs=(P("dp", "chan", None), P("dp", "chan", None), P("chan", None, None)),
        check_vma=False,
    )
```

```python
import functools

import jax
import jax.numpy as jnp
from jax import lax
from jax.experimental import pallas as pl
from jax.experimental.pallas import tpu as pltpu
from jax.sharding import PartitionSpec as P

DILATION_RATE = 12
MAP_HEIGHT = 16
MAP_WIDTH = 72


def translated_input(receptive_field, row_shift, column_shift, reach):
    height, width = (receptive_field.shape[1], receptive_field.shape[2])
    bordered_input = jnp.pad(receptive_field, ((0, 0), (reach, reach), (reach, reach)))
    return bordered_input[
        :,
        reach + row_shift : reach + row_shift + height,
        reach + column_shift : reach + column_shift + width,
    ]


def _allreduce_kernel(axis_names, nz, a_ref, o_ref, rc, s1, f1, rx, rp, rm, ap, am,
                      send_sems, recv_sems):
    rows, cols = a_ref.shape
    half = rows // 2
    chunk = half // nz
    lanes = cols // 2
    MESH = pl.DeviceIdType.MESH
    dp = lax.axis_index("dp")
    core = dp % 2
    xl = (dp // 2) % 2
    z = dp // 4
    nd = 4 * nz
    pc = dp + 1 - 2 * core
    px = dp + 2 - 4 * xl
    zr = (dp + 4) % nd
    zl = (dp + nd - 4) % nd

    def dev(p):
        return tuple(p if n == "dp" else lax.axis_index(n) for n in axis_names)

    barrier = pltpu.get_barrier_semaphore()
    for peer in (pc, px, zr, zl):
        pl.semaphore_signal(barrier, inc=1, device_id=dev(peer), device_id_type=MESH)
    pl.semaphore_wait(barrier, 4)

    sent = []
    counter = [0]

    def remote(src, dst, peer):
        k = counter[0]
        counter[0] += 1
        c = pltpu.make_async_remote_copy(
            src_ref=src, dst_ref=dst, send_sem=send_sems.at[k], recv_sem=recv_sems.at[k],
            device_id=dev(peer), device_id_type=MESH)
        c.start()
        sent.append(c)
        return c

    mine_c = pl.multiple_of(core * half, 8)
    other_c = pl.multiple_of((1 - core) * half, 8)
    c = remote(a_ref.at[pl.ds(other_c, half)], rc, pc)
    c.wait_recv()
    s1[...] = a_ref[pl.ds(mine_c, half), :] + rc[...]

    def rows_of(j):
        return pl.ds(pl.multiple_of(j * chunk, 8), chunk)

    lo = pl.ds(0, lanes)
    hi = pl.ds(lanes, lanes)
    for s in range(nz - 1):
        jp = (z + 2 * nz - 1 - s) % nz
        jm = (z + 1 + s) % nz
        if s == 0:
            src_p = s1.at[rows_of(jp), lo]
            src_m = s1.at[rows_of(jm), hi]
        else:
            ap[s] = s1[rows_of(jp), lo] + rp[s - 1]
            am[s] = s1[rows_of(jm), hi] + rm[s - 1]
            src_p = ap.at[s]
            src_m = am.at[s]
        cp = remote(src_p, rp.at[s], zr)
        cm = remote(src_m, rm.at[s], zl)
        cp.wait_recv()
        cm.wait_recv()
    f1[:, lo] = s1[rows_of(z), lo] + rp[nz - 2]
    f1[:, hi] = s1[rows_of(z), hi] + rm[nz - 2]

    piece = chunk // 2
    mine_x = pl.multiple_of(xl * piece, 8)
    other_x = pl.multiple_of((1 - xl) * piece, 8)
    c = remote(f1.at[pl.ds(other_x, piece)], rx, px)
    c.wait_recv()
    base = core * half + z * chunk
    own = pl.ds(pl.multiple_of(base + xl * piece, 8), piece)
    o_ref[own, :] = f1[pl.ds(mine_x, piece), :] + rx[...]

    c = remote(o_ref.at[own], o_ref.at[own], px)
    c.wait_recv()

    for s in range(nz - 1):
        jp = (z + nz - s) % nz
        jm = (z + s) % nz
        rp_rows = pl.ds(pl.multiple_of(core * half + jp * chunk, 8), chunk)
        rm_rows = pl.ds(pl.multiple_of(core * half + jm * chunk, 8), chunk)
        cp = remote(o_ref.at[rp_rows, lo], o_ref.at[rp_rows, lo], zr)
        cm = remote(o_ref.at[rm_rows, hi], o_ref.at[rm_rows, hi], zl)
        cp.wait_recv()
        cm.wait_recv()

    h_rows = pl.ds(pl.multiple_of(core * half, 8), half)
    c = remote(o_ref.at[h_rows], o_ref.at[h_rows], pc)
    c.wait_recv()

    for c in sent:
        c.wait_send()


def dp_allreduce(a, axis_names):
    rows, cols = a.shape
    nz = lax.axis_size("dp") // 4
    half = rows // 2
    chunk = half // nz
    lanes = cols // 2
    n_copies = 2 + 2 * (nz - 1) * 2 + 2
    vmem = pltpu.VMEM
    return pl.pallas_call(
        functools.partial(_allreduce_kernel, axis_names, nz),
        out_shape=jax.ShapeDtypeStruct((rows, cols), a.dtype),
        in_specs=[pl.BlockSpec(memory_space=vmem)],
        out_specs=pl.BlockSpec(memory_space=vmem),
        scratch_shapes=[
            vmem((half, cols), a.dtype),
            vmem((half, cols), a.dtype),
            vmem((chunk, cols), a.dtype),
            vmem((chunk // 2, cols), a.dtype),
            vmem((nz - 1, chunk, lanes), a.dtype),
            vmem((nz - 1, chunk, lanes), a.dtype),
            vmem((nz - 1, chunk, lanes), a.dtype),
            vmem((nz - 1, chunk, lanes), a.dtype),
            pltpu.SemaphoreType.DMA((n_copies,)),
            pltpu.SemaphoreType.DMA((n_copies,)),
        ],
        compiler_params=pltpu.CompilerParams(
            collective_id=0, has_side_effects=True, vmem_limit_bytes=48 * 1024 * 1024
        ),
    )(a)


def _allgather_kernel(axis_names, n, x_ref, o_ref, send_sems, recv_sems):
    rows = x_ref.shape[0]
    MESH = pl.DeviceIdType.MESH
    me = lax.axis_index("chan")

    def dev(p):
        return tuple(p if a == "chan" else lax.axis_index(a) for a in axis_names)

    barrier = pltpu.get_barrier_semaphore()
    for k in range(1, n):
        pl.semaphore_signal(barrier, inc=1, device_id=dev((me + k) % n), device_id_type=MESH)
    pl.semaphore_wait(barrier, n - 1)

    mine = pl.ds(pl.multiple_of(me * rows, 16), rows)
    copies = []
    for k in range(1, n):
        peer = (me + k) % n
        c = pltpu.make_async_remote_copy(
            src_ref=x_ref, dst_ref=o_ref.at[mine], send_sem=send_sems.at[k],
            recv_sem=recv_sems.at[k], device_id=dev(peer), device_id_type=MESH)
        c.start()
        copies.append(c)
    o_ref[mine, :] = x_ref[...]
    for k in range(1, n):
        src = (me + n - k) % n
        theirs = pl.ds(pl.multiple_of(src * rows, 16), rows)
        pltpu.make_async_remote_copy(
            src_ref=x_ref, dst_ref=o_ref.at[theirs], send_sem=send_sems.at[k],
            recv_sem=recv_sems.at[k], device_id=dev(src), device_id_type=MESH).wait_recv()
    for c in copies:
        c.wait_send()


def chan_allgather(x, axis_names):
    rows, cols = x.shape
    n = lax.axis_size("chan")
    vmem = pltpu.VMEM
    return pl.pallas_call(
        functools.partial(_allgather_kernel, axis_names, n),
        out_shape=jax.ShapeDtypeStruct((rows * n, cols), x.dtype),
        in_specs=[pl.BlockSpec(memory_space=vmem)],
        out_specs=pl.BlockSpec(memory_space=vmem),
        scratch_shapes=[pltpu.SemaphoreType.DMA((n,)), pltpu.SemaphoreType.DMA((n,))],
        compiler_params=pltpu.CompilerParams(collective_id=1, has_side_effects=True),
    )(x)


def on_device(axis_names, inputs, weight, cotangent):
    input_channels_local = inputs.shape[1]
    cout_local = cotangent.shape[1]
    tap_locations = MAP_HEIGHT * MAP_WIDTH
    feature_map = inputs[0].reshape(input_channels_local, MAP_HEIGHT, MAP_WIDTH)
    tap_list = weight.shape[1]
    output_channels_total = weight.shape[2]
    tap_shifts = [
        (DILATION_RATE * (tap_index // 3 - 1), DILATION_RATE * (tap_index % 3 - 1))
        for tap_index in range(tap_list)
    ]
    displaced_input = [
        translated_input(feature_map, first_operand, second_operand, DILATION_RATE).reshape(
            input_channels_local, tap_locations
        )
        for first_operand, second_operand in tap_shifts
    ]
    flat_grads = chan_allgather(cotangent[0], axis_names)
    contract_cols = (((1,), (1,)), ((), ()))
    local_grad = jnp.stack(
        [
            lax.dot_general(
                displaced_input[tap_index],
                flat_grads,
                contract_cols,
                preferred_element_type=jnp.float32,
            )
            for tap_index in range(tap_list)
        ],
        axis=0,
    )
    summed = dp_allreduce(
        local_grad.reshape(tap_list * input_channels_local, output_channels_total), axis_names
    )
    summed_grad = jnp.transpose(
        summed.reshape(tap_list, input_channels_local, output_channels_total), (1, 0, 2)
    )
    weight_grad = summed_grad / jnp.float32(lax.axis_size("dp"))

    contract_rows = (((0,), (0,)), ((), ()))
    total = jnp.zeros((cout_local * lax.axis_size("chan"), tap_locations), jnp.float32)
    for tap_index in range(tap_list):
        columns = weight[:, tap_index, :]
        total = total + lax.dot_general(
            columns, displaced_input[tap_index], contract_rows, preferred_element_type=jnp.float32
        )
    owned = lax.psum_scatter(total, "chan", scatter_dimension=0, tiled=True)
    result = owned.astype(jnp.bfloat16).reshape(1, cout_local, tap_locations)
    collected_input = flat_grads.reshape(output_channels_total, MAP_HEIGHT, MAP_WIDTH)
    back_sum = jnp.zeros((input_channels_local, tap_locations), jnp.float32)
    for tap_index in range(tap_list):
        row_shift, column_shift = tap_shifts[tap_index]
        displaced_gradient = translated_input(
            collected_input, -row_shift, -column_shift, DILATION_RATE
        ).reshape(output_channels_total, tap_locations)
        back_sum = back_sum + jnp.dot(
            weight[:, tap_index, :], displaced_gradient, preferred_element_type=jnp.float32
        )
    input_grad = back_sum.astype(jnp.bfloat16).reshape(1, input_channels_local, tap_locations)
    return (result, input_grad, weight_grad)


def solution(mesh):
    placed = (P("dp", "chan", None), P("chan", None, None), P("dp", "chan", None))
    return jax.shard_map(
        functools.partial(on_device, tuple(mesh.axis_names)),
        mesh=mesh,
        in_specs=placed,
        out_specs=(P("dp", "chan", None), P("dp", "chan", None), P("chan", None, None)),
        check_vma=False,
    )
```

```python
import functools

import jax
import jax.numpy as jnp
from jax import lax
from jax.experimental import pallas as pl
from jax.experimental.pallas import tpu as pltpu
from jax.sharding import PartitionSpec as P

DILATION_RATE = 12
MAP_HEIGHT = 16
MAP_WIDTH = 72


def translated_input(receptive_field, row_shift, column_shift, reach):
    height, width = (receptive_field.shape[1], receptive_field.shape[2])
    bordered_input = jnp.pad(receptive_field, ((0, 0), (reach, reach), (reach, reach)))
    return bordered_input[
        :,
        reach + row_shift : reach + row_shift + height,
        reach + column_shift : reach + column_shift + width,
    ]


def _allreduce_kernel(axis_names, nz, nc, a_ref, t_ref, o_ref, res_ref, rc, s1, f1, rx, rp, rm,
                      ap, am, rs_buf, send_sems, recv_sems, rs_send, rs_recv):
    rows, cols = a_ref.shape
    half = rows // 2
    chunk = half // nz
    lanes = cols // 2
    MESH = pl.DeviceIdType.MESH
    dp = lax.axis_index("dp")
    core = dp % 2
    xl = (dp // 2) % 2
    z = dp // 4
    nd = 4 * nz
    pc = dp + 1 - 2 * core
    px = dp + 2 - 4 * xl
    zr = (dp + 4) % nd
    zl = (dp + nd - 4) % nd

    me = lax.axis_index("chan")

    def dev(p):
        return tuple(p if n == "dp" else lax.axis_index(n) for n in axis_names)

    def cdev(p):
        return tuple(p if n == "chan" else lax.axis_index(n) for n in axis_names)

    barrier = pltpu.get_barrier_semaphore()
    for peer in (pc, px, zr, zl):
        pl.semaphore_signal(barrier, inc=1, device_id=dev(peer), device_id_type=MESH)
    for k in range(1, nc):
        pl.semaphore_signal(barrier, inc=1, device_id=cdev((me + k) % nc), device_id_type=MESH)
    pl.semaphore_wait(barrier, 4 + nc - 1)

    owned = res_ref.shape[0]
    rs_copies = []
    for k in range(1, nc):
        peer = (me + k) % nc
        c = pltpu.make_async_remote_copy(
            src_ref=t_ref.at[pl.ds(pl.multiple_of(peer * owned, 8), owned)],
            dst_ref=rs_buf.at[k], send_sem=rs_send.at[k], recv_sem=rs_recv.at[k],
            device_id=cdev(peer), device_id_type=MESH)
        c.start()
        rs_copies.append(c)

    sent = []
    counter = [0]

    def remote(src, dst, peer):
        k = counter[0]
        counter[0] += 1
        c = pltpu.make_async_remote_copy(
            src_ref=src, dst_ref=dst, send_sem=send_sems.at[k], recv_sem=recv_sems.at[k],
            device_id=dev(peer), device_id_type=MESH)
        c.start()
        sent.append(c)
        return c

    mine_c = pl.multiple_of(core * half, 8)
    other_c = pl.multiple_of((1 - core) * half, 8)
    c = remote(a_ref.at[pl.ds(other_c, half)], rc, pc)
    c.wait_recv()
    s1[...] = a_ref[pl.ds(mine_c, half), :] + rc[...]

    def rows_of(j):
        return pl.ds(pl.multiple_of(j * chunk, 8), chunk)

    lo = pl.ds(0, lanes)
    hi = pl.ds(lanes, lanes)
    for s in range(nz - 1):
        jp = (z + 2 * nz - 1 - s) % nz
        jm = (z + 1 + s) % nz
        if s == 0:
            src_p = s1.at[rows_of(jp), lo]
            src_m = s1.at[rows_of(jm), hi]
        else:
            ap[s] = s1[rows_of(jp), lo] + rp[s - 1]
            am[s] = s1[rows_of(jm), hi] + rm[s - 1]
            src_p = ap.at[s]
            src_m = am.at[s]
        cp = remote(src_p, rp.at[s], zr)
        cm = remote(src_m, rm.at[s], zl)
        cp.wait_recv()
        cm.wait_recv()
    f1[:, lo] = s1[rows_of(z), lo] + rp[nz - 2]
    f1[:, hi] = s1[rows_of(z), hi] + rm[nz - 2]

    piece = chunk // 2
    mine_x = pl.multiple_of(xl * piece, 8)
    other_x = pl.multiple_of((1 - xl) * piece, 8)
    c = remote(f1.at[pl.ds(other_x, piece)], rx, px)
    c.wait_recv()
    base = core * half + z * chunk
    own = pl.ds(pl.multiple_of(base + xl * piece, 8), piece)
    o_ref[own, :] = f1[pl.ds(mine_x, piece), :] + rx[...]

    c = remote(o_ref.at[own], o_ref.at[own], px)
    c.wait_recv()

    for s in range(nz - 1):
        jp = (z + nz - s) % nz
        jm = (z + s) % nz
        rp_rows = pl.ds(pl.multiple_of(core * half + jp * chunk, 8), chunk)
        rm_rows = pl.ds(pl.multiple_of(core * half + jm * chunk, 8), chunk)
        cp = remote(o_ref.at[rp_rows, lo], o_ref.at[rp_rows, lo], zr)
        cm = remote(o_ref.at[rm_rows, hi], o_ref.at[rm_rows, hi], zl)
        cp.wait_recv()
        cm.wait_recv()

    h_rows = pl.ds(pl.multiple_of(core * half, 8), half)
    c = remote(o_ref.at[h_rows], o_ref.at[h_rows], pc)
    c.wait_recv()

    for c in rs_copies:
        c.wait_recv()
    acc = t_ref[pl.ds(pl.multiple_of(me * owned, 8), owned), :]
    for k in range(1, nc):
        acc = acc + rs_buf[k]
    res_ref[...] = acc.astype(res_ref.dtype)

    for c in sent + rs_copies:
        c.wait_send()


def dp_allreduce(a, t, axis_names):
    rows, cols = a.shape
    nc = lax.axis_size("chan")
    owned = t.shape[0] // nc
    nz = lax.axis_size("dp") // 4
    half = rows // 2
    chunk = half // nz
    lanes = cols // 2
    n_copies = 2 + 2 * (nz - 1) * 2 + 2
    vmem = pltpu.VMEM
    return pl.pallas_call(
        functools.partial(_allreduce_kernel, axis_names, nz, nc),
        out_shape=(
            jax.ShapeDtypeStruct((rows, cols), a.dtype),
            jax.ShapeDtypeStruct((owned, t.shape[1]), jnp.bfloat16),
        ),
        in_specs=[pl.BlockSpec(memory_space=vmem)] * 2,
        out_specs=(pl.BlockSpec(memory_space=vmem), pl.BlockSpec(memory_space=vmem)),
        scratch_shapes=[
            vmem((half, cols), a.dtype),
            vmem((half, cols), a.dtype),
            vmem((chunk, cols), a.dtype),
            vmem((chunk // 2, cols), a.dtype),
            vmem((nz - 1, chunk, lanes), a.dtype),
            vmem((nz - 1, chunk, lanes), a.dtype),
            vmem((nz - 1, chunk, lanes), a.dtype),
            vmem((nz - 1, chunk, lanes), a.dtype),
            vmem((nc, owned, t.shape[1]), t.dtype),
            pltpu.SemaphoreType.DMA((n_copies,)),
            pltpu.SemaphoreType.DMA((n_copies,)),
            pltpu.SemaphoreType.DMA((nc,)),
            pltpu.SemaphoreType.DMA((nc,)),
        ],
        compiler_params=pltpu.CompilerParams(
            collective_id=0, has_side_effects=True, vmem_limit_bytes=48 * 1024 * 1024
        ),
    )(a, t)


def _allgather_kernel(axis_names, n, x_ref, o_ref, send_sems, recv_sems):
    rows = x_ref.shape[0]
    MESH = pl.DeviceIdType.MESH
    me = lax.axis_index("chan")

    def dev(p):
        return tuple(p if a == "chan" else lax.axis_index(a) for a in axis_names)

    barrier = pltpu.get_barrier_semaphore()
    for k in range(1, n):
        pl.semaphore_signal(barrier, inc=1, device_id=dev((me + k) % n), device_id_type=MESH)
    pl.semaphore_wait(barrier, n - 1)

    mine = pl.ds(pl.multiple_of(me * rows, 16), rows)
    copies = []
    for k in range(1, n):
        peer = (me + k) % n
        c = pltpu.make_async_remote_copy(
            src_ref=x_ref, dst_ref=o_ref.at[mine], send_sem=send_sems.at[k],
            recv_sem=recv_sems.at[k], device_id=dev(peer), device_id_type=MESH)
        c.start()
        copies.append(c)
    o_ref[mine, :] = x_ref[...]
    for k in range(1, n):
        src = (me + n - k) % n
        theirs = pl.ds(pl.multiple_of(src * rows, 16), rows)
        pltpu.make_async_remote_copy(
            src_ref=x_ref, dst_ref=o_ref.at[theirs], send_sem=send_sems.at[k],
            recv_sem=recv_sems.at[k], device_id=dev(src), device_id_type=MESH).wait_recv()
    for c in copies:
        c.wait_send()


def chan_allgather(x, axis_names):
    rows, cols = x.shape
    n = lax.axis_size("chan")
    vmem = pltpu.VMEM
    return pl.pallas_call(
        functools.partial(_allgather_kernel, axis_names, n),
        out_shape=jax.ShapeDtypeStruct((rows * n, cols), x.dtype),
        in_specs=[pl.BlockSpec(memory_space=vmem)],
        out_specs=pl.BlockSpec(memory_space=vmem),
        scratch_shapes=[pltpu.SemaphoreType.DMA((n,)), pltpu.SemaphoreType.DMA((n,))],
        compiler_params=pltpu.CompilerParams(collective_id=1, has_side_effects=True),
    )(x)


def on_device(axis_names, inputs, weight, cotangent):
    input_channels_local = inputs.shape[1]
    cout_local = cotangent.shape[1]
    tap_locations = MAP_HEIGHT * MAP_WIDTH
    feature_map = inputs[0].reshape(input_channels_local, MAP_HEIGHT, MAP_WIDTH)
    tap_list = weight.shape[1]
    output_channels_total = weight.shape[2]
    tap_shifts = [
        (DILATION_RATE * (tap_index // 3 - 1), DILATION_RATE * (tap_index % 3 - 1))
        for tap_index in range(tap_list)
    ]
    displaced_input = [
        translated_input(feature_map, first_operand, second_operand, DILATION_RATE).reshape(
            input_channels_local, tap_locations
        )
        for first_operand, second_operand in tap_shifts
    ]
    flat_grads = chan_allgather(cotangent[0], axis_names)
    contract_cols = (((1,), (1,)), ((), ()))
    local_grad = jnp.stack(
        [
            lax.dot_general(
                displaced_input[tap_index],
                flat_grads,
                contract_cols,
                preferred_element_type=jnp.float32,
            )
            for tap_index in range(tap_list)
        ],
        axis=0,
    )
    contract_rows = (((0,), (0,)), ((), ()))
    total = jnp.zeros((cout_local * lax.axis_size("chan"), tap_locations), jnp.float32)
    for tap_index in range(tap_list):
        columns = weight[:, tap_index, :]
        total = total + lax.dot_general(
            columns, displaced_input[tap_index], contract_rows, preferred_element_type=jnp.float32
        )
    summed, owned = dp_allreduce(
        local_grad.reshape(tap_list * input_channels_local, output_channels_total), total, axis_names
    )
    result = owned.reshape(1, cout_local, tap_locations)
    summed_grad = jnp.transpose(
        summed.reshape(tap_list, input_channels_local, output_channels_total), (1, 0, 2)
    )
    weight_grad = summed_grad / jnp.float32(lax.axis_size("dp"))

    collected_input = flat_grads.reshape(output_channels_total, MAP_HEIGHT, MAP_WIDTH)
    back_sum = jnp.zeros((input_channels_local, tap_locations), jnp.float32)
    for tap_index in range(tap_list):
        row_shift, column_shift = tap_shifts[tap_index]
        displaced_gradient = translated_input(
            collected_input, -row_shift, -column_shift, DILATION_RATE
        ).reshape(output_channels_total, tap_locations)
        back_sum = back_sum + jnp.dot(
            weight[:, tap_index, :], displaced_gradient, preferred_element_type=jnp.float32
        )
    input_grad = back_sum.astype(jnp.bfloat16).reshape(1, input_channels_local, tap_locations)
    return (result, input_grad, weight_grad)


def solution(mesh):
    placed = (P("dp", "chan", None), P("chan", None, None), P("dp", "chan", None))
    return jax.shard_map(
        functools.partial(on_device, tuple(mesh.axis_names)),
        mesh=mesh,
        in_specs=placed,
        out_specs=(P("dp", "chan", None), P("dp", "chan", None), P("chan", None, None)),
        check_vma=False,
    )
```

```python
import functools

import jax
import jax.numpy as jnp
from jax import lax
from jax.experimental import pallas as pl
from jax.experimental.pallas import tpu as pltpu
from jax.sharding import PartitionSpec as P

DILATION_RATE = 12
MAP_HEIGHT = 16
MAP_WIDTH = 72


def translated_input(receptive_field, row_shift, column_shift, reach):
    height, width = (receptive_field.shape[1], receptive_field.shape[2])
    bordered_input = jnp.pad(receptive_field, ((0, 0), (reach, reach), (reach, reach)))
    return bordered_input[
        :,
        reach + row_shift : reach + row_shift + height,
        reach + column_shift : reach + column_shift + width,
    ]


def _allreduce_kernel(axis_names, nz, nc, a_ref, t_ref, o_ref, res_ref, rc, s1, f1, rx, rp, rm,
                      ap, am, rs_buf, send_sems, recv_sems, rs_send, rs_recv):
    rows, cols = a_ref.shape
    half = rows // 2
    chunk = half // nz
    lanes = cols // 2
    MESH = pl.DeviceIdType.MESH
    dp = lax.axis_index("dp")
    core = dp % 2
    xl = (dp // 2) % 2
    z = dp // 4
    nd = 4 * nz
    pc = dp + 1 - 2 * core
    px = dp + 2 - 4 * xl
    zr = (dp + 4) % nd
    zl = (dp + nd - 4) % nd

    me = lax.axis_index("chan")

    def dev(p):
        return tuple(p if n == "dp" else lax.axis_index(n) for n in axis_names)

    def cdev(p):
        return tuple(p if n == "chan" else lax.axis_index(n) for n in axis_names)

    barrier = pltpu.get_barrier_semaphore()
    for peer in (pc, px, zr, zl):
        pl.semaphore_signal(barrier, inc=1, device_id=dev(peer), device_id_type=MESH)
    for k in range(1, nc):
        pl.semaphore_signal(barrier, inc=1, device_id=cdev((me + k) % nc), device_id_type=MESH)
    pl.semaphore_wait(barrier, 4 + nc - 1)

    owned = res_ref.shape[0]
    rs_copies = []
    for k in range(1, nc):
        peer = (me + k) % nc
        c = pltpu.make_async_remote_copy(
            src_ref=t_ref.at[pl.ds(pl.multiple_of(peer * owned, 8), owned)],
            dst_ref=rs_buf.at[k], send_sem=rs_send.at[k], recv_sem=rs_recv.at[k],
            device_id=cdev(peer), device_id_type=MESH)
        c.start()
        rs_copies.append(c)

    sent = []
    counter = [0]

    def remote(src, dst, peer):
        k = counter[0]
        counter[0] += 1
        c = pltpu.make_async_remote_copy(
            src_ref=src, dst_ref=dst, send_sem=send_sems.at[k], recv_sem=recv_sems.at[k],
            device_id=dev(peer), device_id_type=MESH)
        c.start()
        sent.append(c)
        return c

    def rows_of(j):
        return pl.ds(pl.multiple_of(j * chunk, 8), chunk)

    mine_c = core * half
    other_c = (1 - core) * half
    order = []
    for d in range(1, nz // 2 + 1):
        order.append((z + nz - d) % nz)
        if 2 * d != nz:
            order.append((z + d) % nz)
    order.append(z)
    core_in = []
    for j in order:
        src_rows = pl.ds(pl.multiple_of(other_c + j * chunk, 8), chunk)
        core_in.append((j, remote(a_ref.at[src_rows], rc.at[rows_of(j)], pc)))
    ready = [0]

    def ready_upto(n):
        while ready[0] < n:
            j, c = core_in[ready[0]]
            c.wait_recv()
            own_rows = pl.ds(pl.multiple_of(mine_c + j * chunk, 8), chunk)
            s1[rows_of(j), :] = a_ref[own_rows, :] + rc[rows_of(j), :]
            ready[0] += 1

    def needed(d):
        return min(len(order) - 1, 2 * d - (1 if 2 * d == nz else 0))

    lo = pl.ds(0, lanes)
    hi = pl.ds(lanes, lanes)
    for s in range(nz - 1):
        jp = (z + 2 * nz - 1 - s) % nz
        jm = (z + 1 + s) % nz
        if s + 1 <= nz // 2:
            ready_upto(needed(s + 1))
        if s == 0:
            src_p = s1.at[rows_of(jp), lo]
            src_m = s1.at[rows_of(jm), hi]
        else:
            ap[s] = s1[rows_of(jp), lo] + rp[s - 1]
            am[s] = s1[rows_of(jm), hi] + rm[s - 1]
            src_p = ap.at[s]
            src_m = am.at[s]
        cp = remote(src_p, rp.at[s], zr)
        cm = remote(src_m, rm.at[s], zl)
        cp.wait_recv()
        cm.wait_recv()
    ready_upto(len(order))
    f1[:, lo] = s1[rows_of(z), lo] + rp[nz - 2]
    f1[:, hi] = s1[rows_of(z), hi] + rm[nz - 2]

    piece = chunk // 2
    mine_x = pl.multiple_of(xl * piece, 8)
    other_x = pl.multiple_of((1 - xl) * piece, 8)
    c = remote(f1.at[pl.ds(other_x, piece)], rx, px)
    c.wait_recv()
    base = core * half + z * chunk
    own = pl.ds(pl.multiple_of(base + xl * piece, 8), piece)
    o_ref[own, :] = f1[pl.ds(mine_x, piece), :] + rx[...]

    c = remote(o_ref.at[own], o_ref.at[own], px)
    c.wait_recv()

    own_chunk = pl.ds(pl.multiple_of(core * half + z * chunk, 8), chunk)
    to_core = [remote(o_ref.at[own_chunk], o_ref.at[own_chunk], pc)]
    for s in range(nz - 1):
        jp = (z + nz - s) % nz
        jm = (z + s) % nz
        rp_rows = pl.ds(pl.multiple_of(core * half + jp * chunk, 8), chunk)
        rm_rows = pl.ds(pl.multiple_of(core * half + jm * chunk, 8), chunk)
        cp = remote(o_ref.at[rp_rows, lo], o_ref.at[rp_rows, lo], zr)
        cm = remote(o_ref.at[rm_rows, hi], o_ref.at[rm_rows, hi], zl)
        cp.wait_recv()
        cm.wait_recv()
        gp = pl.ds(pl.multiple_of(core * half + ((jp + nz - 1) % nz) * chunk, 8), chunk)
        gm = pl.ds(pl.multiple_of(core * half + ((jm + 1) % nz) * chunk, 8), chunk)
        to_core.append(remote(o_ref.at[gp, lo], o_ref.at[gp, lo], pc))
        to_core.append(remote(o_ref.at[gm, hi], o_ref.at[gm, hi], pc))
    for c in to_core:
        c.wait_recv()

    for c in rs_copies:
        c.wait_recv()
    acc = t_ref[pl.ds(pl.multiple_of(me * owned, 8), owned), :]
    for k in range(1, nc):
        acc = acc + rs_buf[k]
    res_ref[...] = acc.astype(res_ref.dtype)

    for c in sent + rs_copies:
        c.wait_send()


def dp_allreduce(a, t, axis_names):
    rows, cols = a.shape
    nc = lax.axis_size("chan")
    owned = t.shape[0] // nc
    nz = lax.axis_size("dp") // 4
    half = rows // 2
    chunk = half // nz
    lanes = cols // 2
    n_copies = nz + 6 * (nz - 1) + 3
    vmem = pltpu.VMEM
    return pl.pallas_call(
        functools.partial(_allreduce_kernel, axis_names, nz, nc),
        out_shape=(
            jax.ShapeDtypeStruct((rows, cols), a.dtype),
            jax.ShapeDtypeStruct((owned, t.shape[1]), jnp.bfloat16),
        ),
        in_specs=[pl.BlockSpec(memory_space=vmem)] * 2,
        out_specs=(pl.BlockSpec(memory_space=vmem), pl.BlockSpec(memory_space=vmem)),
        scratch_shapes=[
            vmem((half, cols), a.dtype),
            vmem((half, cols), a.dtype),
            vmem((chunk, cols), a.dtype),
            vmem((chunk // 2, cols), a.dtype),
            vmem((nz - 1, chunk, lanes), a.dtype),
            vmem((nz - 1, chunk, lanes), a.dtype),
            vmem((nz - 1, chunk, lanes), a.dtype),
            vmem((nz - 1, chunk, lanes), a.dtype),
            vmem((nc, owned, t.shape[1]), t.dtype),
            pltpu.SemaphoreType.DMA((n_copies,)),
            pltpu.SemaphoreType.DMA((n_copies,)),
            pltpu.SemaphoreType.DMA((nc,)),
            pltpu.SemaphoreType.DMA((nc,)),
        ],
        compiler_params=pltpu.CompilerParams(
            collective_id=0, has_side_effects=True, vmem_limit_bytes=48 * 1024 * 1024
        ),
    )(a, t)


def _allgather_kernel(axis_names, n, x_ref, o_ref, send_sems, recv_sems):
    rows = x_ref.shape[0]
    MESH = pl.DeviceIdType.MESH
    me = lax.axis_index("chan")

    def dev(p):
        return tuple(p if a == "chan" else lax.axis_index(a) for a in axis_names)

    barrier = pltpu.get_barrier_semaphore()
    for k in range(1, n):
        pl.semaphore_signal(barrier, inc=1, device_id=dev((me + k) % n), device_id_type=MESH)
    pl.semaphore_wait(barrier, n - 1)

    mine = pl.ds(pl.multiple_of(me * rows, 16), rows)
    copies = []
    for k in range(1, n):
        peer = (me + k) % n
        c = pltpu.make_async_remote_copy(
            src_ref=x_ref, dst_ref=o_ref.at[mine], send_sem=send_sems.at[k],
            recv_sem=recv_sems.at[k], device_id=dev(peer), device_id_type=MESH)
        c.start()
        copies.append(c)
    o_ref[mine, :] = x_ref[...]
    for k in range(1, n):
        src = (me + n - k) % n
        theirs = pl.ds(pl.multiple_of(src * rows, 16), rows)
        pltpu.make_async_remote_copy(
            src_ref=x_ref, dst_ref=o_ref.at[theirs], send_sem=send_sems.at[k],
            recv_sem=recv_sems.at[k], device_id=dev(src), device_id_type=MESH).wait_recv()
    for c in copies:
        c.wait_send()


def chan_allgather(x, axis_names):
    rows, cols = x.shape
    n = lax.axis_size("chan")
    vmem = pltpu.VMEM
    return pl.pallas_call(
        functools.partial(_allgather_kernel, axis_names, n),
        out_shape=jax.ShapeDtypeStruct((rows * n, cols), x.dtype),
        in_specs=[pl.BlockSpec(memory_space=vmem)],
        out_specs=pl.BlockSpec(memory_space=vmem),
        scratch_shapes=[pltpu.SemaphoreType.DMA((n,)), pltpu.SemaphoreType.DMA((n,))],
        compiler_params=pltpu.CompilerParams(collective_id=1, has_side_effects=True),
    )(x)


def on_device(axis_names, inputs, weight, cotangent):
    input_channels_local = inputs.shape[1]
    cout_local = cotangent.shape[1]
    tap_locations = MAP_HEIGHT * MAP_WIDTH
    feature_map = inputs[0].reshape(input_channels_local, MAP_HEIGHT, MAP_WIDTH)
    tap_list = weight.shape[1]
    output_channels_total = weight.shape[2]
    tap_shifts = [
        (DILATION_RATE * (tap_index // 3 - 1), DILATION_RATE * (tap_index % 3 - 1))
        for tap_index in range(tap_list)
    ]
    displaced_input = [
        translated_input(feature_map, first_operand, second_operand, DILATION_RATE).reshape(
            input_channels_local, tap_locations
        )
        for first_operand, second_operand in tap_shifts
    ]
    flat_grads = chan_allgather(cotangent[0], axis_names)
    contract_cols = (((1,), (1,)), ((), ()))
    local_grad = jnp.stack(
        [
            lax.dot_general(
                displaced_input[tap_index],
                flat_grads,
                contract_cols,
                preferred_element_type=jnp.float32,
            )
            for tap_index in range(tap_list)
        ],
        axis=0,
    )
    contract_rows = (((0,), (0,)), ((), ()))
    total = jnp.zeros((cout_local * lax.axis_size("chan"), tap_locations), jnp.float32)
    for tap_index in range(tap_list):
        columns = weight[:, tap_index, :]
        total = total + lax.dot_general(
            columns, displaced_input[tap_index], contract_rows, preferred_element_type=jnp.float32
        )
    summed, owned = dp_allreduce(
        local_grad.reshape(tap_list * input_channels_local, output_channels_total), total, axis_names
    )
    result = owned.reshape(1, cout_local, tap_locations)
    summed_grad = jnp.transpose(
        summed.reshape(tap_list, input_channels_local, output_channels_total), (1, 0, 2)
    )
    weight_grad = summed_grad / jnp.float32(lax.axis_size("dp"))

    collected_input = flat_grads.reshape(output_channels_total, MAP_HEIGHT, MAP_WIDTH)
    back_sum = jnp.zeros((input_channels_local, tap_locations), jnp.float32)
    for tap_index in range(tap_list):
        row_shift, column_shift = tap_shifts[tap_index]
        displaced_gradient = translated_input(
            collected_input, -row_shift, -column_shift, DILATION_RATE
        ).reshape(output_channels_total, tap_locations)
        back_sum = back_sum + jnp.dot(
            weight[:, tap_index, :], displaced_gradient, preferred_element_type=jnp.float32
        )
    input_grad = back_sum.astype(jnp.bfloat16).reshape(1, input_channels_local, tap_locations)
    return (result, input_grad, weight_grad)


def solution(mesh):
    placed = (P("dp", "chan", None), P("chan", None, None), P("dp", "chan", None))
    return jax.shard_map(
        functools.partial(on_device, tuple(mesh.axis_names)),
        mesh=mesh,
        in_specs=placed,
        out_specs=(P("dp", "chan", None), P("dp", "chan", None), P("chan", None, None)),
        check_vma=False,
    )
```

```python
import functools

import jax
import jax.numpy as jnp
from jax import lax
from jax.experimental import pallas as pl
from jax.experimental.pallas import tpu as pltpu
from jax.sharding import PartitionSpec as P

DILATION_RATE = 12
MAP_HEIGHT = 16
MAP_WIDTH = 72
STREAMS = 2


def translated_input(receptive_field, row_shift, column_shift, reach):
    height, width = (receptive_field.shape[1], receptive_field.shape[2])
    bordered_input = jnp.pad(receptive_field, ((0, 0), (reach, reach), (reach, reach)))
    return bordered_input[
        :,
        reach + row_shift : reach + row_shift + height,
        reach + column_shift : reach + column_shift + width,
    ]


def _allreduce_kernel(axis_names, nz, nc, streams, a_ref, t_ref, o_ref, res_ref, rc, s1, f1, rx, rp, rm,
                      ap, am, rs_buf, send_sems, recv_sems, rs_send, rs_recv):
    rows, cols = a_ref.shape
    half = rows // 2
    chunk = half // nz
    lanes = cols // 2
    MESH = pl.DeviceIdType.MESH
    dp = lax.axis_index("dp")
    core = dp % 2
    xl = (dp // 2) % 2
    z = dp // 4
    nd = 4 * nz
    pc = dp + 1 - 2 * core
    px = dp + 2 - 4 * xl
    zr = (dp + 4) % nd
    zl = (dp + nd - 4) % nd

    me = lax.axis_index("chan")

    def dev(p):
        return tuple(p if n == "dp" else lax.axis_index(n) for n in axis_names)

    def cdev(p):
        return tuple(p if n == "chan" else lax.axis_index(n) for n in axis_names)

    barrier = pltpu.get_barrier_semaphore()
    for peer in (pc, px, zr, zl):
        pl.semaphore_signal(barrier, inc=1, device_id=dev(peer), device_id_type=MESH)
    for k in range(1, nc):
        pl.semaphore_signal(barrier, inc=1, device_id=cdev((me + k) % nc), device_id_type=MESH)
    pl.semaphore_wait(barrier, 4 + nc - 1)

    owned = res_ref.shape[0]
    rs_copies = []
    for k in range(1, nc):
        peer = (me + k) % nc
        c = pltpu.make_async_remote_copy(
            src_ref=t_ref.at[pl.ds(pl.multiple_of(peer * owned, 8), owned)],
            dst_ref=rs_buf.at[k], send_sem=rs_send.at[k], recv_sem=rs_recv.at[k],
            device_id=cdev(peer), device_id_type=MESH)
        c.start()
        rs_copies.append(c)

    sent = []
    counter = [0]

    def remote(src, dst, peer):
        k = counter[0]
        counter[0] += 1
        c = pltpu.make_async_remote_copy(
            src_ref=src, dst_ref=dst, send_sem=send_sems.at[k], recv_sem=recv_sems.at[k],
            device_id=dev(peer), device_id_type=MESH)
        c.start()
        sent.append(c)
        return c

    def rows_of(j):
        return pl.ds(pl.multiple_of(j * chunk, 8), chunk)

    mine_c = core * half
    other_c = (1 - core) * half
    order = []
    for d in range(1, nz // 2 + 1):
        order.append((z + nz - d) % nz)
        if 2 * d != nz:
            order.append((z + d) % nz)
    order.append(z)
    core_in = []
    for j in order:
        src_rows = pl.ds(pl.multiple_of(other_c + j * chunk, 8), chunk)
        core_in.append((j, remote(a_ref.at[src_rows], rc.at[rows_of(j)], pc)))
    ready = [0]

    def ready_upto(n):
        while ready[0] < n:
            j, c = core_in[ready[0]]
            c.wait_recv()
            own_rows = pl.ds(pl.multiple_of(mine_c + j * chunk, 8), chunk)
            s1[rows_of(j), :] = a_ref[own_rows, :] + rc[rows_of(j), :]
            ready[0] += 1

    def needed(d):
        return min(len(order) - 1, 2 * d - (1 if 2 * d == nz else 0))

    lo = pl.ds(0, lanes)
    hi = pl.ds(lanes, lanes)
    sub = chunk // streams

    def srows(j, q):
        return pl.ds(pl.multiple_of(j * chunk + q * sub, 8), sub)

    blk = [pl.ds(q * sub, sub) for q in range(streams)]
    pending = [None] * streams
    for s in range(nz - 1):
        jp = (z + 2 * nz - 1 - s) % nz
        jm = (z + 1 + s) % nz
        if s + 1 <= nz // 2:
            ready_upto(needed(s + 1))
        for q in range(streams):
            if s == 0:
                src_p = s1.at[srows(jp, q), lo]
                src_m = s1.at[srows(jm, q), hi]
            else:
                pending[q][0].wait_recv()
                pending[q][1].wait_recv()
                ap[s, blk[q], :] = s1[srows(jp, q), lo] + rp[s - 1, blk[q], :]
                am[s, blk[q], :] = s1[srows(jm, q), hi] + rm[s - 1, blk[q], :]
                src_p = ap.at[s, blk[q]]
                src_m = am.at[s, blk[q]]
            pending[q] = (remote(src_p, rp.at[s, blk[q]], zr), remote(src_m, rm.at[s, blk[q]], zl))
    for q in range(streams):
        pending[q][0].wait_recv()
        pending[q][1].wait_recv()
    ready_upto(len(order))
    f1[:, lo] = s1[rows_of(z), lo] + rp[nz - 2]
    f1[:, hi] = s1[rows_of(z), hi] + rm[nz - 2]

    piece = chunk // 2
    mine_x = pl.multiple_of(xl * piece, 8)
    other_x = pl.multiple_of((1 - xl) * piece, 8)
    c = remote(f1.at[pl.ds(other_x, piece)], rx, px)
    c.wait_recv()
    base = core * half + z * chunk
    own = pl.ds(pl.multiple_of(base + xl * piece, 8), piece)
    o_ref[own, :] = f1[pl.ds(mine_x, piece), :] + rx[...]

    c = remote(o_ref.at[own], o_ref.at[own], px)
    c.wait_recv()

    own_chunk = pl.ds(pl.multiple_of(core * half + z * chunk, 8), chunk)
    to_core = [remote(o_ref.at[own_chunk], o_ref.at[own_chunk], pc)]

    def grows(j, q):
        return pl.ds(pl.multiple_of(core * half + j * chunk + q * sub, 8), sub)

    def arrived(q, jp, jm):
        pending[q][0].wait_recv()
        pending[q][1].wait_recv()
        gp = grows((jp + nz - 1) % nz, q)
        gm = grows((jm + 1) % nz, q)
        to_core.append(remote(o_ref.at[gp, lo], o_ref.at[gp, lo], pc))
        to_core.append(remote(o_ref.at[gm, hi], o_ref.at[gm, hi], pc))

    for s in range(nz - 1):
        jp = (z + nz - s) % nz
        jm = (z + s) % nz
        for q in range(streams):
            if s > 0:
                arrived(q, (jp + 1) % nz, (jm + nz - 1) % nz)
            gp = grows(jp, q)
            gm = grows(jm, q)
            pending[q] = (remote(o_ref.at[gp, lo], o_ref.at[gp, lo], zr),
                          remote(o_ref.at[gm, hi], o_ref.at[gm, hi], zl))
    for q in range(streams):
        arrived(q, (z + 2) % nz, (z + nz - 2) % nz)
    for c in to_core:
        c.wait_recv()

    for c in rs_copies:
        c.wait_recv()
    acc = t_ref[pl.ds(pl.multiple_of(me * owned, 8), owned), :]
    for k in range(1, nc):
        acc = acc + rs_buf[k]
    res_ref[...] = acc.astype(res_ref.dtype)

    for c in sent + rs_copies:
        c.wait_send()


def dp_allreduce(a, t, axis_names):
    rows, cols = a.shape
    nc = lax.axis_size("chan")
    owned = t.shape[0] // nc
    nz = lax.axis_size("dp") // 4
    half = rows // 2
    chunk = half // nz
    lanes = cols // 2
    n_copies = nz + 3 + 6 * (nz - 1) * STREAMS
    vmem = pltpu.VMEM
    return pl.pallas_call(
        functools.partial(_allreduce_kernel, axis_names, nz, nc, STREAMS),
        out_shape=(
            jax.ShapeDtypeStruct((rows, cols), a.dtype),
            jax.ShapeDtypeStruct((owned, t.shape[1]), jnp.bfloat16),
        ),
        in_specs=[pl.BlockSpec(memory_space=vmem)] * 2,
        out_specs=(pl.BlockSpec(memory_space=vmem), pl.BlockSpec(memory_space=vmem)),
        scratch_shapes=[
            vmem((half, cols), a.dtype),
            vmem((half, cols), a.dtype),
            vmem((chunk, cols), a.dtype),
            vmem((chunk // 2, cols), a.dtype),
            vmem((nz - 1, chunk, lanes), a.dtype),
            vmem((nz - 1, chunk, lanes), a.dtype),
            vmem((nz - 1, chunk, lanes), a.dtype),
            vmem((nz - 1, chunk, lanes), a.dtype),
            vmem((nc, owned, t.shape[1]), t.dtype),
            pltpu.SemaphoreType.DMA((n_copies,)),
            pltpu.SemaphoreType.DMA((n_copies,)),
            pltpu.SemaphoreType.DMA((nc,)),
            pltpu.SemaphoreType.DMA((nc,)),
        ],
        compiler_params=pltpu.CompilerParams(
            collective_id=0, has_side_effects=True, vmem_limit_bytes=48 * 1024 * 1024
        ),
    )(a, t)


def _allgather_kernel(axis_names, n, x_ref, o_ref, send_sems, recv_sems):
    rows = x_ref.shape[0]
    MESH = pl.DeviceIdType.MESH
    me = lax.axis_index("chan")

    def dev(p):
        return tuple(p if a == "chan" else lax.axis_index(a) for a in axis_names)

    barrier = pltpu.get_barrier_semaphore()
    for k in range(1, n):
        pl.semaphore_signal(barrier, inc=1, device_id=dev((me + k) % n), device_id_type=MESH)
    pl.semaphore_wait(barrier, n - 1)

    mine = pl.ds(pl.multiple_of(me * rows, 16), rows)
    copies = []
    for k in range(1, n):
        peer = (me + k) % n
        c = pltpu.make_async_remote_copy(
            src_ref=x_ref, dst_ref=o_ref.at[mine], send_sem=send_sems.at[k],
            recv_sem=recv_sems.at[k], device_id=dev(peer), device_id_type=MESH)
        c.start()
        copies.append(c)
    o_ref[mine, :] = x_ref[...]
    for k in range(1, n):
        src = (me + n - k) % n
        theirs = pl.ds(pl.multiple_of(src * rows, 16), rows)
        pltpu.make_async_remote_copy(
            src_ref=x_ref, dst_ref=o_ref.at[theirs], send_sem=send_sems.at[k],
            recv_sem=recv_sems.at[k], device_id=dev(src), device_id_type=MESH).wait_recv()
    for c in copies:
        c.wait_send()


def chan_allgather(x, axis_names):
    rows, cols = x.shape
    n = lax.axis_size("chan")
    vmem = pltpu.VMEM
    return pl.pallas_call(
        functools.partial(_allgather_kernel, axis_names, n),
        out_shape=jax.ShapeDtypeStruct((rows * n, cols), x.dtype),
        in_specs=[pl.BlockSpec(memory_space=vmem)],
        out_specs=pl.BlockSpec(memory_space=vmem),
        scratch_shapes=[pltpu.SemaphoreType.DMA((n,)), pltpu.SemaphoreType.DMA((n,))],
        compiler_params=pltpu.CompilerParams(collective_id=1, has_side_effects=True),
    )(x)


def on_device(axis_names, inputs, weight, cotangent):
    input_channels_local = inputs.shape[1]
    cout_local = cotangent.shape[1]
    tap_locations = MAP_HEIGHT * MAP_WIDTH
    feature_map = inputs[0].reshape(input_channels_local, MAP_HEIGHT, MAP_WIDTH)
    tap_list = weight.shape[1]
    output_channels_total = weight.shape[2]
    tap_shifts = [
        (DILATION_RATE * (tap_index // 3 - 1), DILATION_RATE * (tap_index % 3 - 1))
        for tap_index in range(tap_list)
    ]
    displaced_input = [
        translated_input(feature_map, first_operand, second_operand, DILATION_RATE).reshape(
            input_channels_local, tap_locations
        )
        for first_operand, second_operand in tap_shifts
    ]
    flat_grads = chan_allgather(cotangent[0], axis_names)
    contract_cols = (((1,), (1,)), ((), ()))
    local_grad = jnp.stack(
        [
            lax.dot_general(
                displaced_input[tap_index],
                flat_grads,
                contract_cols,
                preferred_element_type=jnp.float32,
            )
            for tap_index in range(tap_list)
        ],
        axis=0,
    )
    contract_rows = (((0,), (0,)), ((), ()))
    total = jnp.zeros((cout_local * lax.axis_size("chan"), tap_locations), jnp.float32)
    for tap_index in range(tap_list):
        columns = weight[:, tap_index, :]
        total = total + lax.dot_general(
            columns, displaced_input[tap_index], contract_rows, preferred_element_type=jnp.float32
        )
    summed, owned = dp_allreduce(
        local_grad.reshape(tap_list * input_channels_local, output_channels_total), total, axis_names
    )
    result = owned.reshape(1, cout_local, tap_locations)
    summed_grad = jnp.transpose(
        summed.reshape(tap_list, input_channels_local, output_channels_total), (1, 0, 2)
    )
    weight_grad = summed_grad / jnp.float32(lax.axis_size("dp"))

    collected_input = flat_grads.reshape(output_channels_total, MAP_HEIGHT, MAP_WIDTH)
    back_sum = jnp.zeros((input_channels_local, tap_locations), jnp.float32)
    for tap_index in range(tap_list):
        row_shift, column_shift = tap_shifts[tap_index]
        displaced_gradient = translated_input(
            collected_input, -row_shift, -column_shift, DILATION_RATE
        ).reshape(output_channels_total, tap_locations)
        back_sum = back_sum + jnp.dot(
            weight[:, tap_index, :], displaced_gradient, preferred_element_type=jnp.float32
        )
    input_grad = back_sum.astype(jnp.bfloat16).reshape(1, input_channels_local, tap_locations)
    return (result, input_grad, weight_grad)


def solution(mesh):
    placed = (P("dp", "chan", None), P("chan", None, None), P("dp", "chan", None))
    return jax.shard_map(
        functools.partial(on_device, tuple(mesh.axis_names)),
        mesh=mesh,
        in_specs=placed,
        out_specs=(P("dp", "chan", None), P("dp", "chan", None), P("chan", None, None)),
        check_vma=False,
    )
```

```python
import functools

import jax
import jax.numpy as jnp
from jax import lax
from jax.experimental import pallas as pl
from jax.experimental.pallas import tpu as pltpu
from jax.sharding import PartitionSpec as P

DILATION_RATE = 12
MAP_HEIGHT = 16
MAP_WIDTH = 72
STREAMS = 3


def translated_input(receptive_field, row_shift, column_shift, reach):
    height, width = (receptive_field.shape[1], receptive_field.shape[2])
    bordered_input = jnp.pad(receptive_field, ((0, 0), (reach, reach), (reach, reach)))
    return bordered_input[
        :,
        reach + row_shift : reach + row_shift + height,
        reach + column_shift : reach + column_shift + width,
    ]


def _allreduce_kernel(axis_names, nz, nc, streams, a_ref, t_ref, o_ref, res_ref, rc, s1, f1, rx, rp, rm,
                      ap, am, rs_buf, send_sems, recv_sems, rs_send, rs_recv):
    rows, cols = a_ref.shape
    half = rows // 2
    chunk = half // nz
    lanes = cols // 2
    MESH = pl.DeviceIdType.MESH
    dp = lax.axis_index("dp")
    core = dp % 2
    xl = (dp // 2) % 2
    z = dp // 4
    nd = 4 * nz
    pc = dp + 1 - 2 * core
    px = dp + 2 - 4 * xl
    zr = (dp + 4) % nd
    zl = (dp + nd - 4) % nd

    me = lax.axis_index("chan")

    def dev(p):
        return tuple(p if n == "dp" else lax.axis_index(n) for n in axis_names)

    def cdev(p):
        return tuple(p if n == "chan" else lax.axis_index(n) for n in axis_names)

    barrier = pltpu.get_barrier_semaphore()
    for peer in (pc, px, zr, zl):
        pl.semaphore_signal(barrier, inc=1, device_id=dev(peer), device_id_type=MESH)
    for k in range(1, nc):
        pl.semaphore_signal(barrier, inc=1, device_id=cdev((me + k) % nc), device_id_type=MESH)
    pl.semaphore_wait(barrier, 4 + nc - 1)

    owned = res_ref.shape[0]
    rs_copies = []
    for k in range(1, nc):
        peer = (me + k) % nc
        c = pltpu.make_async_remote_copy(
            src_ref=t_ref.at[pl.ds(pl.multiple_of(peer * owned, 8), owned)],
            dst_ref=rs_buf.at[k], send_sem=rs_send.at[k], recv_sem=rs_recv.at[k],
            device_id=cdev(peer), device_id_type=MESH)
        c.start()
        rs_copies.append(c)

    sent = []
    counter = [0]

    def remote(src, dst, peer):
        k = counter[0]
        counter[0] += 1
        c = pltpu.make_async_remote_copy(
            src_ref=src, dst_ref=dst, send_sem=send_sems.at[k], recv_sem=recv_sems.at[k],
            device_id=dev(peer), device_id_type=MESH)
        c.start()
        sent.append(c)
        return c

    def rows_of(j):
        return pl.ds(pl.multiple_of(j * chunk, 8), chunk)

    mine_c = core * half
    other_c = (1 - core) * half
    order = []
    for d in range(1, nz // 2 + 1):
        order.append((z + nz - d) % nz)
        if 2 * d != nz:
            order.append((z + d) % nz)
    order.append(z)
    core_in = []
    for j in order:
        src_rows = pl.ds(pl.multiple_of(other_c + j * chunk, 8), chunk)
        core_in.append((j, remote(a_ref.at[src_rows], rc.at[rows_of(j)], pc)))
    ready = [0]

    def ready_upto(n):
        while ready[0] < n:
            j, c = core_in[ready[0]]
            c.wait_recv()
            own_rows = pl.ds(pl.multiple_of(mine_c + j * chunk, 8), chunk)
            s1[rows_of(j), :] = a_ref[own_rows, :] + rc[rows_of(j), :]
            ready[0] += 1

    def needed(d):
        return min(len(order) - 1, 2 * d - (1 if 2 * d == nz else 0))

    lo = pl.ds(0, lanes)
    hi = pl.ds(lanes, lanes)
    sub = chunk // streams

    def srows(j, q):
        return pl.ds(pl.multiple_of(j * chunk + q * sub, 8), sub)

    blk = [pl.ds(q * sub, sub) for q in range(streams)]
    pending = [None] * streams
    for s in range(nz - 1):
        jp = (z + 2 * nz - 1 - s) % nz
        jm = (z + 1 + s) % nz
        if s + 1 <= nz // 2:
            ready_upto(needed(s + 1))
        for q in range(streams):
            if s == 0:
                src_p = s1.at[srows(jp, q), lo]
                src_m = s1.at[srows(jm, q), hi]
            else:
                pending[q][0].wait_recv()
                pending[q][1].wait_recv()
                ap[s, blk[q], :] = s1[srows(jp, q), lo] + rp[s - 1, blk[q], :]
                am[s, blk[q], :] = s1[srows(jm, q), hi] + rm[s - 1, blk[q], :]
                src_p = ap.at[s, blk[q]]
                src_m = am.at[s, blk[q]]
            pending[q] = (remote(src_p, rp.at[s, blk[q]], zr), remote(src_m, rm.at[s, blk[q]], zl))
    for q in range(streams):
        pending[q][0].wait_recv()
        pending[q][1].wait_recv()
    ready_upto(len(order))
    f1[:, lo] = s1[rows_of(z), lo] + rp[nz - 2]
    f1[:, hi] = s1[rows_of(z), hi] + rm[nz - 2]

    c = remote(f1, rx, px)
    c.wait_recv()
    own_chunk = pl.ds(pl.multiple_of(core * half + z * chunk, 8), chunk)
    o_ref[own_chunk, :] = f1[...] + rx[...]

    to_core = [remote(o_ref.at[own_chunk], o_ref.at[own_chunk], pc)]

    def grows(j, q):
        return pl.ds(pl.multiple_of(core * half + j * chunk + q * sub, 8), sub)

    def arrived(q, jp, jm):
        pending[q][0].wait_recv()
        pending[q][1].wait_recv()
        gp = grows((jp + nz - 1) % nz, q)
        gm = grows((jm + 1) % nz, q)
        to_core.append(remote(o_ref.at[gp, lo], o_ref.at[gp, lo], pc))
        to_core.append(remote(o_ref.at[gm, hi], o_ref.at[gm, hi], pc))

    for s in range(nz - 1):
        jp = (z + nz - s) % nz
        jm = (z + s) % nz
        for q in range(streams):
            if s > 0:
                arrived(q, (jp + 1) % nz, (jm + nz - 1) % nz)
            gp = grows(jp, q)
            gm = grows(jm, q)
            pending[q] = (remote(o_ref.at[gp, lo], o_ref.at[gp, lo], zr),
                          remote(o_ref.at[gm, hi], o_ref.at[gm, hi], zl))
    for q in range(streams):
        arrived(q, (z + 2) % nz, (z + nz - 2) % nz)
    for c in to_core:
        c.wait_recv()

    for c in rs_copies:
        c.wait_recv()
    acc = t_ref[pl.ds(pl.multiple_of(me * owned, 8), owned), :]
    for k in range(1, nc):
        acc = acc + rs_buf[k]
    res_ref[...] = acc.astype(res_ref.dtype)

    for c in sent + rs_copies:
        c.wait_send()


def dp_allreduce(a, t, axis_names):
    rows, cols = a.shape
    nc = lax.axis_size("chan")
    owned = t.shape[0] // nc
    nz = lax.axis_size("dp") // 4
    half = rows // 2
    chunk = half // nz
    lanes = cols // 2
    n_copies = nz + 3 + 6 * (nz - 1) * STREAMS
    vmem = pltpu.VMEM
    return pl.pallas_call(
        functools.partial(_allreduce_kernel, axis_names, nz, nc, STREAMS),
        out_shape=(
            jax.ShapeDtypeStruct((rows, cols), a.dtype),
            jax.ShapeDtypeStruct((owned, t.shape[1]), jnp.bfloat16),
        ),
        in_specs=[pl.BlockSpec(memory_space=vmem)] * 2,
        out_specs=(pl.BlockSpec(memory_space=vmem), pl.BlockSpec(memory_space=vmem)),
        scratch_shapes=[
            vmem((half, cols), a.dtype),
            vmem((half, cols), a.dtype),
            vmem((chunk, cols), a.dtype),
            vmem((chunk, cols), a.dtype),
            vmem((nz - 1, chunk, lanes), a.dtype),
            vmem((nz - 1, chunk, lanes), a.dtype),
            vmem((nz - 1, chunk, lanes), a.dtype),
            vmem((nz - 1, chunk, lanes), a.dtype),
            vmem((nc, owned, t.shape[1]), t.dtype),
            pltpu.SemaphoreType.DMA((n_copies,)),
            pltpu.SemaphoreType.DMA((n_copies,)),
            pltpu.SemaphoreType.DMA((nc,)),
            pltpu.SemaphoreType.DMA((nc,)),
        ],
        compiler_params=pltpu.CompilerParams(
            collective_id=0, has_side_effects=True, vmem_limit_bytes=48 * 1024 * 1024
        ),
    )(a, t)


def _allgather_kernel(axis_names, n, x_ref, o_ref, send_sems, recv_sems):
    rows = x_ref.shape[0]
    MESH = pl.DeviceIdType.MESH
    me = lax.axis_index("chan")

    def dev(p):
        return tuple(p if a == "chan" else lax.axis_index(a) for a in axis_names)

    barrier = pltpu.get_barrier_semaphore()
    for k in range(1, n):
        pl.semaphore_signal(barrier, inc=1, device_id=dev((me + k) % n), device_id_type=MESH)
    pl.semaphore_wait(barrier, n - 1)

    mine = pl.ds(pl.multiple_of(me * rows, 16), rows)
    copies = []
    for k in range(1, n):
        peer = (me + k) % n
        c = pltpu.make_async_remote_copy(
            src_ref=x_ref, dst_ref=o_ref.at[mine], send_sem=send_sems.at[k],
            recv_sem=recv_sems.at[k], device_id=dev(peer), device_id_type=MESH)
        c.start()
        copies.append(c)
    o_ref[mine, :] = x_ref[...]
    for k in range(1, n):
        src = (me + n - k) % n
        theirs = pl.ds(pl.multiple_of(src * rows, 16), rows)
        pltpu.make_async_remote_copy(
            src_ref=x_ref, dst_ref=o_ref.at[theirs], send_sem=send_sems.at[k],
            recv_sem=recv_sems.at[k], device_id=dev(src), device_id_type=MESH).wait_recv()
    for c in copies:
        c.wait_send()


def chan_allgather(x, axis_names):
    rows, cols = x.shape
    n = lax.axis_size("chan")
    vmem = pltpu.VMEM
    return pl.pallas_call(
        functools.partial(_allgather_kernel, axis_names, n),
        out_shape=jax.ShapeDtypeStruct((rows * n, cols), x.dtype),
        in_specs=[pl.BlockSpec(memory_space=vmem)],
        out_specs=pl.BlockSpec(memory_space=vmem),
        scratch_shapes=[pltpu.SemaphoreType.DMA((n,)), pltpu.SemaphoreType.DMA((n,))],
        compiler_params=pltpu.CompilerParams(collective_id=1, has_side_effects=True),
    )(x)


def on_device(axis_names, inputs, weight, cotangent):
    input_channels_local = inputs.shape[1]
    cout_local = cotangent.shape[1]
    tap_locations = MAP_HEIGHT * MAP_WIDTH
    feature_map = inputs[0].reshape(input_channels_local, MAP_HEIGHT, MAP_WIDTH)
    tap_list = weight.shape[1]
    output_channels_total = weight.shape[2]
    tap_shifts = [
        (DILATION_RATE * (tap_index // 3 - 1), DILATION_RATE * (tap_index % 3 - 1))
        for tap_index in range(tap_list)
    ]
    displaced_input = [
        translated_input(feature_map, first_operand, second_operand, DILATION_RATE).reshape(
            input_channels_local, tap_locations
        )
        for first_operand, second_operand in tap_shifts
    ]
    flat_grads = chan_allgather(cotangent[0], axis_names)
    contract_cols = (((1,), (1,)), ((), ()))
    local_grad = jnp.stack(
        [
            lax.dot_general(
                displaced_input[tap_index],
                flat_grads,
                contract_cols,
                preferred_element_type=jnp.float32,
            )
            for tap_index in range(tap_list)
        ],
        axis=0,
    )
    contract_rows = (((0,), (0,)), ((), ()))
    total = jnp.zeros((cout_local * lax.axis_size("chan"), tap_locations), jnp.float32)
    for tap_index in range(tap_list):
        columns = weight[:, tap_index, :]
        total = total + lax.dot_general(
            columns, displaced_input[tap_index], contract_rows, preferred_element_type=jnp.float32
        )
    summed, owned = dp_allreduce(
        local_grad.reshape(tap_list * input_channels_local, output_channels_total), total, axis_names
    )
    result = owned.reshape(1, cout_local, tap_locations)
    summed_grad = jnp.transpose(
        summed.reshape(tap_list, input_channels_local, output_channels_total), (1, 0, 2)
    )
    weight_grad = summed_grad / jnp.float32(lax.axis_size("dp"))

    collected_input = flat_grads.reshape(output_channels_total, MAP_HEIGHT, MAP_WIDTH)
    back_sum = jnp.zeros((input_channels_local, tap_locations), jnp.float32)
    for tap_index in range(tap_list):
        row_shift, column_shift = tap_shifts[tap_index]
        displaced_gradient = translated_input(
            collected_input, -row_shift, -column_shift, DILATION_RATE
        ).reshape(output_channels_total, tap_locations)
        back_sum = back_sum + jnp.dot(
            weight[:, tap_index, :], displaced_gradient, preferred_element_type=jnp.float32
        )
    input_grad = back_sum.astype(jnp.bfloat16).reshape(1, input_channels_local, tap_locations)
    return (result, input_grad, weight_grad)


def solution(mesh):
    placed = (P("dp", "chan", None), P("chan", None, None), P("dp", "chan", None))
    return jax.shard_map(
        functools.partial(on_device, tuple(mesh.axis_names)),
        mesh=mesh,
        in_specs=placed,
        out_specs=(P("dp", "chan", None), P("dp", "chan", None), P("chan", None, None)),
        check_vma=False,
    )
```

```python
import functools

import jax
import jax.numpy as jnp
from jax import lax
from jax.experimental import pallas as pl
from jax.experimental.pallas import tpu as pltpu
from jax.sharding import PartitionSpec as P

DILATION_RATE = 12
MAP_HEIGHT = 16
MAP_WIDTH = 72
STREAMS = 6


def translated_input(receptive_field, row_shift, column_shift, reach):
    height, width = (receptive_field.shape[1], receptive_field.shape[2])
    bordered_input = jnp.pad(receptive_field, ((0, 0), (reach, reach), (reach, reach)))
    return bordered_input[
        :,
        reach + row_shift : reach + row_shift + height,
        reach + column_shift : reach + column_shift + width,
    ]


def _allreduce_kernel(axis_names, nz, nc, streams, a_ref, t_ref, o_ref, res_ref, rc, s1, f1, rx, rp, rm,
                      ap, am, rs_buf, send_sems, recv_sems, rs_send, rs_recv):
    rows, cols = a_ref.shape
    half = rows // 2
    chunk = half // nz
    lanes = cols // 2
    MESH = pl.DeviceIdType.MESH
    dp = lax.axis_index("dp")
    core = dp % 2
    xl = (dp // 2) % 2
    z = dp // 4
    nd = 4 * nz
    pc = dp + 1 - 2 * core
    px = dp + 2 - 4 * xl
    zr = (dp + 4) % nd
    zl = (dp + nd - 4) % nd

    me = lax.axis_index("chan")

    def dev(p):
        return tuple(p if n == "dp" else lax.axis_index(n) for n in axis_names)

    def cdev(p):
        return tuple(p if n == "chan" else lax.axis_index(n) for n in axis_names)

    barrier = pltpu.get_barrier_semaphore()
    for peer in (pc, px, zr, zl):
        pl.semaphore_signal(barrier, inc=1, device_id=dev(peer), device_id_type=MESH)
    for k in range(1, nc):
        pl.semaphore_signal(barrier, inc=1, device_id=cdev((me + k) % nc), device_id_type=MESH)
    pl.semaphore_wait(barrier, 4 + nc - 1)

    owned = res_ref.shape[0]
    rs_copies = []
    for k in range(1, nc):
        peer = (me + k) % nc
        c = pltpu.make_async_remote_copy(
            src_ref=t_ref.at[pl.ds(pl.multiple_of(peer * owned, 8), owned)],
            dst_ref=rs_buf.at[k], send_sem=rs_send.at[k], recv_sem=rs_recv.at[k],
            device_id=cdev(peer), device_id_type=MESH)
        c.start()
        rs_copies.append(c)

    sent = []
    counter = [0]

    def remote(src, dst, peer):
        k = counter[0]
        counter[0] += 1
        c = pltpu.make_async_remote_copy(
            src_ref=src, dst_ref=dst, send_sem=send_sems.at[k], recv_sem=recv_sems.at[k],
            device_id=dev(peer), device_id_type=MESH)
        c.start()
        sent.append(c)
        return c

    def rows_of(j):
        return pl.ds(pl.multiple_of(j * chunk, 8), chunk)

    mine_c = core * half
    other_c = (1 - core) * half
    order = []
    for d in range(1, nz // 2 + 1):
        order.append((z + nz - d) % nz)
        if 2 * d != nz:
            order.append((z + d) % nz)
    order.append(z)
    core_in = []
    for j in order:
        src_rows = pl.ds(pl.multiple_of(other_c + j * chunk, 8), chunk)
        core_in.append((j, remote(a_ref.at[src_rows], rc.at[rows_of(j)], pc)))
    ready = [0]

    def ready_upto(n):
        while ready[0] < n:
            j, c = core_in[ready[0]]
            c.wait_recv()
            own_rows = pl.ds(pl.multiple_of(mine_c + j * chunk, 8), chunk)
            s1[rows_of(j), :] = a_ref[own_rows, :] + rc[rows_of(j), :]
            ready[0] += 1

    def needed(d):
        return min(len(order) - 1, 2 * d - (1 if 2 * d == nz else 0))

    lo = pl.ds(0, lanes)
    hi = pl.ds(lanes, lanes)
    sub = chunk // streams

    def srows(j, q):
        return pl.ds(pl.multiple_of(j * chunk + q * sub, 8), sub)

    blk = [pl.ds(q * sub, sub) for q in range(streams)]
    pending = [None] * streams
    for s in range(nz - 1):
        jp = (z + 2 * nz - 1 - s) % nz
        jm = (z + 1 + s) % nz
        if s + 1 <= nz // 2:
            ready_upto(needed(s + 1))
        for q in range(streams):
            if s == 0:
                src_p = s1.at[srows(jp, q), lo]
                src_m = s1.at[srows(jm, q), hi]
            else:
                pending[q][0].wait_recv()
                pending[q][1].wait_recv()
                ap[s, blk[q], :] = s1[srows(jp, q), lo] + rp[s - 1, blk[q], :]
                am[s, blk[q], :] = s1[srows(jm, q), hi] + rm[s - 1, blk[q], :]
                src_p = ap.at[s, blk[q]]
                src_m = am.at[s, blk[q]]
            pending[q] = (remote(src_p, rp.at[s, blk[q]], zr), remote(src_m, rm.at[s, blk[q]], zl))
    for q in range(streams):
        pending[q][0].wait_recv()
        pending[q][1].wait_recv()
    ready_upto(len(order))
    f1[:, lo] = s1[rows_of(z), lo] + rp[nz - 2]
    f1[:, hi] = s1[rows_of(z), hi] + rm[nz - 2]

    c = remote(f1, rx, px)
    c.wait_recv()
    own_chunk = pl.ds(pl.multiple_of(core * half + z * chunk, 8), chunk)
    o_ref[own_chunk, :] = f1[...] + rx[...]

    to_core = [remote(o_ref.at[own_chunk], o_ref.at[own_chunk], pc)]

    def grows(j, q):
        return pl.ds(pl.multiple_of(core * half + j * chunk + q * sub, 8), sub)

    def arrived(q, jp, jm):
        pending[q][0].wait_recv()
        pending[q][1].wait_recv()
        gp = grows((jp + nz - 1) % nz, q)
        gm = grows((jm + 1) % nz, q)
        to_core.append(remote(o_ref.at[gp, lo], o_ref.at[gp, lo], pc))
        to_core.append(remote(o_ref.at[gm, hi], o_ref.at[gm, hi], pc))

    for s in range(nz - 1):
        jp = (z + nz - s) % nz
        jm = (z + s) % nz
        for q in range(streams):
            if s > 0:
                arrived(q, (jp + 1) % nz, (jm + nz - 1) % nz)
            gp = grows(jp, q)
            gm = grows(jm, q)
            pending[q] = (remote(o_ref.at[gp, lo], o_ref.at[gp, lo], zr),
                          remote(o_ref.at[gm, hi], o_ref.at[gm, hi], zl))
    for q in range(streams):
        arrived(q, (z + 2) % nz, (z + nz - 2) % nz)
    for c in to_core:
        c.wait_recv()

    for c in rs_copies:
        c.wait_recv()
    acc = t_ref[pl.ds(pl.multiple_of(me * owned, 8), owned), :]
    for k in range(1, nc):
        acc = acc + rs_buf[k]
    res_ref[...] = acc.astype(res_ref.dtype)

    for c in sent + rs_copies:
        c.wait_send()


def dp_allreduce(a, t, axis_names):
    rows, cols = a.shape
    nc = lax.axis_size("chan")
    owned = t.shape[0] // nc
    nz = lax.axis_size("dp") // 4
    half = rows // 2
    chunk = half // nz
    lanes = cols // 2
    n_copies = nz + 3 + 6 * (nz - 1) * STREAMS
    vmem = pltpu.VMEM
    return pl.pallas_call(
        functools.partial(_allreduce_kernel, axis_names, nz, nc, STREAMS),
        out_shape=(
            jax.ShapeDtypeStruct((rows, cols), a.dtype),
            jax.ShapeDtypeStruct((owned, t.shape[1]), jnp.bfloat16),
        ),
        in_specs=[pl.BlockSpec(memory_space=vmem)] * 2,
        out_specs=(pl.BlockSpec(memory_space=vmem), pl.BlockSpec(memory_space=vmem)),
        scratch_shapes=[
            vmem((half, cols), a.dtype),
            vmem((half, cols), a.dtype),
            vmem((chunk, cols), a.dtype),
            vmem((chunk, cols), a.dtype),
            vmem((nz - 1, chunk, lanes), a.dtype),
            vmem((nz - 1, chunk, lanes), a.dtype),
            vmem((nz - 1, chunk, lanes), a.dtype),
            vmem((nz - 1, chunk, lanes), a.dtype),
            vmem((nc, owned, t.shape[1]), t.dtype),
            pltpu.SemaphoreType.DMA((n_copies,)),
            pltpu.SemaphoreType.DMA((n_copies,)),
            pltpu.SemaphoreType.DMA((nc,)),
            pltpu.SemaphoreType.DMA((nc,)),
        ],
        compiler_params=pltpu.CompilerParams(
            collective_id=0, has_side_effects=True, vmem_limit_bytes=48 * 1024 * 1024
        ),
    )(a, t)


def _allgather_kernel(axis_names, n, x_ref, o_ref, send_sems, recv_sems):
    rows = x_ref.shape[0]
    MESH = pl.DeviceIdType.MESH
    me = lax.axis_index("chan")

    def dev(p):
        return tuple(p if a == "chan" else lax.axis_index(a) for a in axis_names)

    barrier = pltpu.get_barrier_semaphore()
    for k in range(1, n):
        pl.semaphore_signal(barrier, inc=1, device_id=dev((me + k) % n), device_id_type=MESH)
    pl.semaphore_wait(barrier, n - 1)

    mine = pl.ds(pl.multiple_of(me * rows, 16), rows)
    copies = []
    for k in range(1, n):
        peer = (me + k) % n
        c = pltpu.make_async_remote_copy(
            src_ref=x_ref, dst_ref=o_ref.at[mine], send_sem=send_sems.at[k],
            recv_sem=recv_sems.at[k], device_id=dev(peer), device_id_type=MESH)
        c.start()
        copies.append(c)
    o_ref[mine, :] = x_ref[...]
    for k in range(1, n):
        src = (me + n - k) % n
        theirs = pl.ds(pl.multiple_of(src * rows, 16), rows)
        pltpu.make_async_remote_copy(
            src_ref=x_ref, dst_ref=o_ref.at[theirs], send_sem=send_sems.at[k],
            recv_sem=recv_sems.at[k], device_id=dev(src), device_id_type=MESH).wait_recv()
    for c in copies:
        c.wait_send()


def chan_allgather(x, axis_names):
    rows, cols = x.shape
    n = lax.axis_size("chan")
    vmem = pltpu.VMEM
    return pl.pallas_call(
        functools.partial(_allgather_kernel, axis_names, n),
        out_shape=jax.ShapeDtypeStruct((rows * n, cols), x.dtype),
        in_specs=[pl.BlockSpec(memory_space=vmem)],
        out_specs=pl.BlockSpec(memory_space=vmem),
        scratch_shapes=[pltpu.SemaphoreType.DMA((n,)), pltpu.SemaphoreType.DMA((n,))],
        compiler_params=pltpu.CompilerParams(collective_id=1, has_side_effects=True),
    )(x)


def on_device(axis_names, inputs, weight, cotangent):
    input_channels_local = inputs.shape[1]
    cout_local = cotangent.shape[1]
    tap_locations = MAP_HEIGHT * MAP_WIDTH
    feature_map = inputs[0].reshape(input_channels_local, MAP_HEIGHT, MAP_WIDTH)
    tap_list = weight.shape[1]
    output_channels_total = weight.shape[2]
    tap_shifts = [
        (DILATION_RATE * (tap_index // 3 - 1), DILATION_RATE * (tap_index % 3 - 1))
        for tap_index in range(tap_list)
    ]
    displaced_input = [
        translated_input(feature_map, first_operand, second_operand, DILATION_RATE).reshape(
            input_channels_local, tap_locations
        )
        for first_operand, second_operand in tap_shifts
    ]
    flat_grads = chan_allgather(cotangent[0], axis_names)
    contract_cols = (((1,), (1,)), ((), ()))
    local_grad = jnp.stack(
        [
            lax.dot_general(
                displaced_input[tap_index],
                flat_grads,
                contract_cols,
                preferred_element_type=jnp.float32,
            )
            for tap_index in range(tap_list)
        ],
        axis=0,
    )
    contract_rows = (((0,), (0,)), ((), ()))
    total = jnp.zeros((cout_local * lax.axis_size("chan"), tap_locations), jnp.float32)
    for tap_index in range(tap_list):
        columns = weight[:, tap_index, :]
        total = total + lax.dot_general(
            columns, displaced_input[tap_index], contract_rows, preferred_element_type=jnp.float32
        )
    summed, owned = dp_allreduce(
        local_grad.reshape(tap_list * input_channels_local, output_channels_total), total, axis_names
    )
    result = owned.reshape(1, cout_local, tap_locations)
    summed_grad = jnp.transpose(
        summed.reshape(tap_list, input_channels_local, output_channels_total), (1, 0, 2)
    )
    weight_grad = summed_grad / jnp.float32(lax.axis_size("dp"))

    collected_input = flat_grads.reshape(output_channels_total, MAP_HEIGHT, MAP_WIDTH)
    back_sum = jnp.zeros((input_channels_local, tap_locations), jnp.float32)
    for tap_index in range(tap_list):
        row_shift, column_shift = tap_shifts[tap_index]
        displaced_gradient = translated_input(
            collected_input, -row_shift, -column_shift, DILATION_RATE
        ).reshape(output_channels_total, tap_locations)
        back_sum = back_sum + jnp.dot(
            weight[:, tap_index, :], displaced_gradient, preferred_element_type=jnp.float32
        )
    input_grad = back_sum.astype(jnp.bfloat16).reshape(1, input_channels_local, tap_locations)
    return (result, input_grad, weight_grad)


def solution(mesh):
    placed = (P("dp", "chan", None), P("chan", None, None), P("dp", "chan", None))
    return jax.shard_map(
        functools.partial(on_device, tuple(mesh.axis_names)),
        mesh=mesh,
        in_specs=placed,
        out_specs=(P("dp", "chan", None), P("dp", "chan", None), P("chan", None, None)),
        check_vma=False,
    )
```

```python
import functools

import jax
import jax.numpy as jnp
from jax import lax
from jax.experimental import pallas as pl
from jax.experimental.pallas import tpu as pltpu
from jax.sharding import PartitionSpec as P

DILATION_RATE = 12
MAP_HEIGHT = 16
MAP_WIDTH = 72
STREAMS = 3


def translated_input(receptive_field, row_shift, column_shift, reach):
    height, width = (receptive_field.shape[1], receptive_field.shape[2])
    bordered_input = jnp.pad(receptive_field, ((0, 0), (reach, reach), (reach, reach)))
    return bordered_input[
        :,
        reach + row_shift : reach + row_shift + height,
        reach + column_shift : reach + column_shift + width,
    ]


def _allreduce_kernel(axis_names, nz, nc, streams, a_ref, t_ref, o_ref, res_ref, rc, s1, f1, rx, rp, rm,
                      ap, am, rs_buf, send_sems, recv_sems, rs_send, rs_recv):
    rows, cols = a_ref.shape
    half = rows // 2
    chunk = half // nz
    lanes = cols // 2
    MESH = pl.DeviceIdType.MESH
    dp = lax.axis_index("dp")
    core = dp % 2
    xl = (dp // 2) % 2
    z = dp // 4
    nd = 4 * nz
    pc = dp + 1 - 2 * core
    px = dp + 2 - 4 * xl
    zr = (dp + 4) % nd
    zl = (dp + nd - 4) % nd

    me = lax.axis_index("chan")

    def dev(p):
        return tuple(p if n == "dp" else lax.axis_index(n) for n in axis_names)

    def cdev(p):
        return tuple(p if n == "chan" else lax.axis_index(n) for n in axis_names)

    barrier = pltpu.get_barrier_semaphore()
    for peer in (pc, px, zr, zl):
        pl.semaphore_signal(barrier, inc=1, device_id=dev(peer), device_id_type=MESH)
    for k in range(1, nc):
        pl.semaphore_signal(barrier, inc=1, device_id=cdev((me + k) % nc), device_id_type=MESH)
    pl.semaphore_wait(barrier, 4 + nc - 1)

    owned = res_ref.shape[0]
    rs_copies = []
    for k in range(1, nc):
        peer = (me + k) % nc
        c = pltpu.make_async_remote_copy(
            src_ref=t_ref.at[pl.ds(pl.multiple_of(peer * owned, 8), owned)],
            dst_ref=rs_buf.at[k], send_sem=rs_send.at[k], recv_sem=rs_recv.at[k],
            device_id=cdev(peer), device_id_type=MESH)
        c.start()
        rs_copies.append(c)

    sent = []
    counter = [0]

    def remote(src, dst, peer):
        k = counter[0]
        counter[0] += 1
        c = pltpu.make_async_remote_copy(
            src_ref=src, dst_ref=dst, send_sem=send_sems.at[k], recv_sem=recv_sems.at[k],
            device_id=dev(peer), device_id_type=MESH)
        c.start()
        sent.append(c)
        return c

    def rows_of(j):
        return pl.ds(pl.multiple_of(j * chunk, 8), chunk)

    mine_c = core * half
    other_c = (1 - core) * half
    order = []
    for d in range(1, nz // 2 + 1):
        order.append((z + nz - d) % nz)
        if 2 * d != nz:
            order.append((z + d) % nz)
    order.append(z)
    core_in = []
    for j in order:
        src_rows = pl.ds(pl.multiple_of(other_c + j * chunk, 8), chunk)
        core_in.append((j, remote(a_ref.at[src_rows], rc.at[rows_of(j)], pc)))
    ready = [0]

    def ready_upto(n):
        while ready[0] < n:
            j, c = core_in[ready[0]]
            c.wait_recv()
            own_rows = pl.ds(pl.multiple_of(mine_c + j * chunk, 8), chunk)
            s1[rows_of(j), :] = a_ref[own_rows, :] + rc[rows_of(j), :]
            ready[0] += 1

    def needed(d):
        return min(len(order) - 1, 2 * d - (1 if 2 * d == nz else 0))

    lo = pl.ds(0, lanes)
    hi = pl.ds(lanes, lanes)
    sub = chunk // streams

    def srows(j, q):
        return pl.ds(pl.multiple_of(j * chunk + q * sub, 8), sub)

    blk = [pl.ds(q * sub, sub) for q in range(streams)]
    pending = [None] * streams
    for s in range(nz - 1):
        jp = (z + 2 * nz - 1 - s) % nz
        jm = (z + 1 + s) % nz
        if s + 1 <= nz // 2:
            ready_upto(needed(s + 1))
        for q in range(streams):
            if s == 0:
                src_p = s1.at[srows(jp, q), lo]
                src_m = s1.at[srows(jm, q), hi]
            else:
                pending[q][0].wait_recv()
                pending[q][1].wait_recv()
                ap[s, blk[q], :] = s1[srows(jp, q), lo] + rp[s - 1, blk[q], :]
                am[s, blk[q], :] = s1[srows(jm, q), hi] + rm[s - 1, blk[q], :]
                src_p = ap.at[s, blk[q]]
                src_m = am.at[s, blk[q]]
            pending[q] = (remote(src_p, rp.at[s, blk[q]], zr), remote(src_m, rm.at[s, blk[q]], zl))
    for q in range(streams):
        pending[q][0].wait_recv()
        pending[q][1].wait_recv()
    ready_upto(len(order))
    f1[:, lo] = s1[rows_of(z), lo] + rp[nz - 2]
    f1[:, hi] = s1[rows_of(z), hi] + rm[nz - 2]

    c = remote(f1, rx, px)
    c.wait_recv()
    own_chunk = pl.ds(pl.multiple_of(core * half + z * chunk, 8), chunk)
    o_ref[own_chunk, :] = f1[...] + rx[...]

    to_core = [remote(o_ref.at[own_chunk], o_ref.at[own_chunk], pc)]

    def grows(j, q):
        return pl.ds(pl.multiple_of(core * half + j * chunk + q * sub, 8), sub)

    def arrived(q, jp, jm):
        pending[q][0].wait_recv()
        pending[q][1].wait_recv()
        gp = grows((jp + nz - 1) % nz, q)
        gm = grows((jm + 1) % nz, q)
        to_core.append(remote(o_ref.at[gp, lo], o_ref.at[gp, lo], pc))
        to_core.append(remote(o_ref.at[gm, hi], o_ref.at[gm, hi], pc))

    for s in range(nz - 1):
        jp = (z + nz - s) % nz
        jm = (z + s) % nz
        for q in range(streams):
            if s > 0:
                arrived(q, (jp + 1) % nz, (jm + nz - 1) % nz)
            gp = grows(jp, q)
            gm = grows(jm, q)
            pending[q] = (remote(o_ref.at[gp, lo], o_ref.at[gp, lo], zr),
                          remote(o_ref.at[gm, hi], o_ref.at[gm, hi], zl))
    for q in range(streams):
        arrived(q, (z + 2) % nz, (z + nz - 2) % nz)
    for c in to_core:
        c.wait_recv()

    for c in rs_copies:
        c.wait_recv()
    acc = t_ref[pl.ds(pl.multiple_of(me * owned, 8), owned), :]
    for k in range(1, nc):
        acc = acc + rs_buf[k]
    res_ref[...] = acc.astype(res_ref.dtype)

    for c in sent + rs_copies:
        c.wait_send()


def dp_allreduce(a, t, axis_names):
    rows, cols = a.shape
    nc = lax.axis_size("chan")
    owned = t.shape[0] // nc
    nz = lax.axis_size("dp") // 4
    half = rows // 2
    chunk = half // nz
    lanes = cols // 2
    n_copies = nz + 3 + 6 * (nz - 1) * STREAMS
    vmem = pltpu.VMEM
    return pl.pallas_call(
        functools.partial(_allreduce_kernel, axis_names, nz, nc, STREAMS),
        out_shape=(
            jax.ShapeDtypeStruct((rows, cols), a.dtype),
            jax.ShapeDtypeStruct((owned, t.shape[1]), jnp.bfloat16),
        ),
        in_specs=[pl.BlockSpec(memory_space=vmem)] * 2,
        out_specs=(pl.BlockSpec(memory_space=vmem), pl.BlockSpec(memory_space=vmem)),
        scratch_shapes=[
            vmem((half, cols), a.dtype),
            vmem((half, cols), a.dtype),
            vmem((chunk, cols), a.dtype),
            vmem((chunk, cols), a.dtype),
            vmem((nz - 1, chunk, lanes), a.dtype),
            vmem((nz - 1, chunk, lanes), a.dtype),
            vmem((nz - 1, chunk, lanes), a.dtype),
            vmem((nz - 1, chunk, lanes), a.dtype),
            vmem((nc, owned, t.shape[1]), t.dtype),
            pltpu.SemaphoreType.DMA((n_copies,)),
            pltpu.SemaphoreType.DMA((n_copies,)),
            pltpu.SemaphoreType.DMA((nc,)),
            pltpu.SemaphoreType.DMA((nc,)),
        ],
        compiler_params=pltpu.CompilerParams(
            collective_id=0, has_side_effects=True, vmem_limit_bytes=48 * 1024 * 1024
        ),
    )(a, t)


def _allgather_kernel(axis_names, n, x_ref, o_ref, send_sems, recv_sems):
    rows = x_ref.shape[0]
    MESH = pl.DeviceIdType.MESH
    me = lax.axis_index("chan")

    def dev(p):
        return tuple(p if a == "chan" else lax.axis_index(a) for a in axis_names)

    barrier = pltpu.get_barrier_semaphore()
    for k in range(1, n):
        pl.semaphore_signal(barrier, inc=1, device_id=dev((me + k) % n), device_id_type=MESH)
    pl.semaphore_wait(barrier, n - 1)

    mine = pl.ds(pl.multiple_of(me * rows, 16), rows)
    copies = []
    for k in range(1, n):
        peer = (me + k) % n
        c = pltpu.make_async_remote_copy(
            src_ref=x_ref, dst_ref=o_ref.at[mine], send_sem=send_sems.at[k],
            recv_sem=recv_sems.at[k], device_id=dev(peer), device_id_type=MESH)
        c.start()
        copies.append(c)
    o_ref[mine, :] = x_ref[...]
    for k in range(1, n):
        src = (me + n - k) % n
        theirs = pl.ds(pl.multiple_of(src * rows, 16), rows)
        pltpu.make_async_remote_copy(
            src_ref=x_ref, dst_ref=o_ref.at[theirs], send_sem=send_sems.at[k],
            recv_sem=recv_sems.at[k], device_id=dev(src), device_id_type=MESH).wait_recv()
    for c in copies:
        c.wait_send()


def chan_allgather(x, axis_names):
    rows, cols = x.shape
    n = lax.axis_size("chan")
    vmem = pltpu.VMEM
    return pl.pallas_call(
        functools.partial(_allgather_kernel, axis_names, n),
        out_shape=jax.ShapeDtypeStruct((rows * n, cols), x.dtype),
        in_specs=[pl.BlockSpec(memory_space=vmem)],
        out_specs=pl.BlockSpec(memory_space=vmem),
        scratch_shapes=[pltpu.SemaphoreType.DMA((n,)), pltpu.SemaphoreType.DMA((n,))],
        compiler_params=pltpu.CompilerParams(collective_id=1, has_side_effects=True),
    )(x)


def permute_allgather(x):
    n = lax.axis_size("chan")
    me = lax.axis_index("chan")
    rows = x.shape[0]
    out = jnp.zeros((n * rows,) + x.shape[1:], x.dtype)
    out = lax.dynamic_update_slice_in_dim(out, x, me * rows, axis=0)
    for k in range(1, n):
        got = lax.ppermute(x, "chan", [(j, (j + k) % n) for j in range(n)])
        out = lax.dynamic_update_slice_in_dim(out, got, ((me + n - k) % n) * rows, axis=0)
    return out


def on_device(axis_names, inputs, weight, cotangent):
    input_channels_local = inputs.shape[1]
    cout_local = cotangent.shape[1]
    tap_locations = MAP_HEIGHT * MAP_WIDTH
    feature_map = inputs[0].reshape(input_channels_local, MAP_HEIGHT, MAP_WIDTH)
    tap_list = weight.shape[1]
    output_channels_total = weight.shape[2]
    tap_shifts = [
        (DILATION_RATE * (tap_index // 3 - 1), DILATION_RATE * (tap_index % 3 - 1))
        for tap_index in range(tap_list)
    ]
    displaced_input = [
        translated_input(feature_map, first_operand, second_operand, DILATION_RATE).reshape(
            input_channels_local, tap_locations
        )
        for first_operand, second_operand in tap_shifts
    ]
    flat_grads = permute_allgather(cotangent[0])
    contract_cols = (((1,), (1,)), ((), ()))
    local_grad = jnp.stack(
        [
            lax.dot_general(
                displaced_input[tap_index],
                flat_grads,
                contract_cols,
                preferred_element_type=jnp.float32,
            )
            for tap_index in range(tap_list)
        ],
        axis=0,
    )
    contract_rows = (((0,), (0,)), ((), ()))
    total = jnp.zeros((cout_local * lax.axis_size("chan"), tap_locations), jnp.float32)
    for tap_index in range(tap_list):
        columns = weight[:, tap_index, :]
        total = total + lax.dot_general(
            columns, displaced_input[tap_index], contract_rows, preferred_element_type=jnp.float32
        )
    summed, owned = dp_allreduce(
        local_grad.reshape(tap_list * input_channels_local, output_channels_total), total, axis_names
    )
    result = owned.reshape(1, cout_local, tap_locations)
    summed_grad = jnp.transpose(
        summed.reshape(tap_list, input_channels_local, output_channels_total), (1, 0, 2)
    )
    weight_grad = summed_grad / jnp.float32(lax.axis_size("dp"))

    collected_input = flat_grads.reshape(output_channels_total, MAP_HEIGHT, MAP_WIDTH)
    back_sum = jnp.zeros((input_channels_local, tap_locations), jnp.float32)
    for tap_index in range(tap_list):
        row_shift, column_shift = tap_shifts[tap_index]
        displaced_gradient = translated_input(
            collected_input, -row_shift, -column_shift, DILATION_RATE
        ).reshape(output_channels_total, tap_locations)
        back_sum = back_sum + jnp.dot(
            weight[:, tap_index, :], displaced_gradient, preferred_element_type=jnp.float32
        )
    input_grad = back_sum.astype(jnp.bfloat16).reshape(1, input_channels_local, tap_locations)
    return (result, input_grad, weight_grad)


def solution(mesh):
    placed = (P("dp", "chan", None), P("chan", None, None), P("dp", "chan", None))
    return jax.shard_map(
        functools.partial(on_device, tuple(mesh.axis_names)),
        mesh=mesh,
        in_specs=placed,
        out_specs=(P("dp", "chan", None), P("dp", "chan", None), P("chan", None, None)),
        check_vma=False,
    )
```

```python
import functools

import jax
import jax.numpy as jnp
from jax import lax
from jax.experimental import pallas as pl
from jax.experimental.pallas import tpu as pltpu
from jax.sharding import PartitionSpec as P

DILATION_RATE = 12
MAP_HEIGHT = 16
MAP_WIDTH = 72
STREAMS = 3


def translated_input(receptive_field, row_shift, column_shift, reach):
    height, width = (receptive_field.shape[1], receptive_field.shape[2])
    bordered_input = jnp.pad(receptive_field, ((0, 0), (reach, reach), (reach, reach)))
    return bordered_input[
        :,
        reach + row_shift : reach + row_shift + height,
        reach + column_shift : reach + column_shift + width,
    ]


def _allreduce_kernel(axis_names, nz, nc, streams, a_ref, t_ref, w_ref, g_ref, o_ref, res_ref,
                      ig_ref, rc, s1, f1, rx, rp, rm, ap, am, rs_buf, ig_acc, send_sems, recv_sems,
                      rs_send, rs_recv):
    rows, cols = a_ref.shape
    half = rows // 2
    chunk = half // nz
    lanes = cols // 2
    MESH = pl.DeviceIdType.MESH
    dp = lax.axis_index("dp")
    core = dp % 2
    xl = (dp // 2) % 2
    z = dp // 4
    nd = 4 * nz
    pc = dp + 1 - 2 * core
    px = dp + 2 - 4 * xl
    zr = (dp + 4) % nd
    zl = (dp + nd - 4) % nd

    me = lax.axis_index("chan")

    def dev(p):
        return tuple(p if n == "dp" else lax.axis_index(n) for n in axis_names)

    def cdev(p):
        return tuple(p if n == "chan" else lax.axis_index(n) for n in axis_names)

    barrier = pltpu.get_barrier_semaphore()
    for peer in (pc, px, zr, zl):
        pl.semaphore_signal(barrier, inc=1, device_id=dev(peer), device_id_type=MESH)
    for k in range(1, nc):
        pl.semaphore_signal(barrier, inc=1, device_id=cdev((me + k) % nc), device_id_type=MESH)
    pl.semaphore_wait(barrier, 4 + nc - 1)

    owned = res_ref.shape[0]
    rs_copies = []
    for k in range(1, nc):
        peer = (me + k) % nc
        c = pltpu.make_async_remote_copy(
            src_ref=t_ref.at[pl.ds(pl.multiple_of(peer * owned, 8), owned)],
            dst_ref=rs_buf.at[k], send_sem=rs_send.at[k], recv_sem=rs_recv.at[k],
            device_id=cdev(peer), device_id_type=MESH)
        c.start()
        rs_copies.append(c)

    sent = []
    counter = [0]

    def remote(src, dst, peer):
        k = counter[0]
        counter[0] += 1
        c = pltpu.make_async_remote_copy(
            src_ref=src, dst_ref=dst, send_sem=send_sems.at[k], recv_sem=recv_sems.at[k],
            device_id=dev(peer), device_id_type=MESH)
        c.start()
        sent.append(c)
        return c

    def rows_of(j):
        return pl.ds(pl.multiple_of(j * chunk, 8), chunk)

    taps = w_ref.shape[0]
    done_taps = [0]

    def input_grad_tap():
        t = done_taps[0]
        if t < taps:
            term = jnp.dot(w_ref[t], g_ref[t], preferred_element_type=jnp.float32)
            if t == 0:
                ig_acc[...] = term
            else:
                ig_acc[...] += term
            done_taps[0] += 1

    mine_c = core * half
    other_c = (1 - core) * half
    order = []
    for d in range(1, nz // 2 + 1):
        order.append((z + nz - d) % nz)
        if 2 * d != nz:
            order.append((z + d) % nz)
    order.append(z)
    core_in = []
    for j in order:
        src_rows = pl.ds(pl.multiple_of(other_c + j * chunk, 8), chunk)
        core_in.append((j, remote(a_ref.at[src_rows], rc.at[rows_of(j)], pc)))
    ready = [0]

    def ready_upto(n):
        while ready[0] < n:
            j, c = core_in[ready[0]]
            c.wait_recv()
            own_rows = pl.ds(pl.multiple_of(mine_c + j * chunk, 8), chunk)
            s1[rows_of(j), :] = a_ref[own_rows, :] + rc[rows_of(j), :]
            ready[0] += 1

    def needed(d):
        return min(len(order) - 1, 2 * d - (1 if 2 * d == nz else 0))

    lo = pl.ds(0, lanes)
    hi = pl.ds(lanes, lanes)
    sub = chunk // streams

    def srows(j, q):
        return pl.ds(pl.multiple_of(j * chunk + q * sub, 8), sub)

    blk = [pl.ds(q * sub, sub) for q in range(streams)]
    pending = [None] * streams
    for s in range(nz - 1):
        jp = (z + 2 * nz - 1 - s) % nz
        jm = (z + 1 + s) % nz
        if s + 1 <= nz // 2:
            ready_upto(needed(s + 1))
        for q in range(streams):
            if s == 0:
                src_p = s1.at[srows(jp, q), lo]
                src_m = s1.at[srows(jm, q), hi]
            else:
                pending[q][0].wait_recv()
                pending[q][1].wait_recv()
                ap[s, blk[q], :] = s1[srows(jp, q), lo] + rp[s - 1, blk[q], :]
                am[s, blk[q], :] = s1[srows(jm, q), hi] + rm[s - 1, blk[q], :]
                src_p = ap.at[s, blk[q]]
                src_m = am.at[s, blk[q]]
            pending[q] = (remote(src_p, rp.at[s, blk[q]], zr), remote(src_m, rm.at[s, blk[q]], zl))
    for q in range(streams):
        pending[q][0].wait_recv()
        pending[q][1].wait_recv()
    ready_upto(len(order))
    f1[:, lo] = s1[rows_of(z), lo] + rp[nz - 2]
    f1[:, hi] = s1[rows_of(z), hi] + rm[nz - 2]

    c = remote(f1, rx, px)
    c.wait_recv()
    own_chunk = pl.ds(pl.multiple_of(core * half + z * chunk, 8), chunk)
    o_ref[own_chunk, :] = f1[...] + rx[...]

    to_core = [remote(o_ref.at[own_chunk], o_ref.at[own_chunk], pc)]

    def grows(j, q):
        return pl.ds(pl.multiple_of(core * half + j * chunk + q * sub, 8), sub)

    def arrived(q, jp, jm):
        pending[q][0].wait_recv()
        pending[q][1].wait_recv()
        gp = grows((jp + nz - 1) % nz, q)
        gm = grows((jm + 1) % nz, q)
        to_core.append(remote(o_ref.at[gp, lo], o_ref.at[gp, lo], pc))
        to_core.append(remote(o_ref.at[gm, hi], o_ref.at[gm, hi], pc))

    for s in range(nz - 1):
        jp = (z + nz - s) % nz
        jm = (z + s) % nz
        for q in range(streams):
            if s > 0:
                arrived(q, (jp + 1) % nz, (jm + nz - 1) % nz)
            gp = grows(jp, q)
            gm = grows(jm, q)
            pending[q] = (remote(o_ref.at[gp, lo], o_ref.at[gp, lo], zr),
                          remote(o_ref.at[gm, hi], o_ref.at[gm, hi], zl))
        input_grad_tap()
        if s == nz - 2:
            while done_taps[0] < taps:
                input_grad_tap()
    for q in range(streams):
        arrived(q, (z + 2) % nz, (z + nz - 2) % nz)
    for c in to_core:
        c.wait_recv()

    for c in rs_copies:
        c.wait_recv()
    acc = t_ref[pl.ds(pl.multiple_of(me * owned, 8), owned), :]
    for k in range(1, nc):
        acc = acc + rs_buf[k]
    res_ref[...] = acc.astype(res_ref.dtype)
    ig_ref[...] = ig_acc[...].astype(ig_ref.dtype)

    for c in sent + rs_copies:
        c.wait_send()


def dp_allreduce(a, t, w, g, axis_names):
    rows, cols = a.shape
    nc = lax.axis_size("chan")
    owned = t.shape[0] // nc
    nz = lax.axis_size("dp") // 4
    half = rows // 2
    chunk = half // nz
    lanes = cols // 2
    n_copies = nz + 3 + 6 * (nz - 1) * STREAMS
    vmem = pltpu.VMEM
    return pl.pallas_call(
        functools.partial(_allreduce_kernel, axis_names, nz, nc, STREAMS),
        out_shape=(
            jax.ShapeDtypeStruct((rows, cols), a.dtype),
            jax.ShapeDtypeStruct((owned, t.shape[1]), jnp.bfloat16),
            jax.ShapeDtypeStruct((w.shape[1], g.shape[2]), jnp.bfloat16),
        ),
        in_specs=[pl.BlockSpec(memory_space=vmem)] * 4,
        out_specs=(pl.BlockSpec(memory_space=vmem),) * 3,
        scratch_shapes=[
            vmem((half, cols), a.dtype),
            vmem((half, cols), a.dtype),
            vmem((chunk, cols), a.dtype),
            vmem((chunk, cols), a.dtype),
            vmem((nz - 1, chunk, lanes), a.dtype),
            vmem((nz - 1, chunk, lanes), a.dtype),
            vmem((nz - 1, chunk, lanes), a.dtype),
            vmem((nz - 1, chunk, lanes), a.dtype),
            vmem((nc, owned, t.shape[1]), t.dtype),
            vmem((w.shape[1], g.shape[2]), jnp.float32),
            pltpu.SemaphoreType.DMA((n_copies,)),
            pltpu.SemaphoreType.DMA((n_copies,)),
            pltpu.SemaphoreType.DMA((nc,)),
            pltpu.SemaphoreType.DMA((nc,)),
        ],
        compiler_params=pltpu.CompilerParams(
            collective_id=0, has_side_effects=True, vmem_limit_bytes=48 * 1024 * 1024
        ),
    )(a, t, w, g)


def _allgather_kernel(axis_names, n, x_ref, o_ref, send_sems, recv_sems):
    rows = x_ref.shape[0]
    MESH = pl.DeviceIdType.MESH
    me = lax.axis_index("chan")

    def dev(p):
        return tuple(p if a == "chan" else lax.axis_index(a) for a in axis_names)

    barrier = pltpu.get_barrier_semaphore()
    for k in range(1, n):
        pl.semaphore_signal(barrier, inc=1, device_id=dev((me + k) % n), device_id_type=MESH)
    pl.semaphore_wait(barrier, n - 1)

    mine = pl.ds(pl.multiple_of(me * rows, 16), rows)
    copies = []
    for k in range(1, n):
        peer = (me + k) % n
        c = pltpu.make_async_remote_copy(
            src_ref=x_ref, dst_ref=o_ref.at[mine], send_sem=send_sems.at[k],
            recv_sem=recv_sems.at[k], device_id=dev(peer), device_id_type=MESH)
        c.start()
        copies.append(c)
    o_ref[mine, :] = x_ref[...]
    for k in range(1, n):
        src = (me + n - k) % n
        theirs = pl.ds(pl.multiple_of(src * rows, 16), rows)
        pltpu.make_async_remote_copy(
            src_ref=x_ref, dst_ref=o_ref.at[theirs], send_sem=send_sems.at[k],
            recv_sem=recv_sems.at[k], device_id=dev(src), device_id_type=MESH).wait_recv()
    for c in copies:
        c.wait_send()


def chan_allgather(x, axis_names):
    rows, cols = x.shape
    n = lax.axis_size("chan")
    vmem = pltpu.VMEM
    return pl.pallas_call(
        functools.partial(_allgather_kernel, axis_names, n),
        out_shape=jax.ShapeDtypeStruct((rows * n, cols), x.dtype),
        in_specs=[pl.BlockSpec(memory_space=vmem)],
        out_specs=pl.BlockSpec(memory_space=vmem),
        scratch_shapes=[pltpu.SemaphoreType.DMA((n,)), pltpu.SemaphoreType.DMA((n,))],
        compiler_params=pltpu.CompilerParams(collective_id=1, has_side_effects=True),
    )(x)


def on_device(axis_names, inputs, weight, cotangent):
    input_channels_local = inputs.shape[1]
    cout_local = cotangent.shape[1]
    tap_locations = MAP_HEIGHT * MAP_WIDTH
    feature_map = inputs[0].reshape(input_channels_local, MAP_HEIGHT, MAP_WIDTH)
    tap_list = weight.shape[1]
    output_channels_total = weight.shape[2]
    tap_shifts = [
        (DILATION_RATE * (tap_index // 3 - 1), DILATION_RATE * (tap_index % 3 - 1))
        for tap_index in range(tap_list)
    ]
    displaced_input = [
        translated_input(feature_map, first_operand, second_operand, DILATION_RATE).reshape(
            input_channels_local, tap_locations
        )
        for first_operand, second_operand in tap_shifts
    ]
    flat_grads = chan_allgather(cotangent[0], axis_names)
    contract_cols = (((1,), (1,)), ((), ()))
    local_grad = jnp.stack(
        [
            lax.dot_general(
                displaced_input[tap_index],
                flat_grads,
                contract_cols,
                preferred_element_type=jnp.float32,
            )
            for tap_index in range(tap_list)
        ],
        axis=0,
    )
    contract_rows = (((0,), (0,)), ((), ()))
    total = jnp.zeros((cout_local * lax.axis_size("chan"), tap_locations), jnp.float32)
    for tap_index in range(tap_list):
        columns = weight[:, tap_index, :]
        total = total + lax.dot_general(
            columns, displaced_input[tap_index], contract_rows, preferred_element_type=jnp.float32
        )
    collected_input = flat_grads.reshape(output_channels_total, MAP_HEIGHT, MAP_WIDTH)
    displaced_gradient = jnp.stack(
        [
            translated_input(collected_input, -row_shift, -column_shift, DILATION_RATE).reshape(
                output_channels_total, tap_locations
            )
            for row_shift, column_shift in tap_shifts
        ]
    )
    summed, owned, back = dp_allreduce(
        local_grad.reshape(tap_list * input_channels_local, output_channels_total),
        total,
        jnp.transpose(weight, (1, 0, 2)),
        displaced_gradient,
        axis_names,
    )
    result = owned.reshape(1, cout_local, tap_locations)
    summed_grad = jnp.transpose(
        summed.reshape(tap_list, input_channels_local, output_channels_total), (1, 0, 2)
    )
    weight_grad = summed_grad / jnp.float32(lax.axis_size("dp"))
    input_grad = back.reshape(1, input_channels_local, tap_locations)
    return (result, input_grad, weight_grad)


def solution(mesh):
    placed = (P("dp", "chan", None), P("chan", None, None), P("dp", "chan", None))
    return jax.shard_map(
        functools.partial(on_device, tuple(mesh.axis_names)),
        mesh=mesh,
        in_specs=placed,
        out_specs=(P("dp", "chan", None), P("dp", "chan", None), P("chan", None, None)),
        check_vma=False,
    )
```

```python
import functools

import jax
import jax.numpy as jnp
import numpy as np
from jax import lax
from jax.experimental import pallas as pl
from jax.experimental.pallas import tpu as pltpu
from jax.sharding import PartitionSpec as P

DILATION_RATE = 12
MAP_HEIGHT = 16
MAP_WIDTH = 72
STREAMS = 3


def translated_input(receptive_field, row_shift, column_shift, reach):
    height, width = (receptive_field.shape[1], receptive_field.shape[2])
    bordered_input = jnp.pad(receptive_field, ((0, 0), (reach, reach), (reach, reach)))
    return bordered_input[
        :,
        reach + row_shift : reach + row_shift + height,
        reach + column_shift : reach + column_shift + width,
    ]


def _allreduce_kernel(axis_names, nz, nc, streams, a_ref, t_ref, o_ref, res_ref, rc, s1, f1, rx, rp, rm,
                      ap, am, rs_buf, send_sems, recv_sems, rs_send, rs_recv):
    rows, cols = a_ref.shape
    half = rows // 2
    chunk = half // nz
    lanes = cols // 2
    MESH = pl.DeviceIdType.MESH
    dp = lax.axis_index("dp")
    core = dp % 2
    xl = (dp // 2) % 2
    z = dp // 4
    nd = 4 * nz
    pc = dp + 1 - 2 * core
    px = dp + 2 - 4 * xl
    zr = (dp + 4) % nd
    zl = (dp + nd - 4) % nd

    me = lax.axis_index("chan")

    def dev(p):
        return tuple(p if n == "dp" else lax.axis_index(n) for n in axis_names)

    def cdev(p):
        return tuple(p if n == "chan" else lax.axis_index(n) for n in axis_names)

    barrier = pltpu.get_barrier_semaphore()
    for peer in (pc, px, zr, zl):
        pl.semaphore_signal(barrier, inc=1, device_id=dev(peer), device_id_type=MESH)
    for k in range(1, nc):
        pl.semaphore_signal(barrier, inc=1, device_id=cdev((me + k) % nc), device_id_type=MESH)
    pl.semaphore_wait(barrier, 4 + nc - 1)

    owned = res_ref.shape[0]
    rs_copies = []
    for k in range(1, nc):
        peer = (me + k) % nc
        c = pltpu.make_async_remote_copy(
            src_ref=t_ref.at[pl.ds(pl.multiple_of(peer * owned, 8), owned)],
            dst_ref=rs_buf.at[k], send_sem=rs_send.at[k], recv_sem=rs_recv.at[k],
            device_id=cdev(peer), device_id_type=MESH)
        c.start()
        rs_copies.append(c)

    sent = []
    counter = [0]

    def remote(src, dst, peer):
        k = counter[0]
        counter[0] += 1
        c = pltpu.make_async_remote_copy(
            src_ref=src, dst_ref=dst, send_sem=send_sems.at[k], recv_sem=recv_sems.at[k],
            device_id=dev(peer), device_id_type=MESH)
        c.start()
        sent.append(c)
        return c

    def rows_of(j):
        return pl.ds(pl.multiple_of(j * chunk, 8), chunk)

    mine_c = core * half
    other_c = (1 - core) * half
    order = []
    for d in range(1, nz // 2 + 1):
        order.append((z + nz - d) % nz)
        if 2 * d != nz:
            order.append((z + d) % nz)
    order.append(z)
    core_in = []
    for j in order:
        src_rows = pl.ds(pl.multiple_of(other_c + j * chunk, 8), chunk)
        core_in.append((j, remote(a_ref.at[src_rows], rc.at[rows_of(j)], pc)))
    ready = [0]

    def ready_upto(n):
        while ready[0] < n:
            j, c = core_in[ready[0]]
            c.wait_recv()
            own_rows = pl.ds(pl.multiple_of(mine_c + j * chunk, 8), chunk)
            s1[rows_of(j), :] = a_ref[own_rows, :] + rc[rows_of(j), :]
            ready[0] += 1

    def needed(d):
        return min(len(order) - 1, 2 * d - (1 if 2 * d == nz else 0))

    lo = pl.ds(0, lanes)
    hi = pl.ds(lanes, lanes)
    sub = chunk // streams

    def srows(j, q):
        return pl.ds(pl.multiple_of(j * chunk + q * sub, 8), sub)

    blk = [pl.ds(q * sub, sub) for q in range(streams)]
    pending = [None] * streams
    for s in range(nz - 1):
        jp = (z + 2 * nz - 1 - s) % nz
        jm = (z + 1 + s) % nz
        if s + 1 <= nz // 2:
            ready_upto(needed(s + 1))
        for q in range(streams):
            if s == 0:
                src_p = s1.at[srows(jp, q), lo]
                src_m = s1.at[srows(jm, q), hi]
            else:
                pending[q][0].wait_recv()
                pending[q][1].wait_recv()
                ap[s, blk[q], :] = s1[srows(jp, q), lo] + rp[s - 1, blk[q], :]
                am[s, blk[q], :] = s1[srows(jm, q), hi] + rm[s - 1, blk[q], :]
                src_p = ap.at[s, blk[q]]
                src_m = am.at[s, blk[q]]
            pending[q] = (remote(src_p, rp.at[s, blk[q]], zr), remote(src_m, rm.at[s, blk[q]], zl))
    for q in range(streams):
        pending[q][0].wait_recv()
        pending[q][1].wait_recv()
    ready_upto(len(order))
    f1[:, lo] = s1[rows_of(z), lo] + rp[nz - 2]
    f1[:, hi] = s1[rows_of(z), hi] + rm[nz - 2]

    c = remote(f1, rx, px)
    c.wait_recv()
    own_chunk = pl.ds(pl.multiple_of(core * half + z * chunk, 8), chunk)
    o_ref[own_chunk, :] = f1[...] + rx[...]

    to_core = [remote(o_ref.at[own_chunk], o_ref.at[own_chunk], pc)]

    def grows(j, q):
        return pl.ds(pl.multiple_of(core * half + j * chunk + q * sub, 8), sub)

    def arrived(q, jp, jm):
        pending[q][0].wait_recv()
        pending[q][1].wait_recv()
        gp = grows((jp + nz - 1) % nz, q)
        gm = grows((jm + 1) % nz, q)
        to_core.append(remote(o_ref.at[gp, lo], o_ref.at[gp, lo], pc))
        to_core.append(remote(o_ref.at[gm, hi], o_ref.at[gm, hi], pc))

    for s in range(nz - 1):
        jp = (z + nz - s) % nz
        jm = (z + s) % nz
        for q in range(streams):
            if s > 0:
                arrived(q, (jp + 1) % nz, (jm + nz - 1) % nz)
            gp = grows(jp, q)
            gm = grows(jm, q)
            pending[q] = (remote(o_ref.at[gp, lo], o_ref.at[gp, lo], zr),
                          remote(o_ref.at[gm, hi], o_ref.at[gm, hi], zl))
    for q in range(streams):
        arrived(q, (z + 2) % nz, (z + nz - 2) % nz)
    for c in to_core:
        c.wait_recv()

    for c in rs_copies:
        c.wait_recv()
    acc = t_ref[pl.ds(pl.multiple_of(me * owned, 8), owned), :]
    for k in range(1, nc):
        acc = acc + rs_buf[k]
    res_ref[...] = acc.astype(res_ref.dtype)

    for c in sent + rs_copies:
        c.wait_send()


def dp_allreduce(a, t, axis_names):
    rows, cols = a.shape
    nc = lax.axis_size("chan")
    owned = t.shape[0] // nc
    nz = lax.axis_size("dp") // 4
    half = rows // 2
    chunk = half // nz
    lanes = cols // 2
    n_copies = nz + 3 + 6 * (nz - 1) * STREAMS
    vmem = pltpu.VMEM
    return pl.pallas_call(
        functools.partial(_allreduce_kernel, axis_names, nz, nc, STREAMS),
        out_shape=(
            jax.ShapeDtypeStruct((rows, cols), a.dtype),
            jax.ShapeDtypeStruct((owned, t.shape[1]), jnp.bfloat16),
        ),
        in_specs=[pl.BlockSpec(memory_space=vmem)] * 2,
        out_specs=(pl.BlockSpec(memory_space=vmem), pl.BlockSpec(memory_space=vmem)),
        scratch_shapes=[
            vmem((half, cols), a.dtype),
            vmem((half, cols), a.dtype),
            vmem((chunk, cols), a.dtype),
            vmem((chunk, cols), a.dtype),
            vmem((nz - 1, chunk, lanes), a.dtype),
            vmem((nz - 1, chunk, lanes), a.dtype),
            vmem((nz - 1, chunk, lanes), a.dtype),
            vmem((nz - 1, chunk, lanes), a.dtype),
            vmem((nc, owned, t.shape[1]), t.dtype),
            pltpu.SemaphoreType.DMA((n_copies,)),
            pltpu.SemaphoreType.DMA((n_copies,)),
            pltpu.SemaphoreType.DMA((nc,)),
            pltpu.SemaphoreType.DMA((nc,)),
        ],
        compiler_params=pltpu.CompilerParams(
            collective_id=0, has_side_effects=True, vmem_limit_bytes=48 * 1024 * 1024
        ),
    )(a, t)


def _allgather_kernel(axis_names, n, shifts, x_ref, w_ref, f_ref, m_ref, o_ref, t_ref,
                      send_sems, recv_sems):
    rows = x_ref.shape[0]
    MESH = pl.DeviceIdType.MESH
    me = lax.axis_index("chan")

    def dev(p):
        return tuple(p if a == "chan" else lax.axis_index(a) for a in axis_names)

    barrier = pltpu.get_barrier_semaphore()
    for k in range(1, n):
        pl.semaphore_signal(barrier, inc=1, device_id=dev((me + k) % n), device_id_type=MESH)
    pl.semaphore_wait(barrier, n - 1)

    mine = pl.ds(pl.multiple_of(me * rows, 16), rows)
    copies = []
    for k in range(1, n):
        peer = (me + k) % n
        c = pltpu.make_async_remote_copy(
            src_ref=x_ref, dst_ref=o_ref.at[mine], send_sem=send_sems.at[k],
            recv_sem=recv_sems.at[k], device_id=dev(peer), device_id_type=MESH)
        c.start()
        copies.append(c)
    o_ref[mine, :] = x_ref[...]
    size = f_ref.shape[1]
    for t, shift in enumerate(shifts):
        y = jnp.dot(w_ref[t], f_ref[...], preferred_element_type=jnp.float32)
        if shift % size:
            y = pltpu.roll(y, (-shift) % size, 1)
        y = y * m_ref[pl.ds(t, 1), :]
        if t == 0:
            t_ref[...] = y
        else:
            t_ref[...] += y
    for k in range(1, n):
        src = (me + n - k) % n
        theirs = pl.ds(pl.multiple_of(src * rows, 16), rows)
        pltpu.make_async_remote_copy(
            src_ref=x_ref, dst_ref=o_ref.at[theirs], send_sem=send_sems.at[k],
            recv_sem=recv_sems.at[k], device_id=dev(src), device_id_type=MESH).wait_recv()
    for c in copies:
        c.wait_send()


def chan_allgather(x, axis_names, w, f, masks, shifts):
    rows, cols = x.shape
    n = lax.axis_size("chan")
    vmem = pltpu.VMEM
    return pl.pallas_call(
        functools.partial(_allgather_kernel, axis_names, n, shifts),
        out_shape=(
            jax.ShapeDtypeStruct((rows * n, cols), x.dtype),
            jax.ShapeDtypeStruct((w.shape[1], f.shape[1]), jnp.float32),
        ),
        in_specs=[pl.BlockSpec(memory_space=vmem)] * 4,
        out_specs=(pl.BlockSpec(memory_space=vmem),) * 2,
        scratch_shapes=[pltpu.SemaphoreType.DMA((n,)), pltpu.SemaphoreType.DMA((n,))],
        compiler_params=pltpu.CompilerParams(
            collective_id=1, has_side_effects=True, vmem_limit_bytes=48 * 1024 * 1024
        ),
    )(x, w, f, masks)


def on_device(axis_names, inputs, weight, cotangent):
    input_channels_local = inputs.shape[1]
    cout_local = cotangent.shape[1]
    tap_locations = MAP_HEIGHT * MAP_WIDTH
    feature_map = inputs[0].reshape(input_channels_local, MAP_HEIGHT, MAP_WIDTH)
    tap_list = weight.shape[1]
    output_channels_total = weight.shape[2]
    tap_shifts = [
        (DILATION_RATE * (tap_index // 3 - 1), DILATION_RATE * (tap_index % 3 - 1))
        for tap_index in range(tap_list)
    ]
    displaced_input = [
        translated_input(feature_map, first_operand, second_operand, DILATION_RATE).reshape(
            input_channels_local, tap_locations
        )
        for first_operand, second_operand in tap_shifts
    ]
    rows_idx = np.arange(tap_locations) // MAP_WIDTH
    cols_idx = np.arange(tap_locations) % MAP_WIDTH
    masks = np.stack(
        [
            ((rows_idx + a >= 0) & (rows_idx + a < MAP_HEIGHT) & (cols_idx + b >= 0) & (cols_idx + b < MAP_WIDTH))
            for a, b in tap_shifts
        ]
    ).astype(np.float32)
    flat_grads, total = chan_allgather(
        cotangent[0],
        axis_names,
        jnp.transpose(weight, (1, 2, 0)),
        inputs[0],
        jnp.asarray(masks),
        tuple(a * MAP_WIDTH + b for a, b in tap_shifts),
    )
    contract_cols = (((1,), (1,)), ((), ()))
    local_grad = jnp.stack(
        [
            lax.dot_general(
                displaced_input[tap_index],
                flat_grads,
                contract_cols,
                preferred_element_type=jnp.float32,
            )
            for tap_index in range(tap_list)
        ],
        axis=0,
    )
    summed, owned = dp_allreduce(
        local_grad.reshape(tap_list * input_channels_local, output_channels_total), total, axis_names
    )
    result = owned.reshape(1, cout_local, tap_locations)
    summed_grad = jnp.transpose(
        summed.reshape(tap_list, input_channels_local, output_channels_total), (1, 0, 2)
    )
    weight_grad = summed_grad / jnp.float32(lax.axis_size("dp"))

    collected_input = flat_grads.reshape(output_channels_total, MAP_HEIGHT, MAP_WIDTH)
    back_sum = jnp.zeros((input_channels_local, tap_locations), jnp.float32)
    for tap_index in range(tap_list):
        row_shift, column_shift = tap_shifts[tap_index]
        displaced_gradient = translated_input(
            collected_input, -row_shift, -column_shift, DILATION_RATE
        ).reshape(output_channels_total, tap_locations)
        back_sum = back_sum + jnp.dot(
            weight[:, tap_index, :], displaced_gradient, preferred_element_type=jnp.float32
        )
    input_grad = back_sum.astype(jnp.bfloat16).reshape(1, input_channels_local, tap_locations)
    return (result, input_grad, weight_grad)


def solution(mesh):
    placed = (P("dp", "chan", None), P("chan", None, None), P("dp", "chan", None))
    return jax.shard_map(
        functools.partial(on_device, tuple(mesh.axis_names)),
        mesh=mesh,
        in_specs=placed,
        out_specs=(P("dp", "chan", None), P("dp", "chan", None), P("chan", None, None)),
        check_vma=False,
    )
```

```python
import functools

import jax
import jax.numpy as jnp
import numpy as np
from jax import lax
from jax.experimental import pallas as pl
from jax.experimental.pallas import tpu as pltpu
from jax.sharding import PartitionSpec as P

DILATION_RATE = 12
MAP_HEIGHT = 16
MAP_WIDTH = 72
STREAMS = 3


def translated_input(receptive_field, row_shift, column_shift, reach):
    height, width = (receptive_field.shape[1], receptive_field.shape[2])
    bordered_input = jnp.pad(receptive_field, ((0, 0), (reach, reach), (reach, reach)))
    return bordered_input[
        :,
        reach + row_shift : reach + row_shift + height,
        reach + column_shift : reach + column_shift + width,
    ]


def _allreduce_kernel(axis_names, nz, nc, streams, shifts, a_ref, t_ref, w_ref, g_ref, m_ref,
                      o_ref, res_ref, ig_ref, rc, s1, f1, rx, rp, rm, ap, am, rs_buf, ig_acc,
                      send_sems, recv_sems, rs_send, rs_recv):
    rows, cols = a_ref.shape
    half = rows // 2
    chunk = half // nz
    lanes = cols // 2
    MESH = pl.DeviceIdType.MESH
    dp = lax.axis_index("dp")
    core = dp % 2
    xl = (dp // 2) % 2
    z = dp // 4
    nd = 4 * nz
    pc = dp + 1 - 2 * core
    px = dp + 2 - 4 * xl
    zr = (dp + 4) % nd
    zl = (dp + nd - 4) % nd

    me = lax.axis_index("chan")

    def dev(p):
        return tuple(p if n == "dp" else lax.axis_index(n) for n in axis_names)

    def cdev(p):
        return tuple(p if n == "chan" else lax.axis_index(n) for n in axis_names)

    barrier = pltpu.get_barrier_semaphore()
    for peer in (pc, px, zr, zl):
        pl.semaphore_signal(barrier, inc=1, device_id=dev(peer), device_id_type=MESH)
    for k in range(1, nc):
        pl.semaphore_signal(barrier, inc=1, device_id=cdev((me + k) % nc), device_id_type=MESH)
    pl.semaphore_wait(barrier, 4 + nc - 1)

    owned = res_ref.shape[0]
    rs_copies = []
    for k in range(1, nc):
        peer = (me + k) % nc
        c = pltpu.make_async_remote_copy(
            src_ref=t_ref.at[pl.ds(pl.multiple_of(peer * owned, 8), owned)],
            dst_ref=rs_buf.at[k], send_sem=rs_send.at[k], recv_sem=rs_recv.at[k],
            device_id=cdev(peer), device_id_type=MESH)
        c.start()
        rs_copies.append(c)

    sent = []
    counter = [0]

    def remote(src, dst, peer):
        k = counter[0]
        counter[0] += 1
        c = pltpu.make_async_remote_copy(
            src_ref=src, dst_ref=dst, send_sem=send_sems.at[k], recv_sem=recv_sems.at[k],
            device_id=dev(peer), device_id_type=MESH)
        c.start()
        sent.append(c)
        return c

    def rows_of(j):
        return pl.ds(pl.multiple_of(j * chunk, 8), chunk)

    done_taps = [0]
    size = g_ref.shape[1]

    def input_grad_tap():
        t = done_taps[0]
        if t < len(shifts):
            y = jnp.dot(w_ref[t], g_ref[...], preferred_element_type=jnp.float32)
            if shifts[t] % size:
                y = pltpu.roll(y, shifts[t] % size, 1)
            y = y * m_ref[pl.ds(t, 1), :]
            if t == 0:
                ig_acc[...] = y
            else:
                ig_acc[...] += y
            done_taps[0] += 1

    mine_c = core * half
    other_c = (1 - core) * half
    order = []
    for d in range(1, nz // 2 + 1):
        order.append((z + nz - d) % nz)
        if 2 * d != nz:
            order.append((z + d) % nz)
    order.append(z)
    core_in = []
    for j in order:
        src_rows = pl.ds(pl.multiple_of(other_c + j * chunk, 8), chunk)
        core_in.append((j, remote(a_ref.at[src_rows], rc.at[rows_of(j)], pc)))
    ready = [0]

    def ready_upto(n):
        while ready[0] < n:
            j, c = core_in[ready[0]]
            c.wait_recv()
            own_rows = pl.ds(pl.multiple_of(mine_c + j * chunk, 8), chunk)
            s1[rows_of(j), :] = a_ref[own_rows, :] + rc[rows_of(j), :]
            ready[0] += 1

    def needed(d):
        return min(len(order) - 1, 2 * d - (1 if 2 * d == nz else 0))

    lo = pl.ds(0, lanes)
    hi = pl.ds(lanes, lanes)
    sub = chunk // streams

    def srows(j, q):
        return pl.ds(pl.multiple_of(j * chunk + q * sub, 8), sub)

    blk = [pl.ds(q * sub, sub) for q in range(streams)]
    pending = [None] * streams
    for s in range(nz - 1):
        jp = (z + 2 * nz - 1 - s) % nz
        jm = (z + 1 + s) % nz
        if s + 1 <= nz // 2:
            ready_upto(needed(s + 1))
        for q in range(streams):
            if s == 0:
                src_p = s1.at[srows(jp, q), lo]
                src_m = s1.at[srows(jm, q), hi]
            else:
                pending[q][0].wait_recv()
                pending[q][1].wait_recv()
                ap[s, blk[q], :] = s1[srows(jp, q), lo] + rp[s - 1, blk[q], :]
                am[s, blk[q], :] = s1[srows(jm, q), hi] + rm[s - 1, blk[q], :]
                src_p = ap.at[s, blk[q]]
                src_m = am.at[s, blk[q]]
            pending[q] = (remote(src_p, rp.at[s, blk[q]], zr), remote(src_m, rm.at[s, blk[q]], zl))
    for q in range(streams):
        pending[q][0].wait_recv()
        pending[q][1].wait_recv()
    ready_upto(len(order))
    f1[:, lo] = s1[rows_of(z), lo] + rp[nz - 2]
    f1[:, hi] = s1[rows_of(z), hi] + rm[nz - 2]

    c = remote(f1, rx, px)
    c.wait_recv()
    own_chunk = pl.ds(pl.multiple_of(core * half + z * chunk, 8), chunk)
    o_ref[own_chunk, :] = f1[...] + rx[...]

    to_core = [remote(o_ref.at[own_chunk], o_ref.at[own_chunk], pc)]

    def grows(j, q):
        return pl.ds(pl.multiple_of(core * half + j * chunk + q * sub, 8), sub)

    def arrived(q, jp, jm):
        pending[q][0].wait_recv()
        pending[q][1].wait_recv()
        gp = grows((jp + nz - 1) % nz, q)
        gm = grows((jm + 1) % nz, q)
        to_core.append(remote(o_ref.at[gp, lo], o_ref.at[gp, lo], pc))
        to_core.append(remote(o_ref.at[gm, hi], o_ref.at[gm, hi], pc))

    for s in range(nz - 1):
        jp = (z + nz - s) % nz
        jm = (z + s) % nz
        for q in range(streams):
            if s > 0:
                arrived(q, (jp + 1) % nz, (jm + nz - 1) % nz)
            gp = grows(jp, q)
            gm = grows(jm, q)
            pending[q] = (remote(o_ref.at[gp, lo], o_ref.at[gp, lo], zr),
                          remote(o_ref.at[gm, hi], o_ref.at[gm, hi], zl))
        input_grad_tap()
        if s == nz - 2:
            while done_taps[0] < len(shifts):
                input_grad_tap()
    for q in range(streams):
        arrived(q, (z + 2) % nz, (z + nz - 2) % nz)
    for c in to_core:
        c.wait_recv()

    for c in rs_copies:
        c.wait_recv()
    acc = t_ref[pl.ds(pl.multiple_of(me * owned, 8), owned), :]
    for k in range(1, nc):
        acc = acc + rs_buf[k]
    res_ref[...] = acc.astype(res_ref.dtype)
    ig_ref[...] = ig_acc[...].astype(ig_ref.dtype)

    for c in sent + rs_copies:
        c.wait_send()


def dp_allreduce(a, t, w, g, masks, shifts, axis_names):
    rows, cols = a.shape
    nc = lax.axis_size("chan")
    owned = t.shape[0] // nc
    nz = lax.axis_size("dp") // 4
    half = rows // 2
    chunk = half // nz
    lanes = cols // 2
    n_copies = nz + 3 + 6 * (nz - 1) * STREAMS
    vmem = pltpu.VMEM
    return pl.pallas_call(
        functools.partial(_allreduce_kernel, axis_names, nz, nc, STREAMS, shifts),
        out_shape=(
            jax.ShapeDtypeStruct((rows, cols), a.dtype),
            jax.ShapeDtypeStruct((owned, t.shape[1]), jnp.bfloat16),
            jax.ShapeDtypeStruct((w.shape[1], g.shape[1]), jnp.bfloat16),
        ),
        in_specs=[pl.BlockSpec(memory_space=vmem)] * 5,
        out_specs=(pl.BlockSpec(memory_space=vmem),) * 3,
        scratch_shapes=[
            vmem((half, cols), a.dtype),
            vmem((half, cols), a.dtype),
            vmem((chunk, cols), a.dtype),
            vmem((chunk, cols), a.dtype),
            vmem((nz - 1, chunk, lanes), a.dtype),
            vmem((nz - 1, chunk, lanes), a.dtype),
            vmem((nz - 1, chunk, lanes), a.dtype),
            vmem((nz - 1, chunk, lanes), a.dtype),
            vmem((nc, owned, t.shape[1]), t.dtype),
            vmem((w.shape[1], g.shape[1]), jnp.float32),
            pltpu.SemaphoreType.DMA((n_copies,)),
            pltpu.SemaphoreType.DMA((n_copies,)),
            pltpu.SemaphoreType.DMA((nc,)),
            pltpu.SemaphoreType.DMA((nc,)),
        ],
        compiler_params=pltpu.CompilerParams(
            collective_id=0, has_side_effects=True, vmem_limit_bytes=48 * 1024 * 1024
        ),
    )(a, t, w, g, masks)


def _allgather_kernel(axis_names, n, shifts, x_ref, w_ref, f_ref, m_ref, o_ref, t_ref,
                      send_sems, recv_sems):
    rows = x_ref.shape[0]
    MESH = pl.DeviceIdType.MESH
    me = lax.axis_index("chan")

    def dev(p):
        return tuple(p if a == "chan" else lax.axis_index(a) for a in axis_names)

    barrier = pltpu.get_barrier_semaphore()
    for k in range(1, n):
        pl.semaphore_signal(barrier, inc=1, device_id=dev((me + k) % n), device_id_type=MESH)
    pl.semaphore_wait(barrier, n - 1)

    mine = pl.ds(pl.multiple_of(me * rows, 16), rows)
    copies = []
    for k in range(1, n):
        peer = (me + k) % n
        c = pltpu.make_async_remote_copy(
            src_ref=x_ref, dst_ref=o_ref.at[mine], send_sem=send_sems.at[k],
            recv_sem=recv_sems.at[k], device_id=dev(peer), device_id_type=MESH)
        c.start()
        copies.append(c)
    o_ref[mine, :] = x_ref[...]
    size = f_ref.shape[1]
    for t, shift in enumerate(shifts):
        y = jnp.dot(w_ref[t], f_ref[...], preferred_element_type=jnp.float32)
        if shift % size:
            y = pltpu.roll(y, (-shift) % size, 1)
        y = y * m_ref[pl.ds(t, 1), :]
        if t == 0:
            t_ref[...] = y
        else:
            t_ref[...] += y
    for k in range(1, n):
        src = (me + n - k) % n
        theirs = pl.ds(pl.multiple_of(src * rows, 16), rows)
        pltpu.make_async_remote_copy(
            src_ref=x_ref, dst_ref=o_ref.at[theirs], send_sem=send_sems.at[k],
            recv_sem=recv_sems.at[k], device_id=dev(src), device_id_type=MESH).wait_recv()
    for c in copies:
        c.wait_send()


def chan_allgather(x, axis_names, w, f, masks, shifts):
    rows, cols = x.shape
    n = lax.axis_size("chan")
    vmem = pltpu.VMEM
    return pl.pallas_call(
        functools.partial(_allgather_kernel, axis_names, n, shifts),
        out_shape=(
            jax.ShapeDtypeStruct((rows * n, cols), x.dtype),
            jax.ShapeDtypeStruct((w.shape[1], f.shape[1]), jnp.float32),
        ),
        in_specs=[pl.BlockSpec(memory_space=vmem)] * 4,
        out_specs=(pl.BlockSpec(memory_space=vmem),) * 2,
        scratch_shapes=[pltpu.SemaphoreType.DMA((n,)), pltpu.SemaphoreType.DMA((n,))],
        compiler_params=pltpu.CompilerParams(
            collective_id=1, has_side_effects=True, vmem_limit_bytes=48 * 1024 * 1024
        ),
    )(x, w, f, masks)


def on_device(axis_names, inputs, weight, cotangent):
    input_channels_local = inputs.shape[1]
    cout_local = cotangent.shape[1]
    tap_locations = MAP_HEIGHT * MAP_WIDTH
    feature_map = inputs[0].reshape(input_channels_local, MAP_HEIGHT, MAP_WIDTH)
    tap_list = weight.shape[1]
    output_channels_total = weight.shape[2]
    tap_shifts = [
        (DILATION_RATE * (tap_index // 3 - 1), DILATION_RATE * (tap_index % 3 - 1))
        for tap_index in range(tap_list)
    ]
    displaced_input = [
        translated_input(feature_map, first_operand, second_operand, DILATION_RATE).reshape(
            input_channels_local, tap_locations
        )
        for first_operand, second_operand in tap_shifts
    ]
    rows_idx = np.arange(tap_locations) // MAP_WIDTH
    cols_idx = np.arange(tap_locations) % MAP_WIDTH
    masks = np.stack(
        [
            ((rows_idx + a >= 0) & (rows_idx + a < MAP_HEIGHT) & (cols_idx + b >= 0) & (cols_idx + b < MAP_WIDTH))
            for a, b in tap_shifts
        ]
    ).astype(np.float32)
    flat_grads, total = chan_allgather(
        cotangent[0],
        axis_names,
        jnp.transpose(weight, (1, 2, 0)),
        inputs[0],
        jnp.asarray(masks),
        tuple(a * MAP_WIDTH + b for a, b in tap_shifts),
    )
    contract_cols = (((1,), (1,)), ((), ()))
    local_grad = jnp.stack(
        [
            lax.dot_general(
                displaced_input[tap_index],
                flat_grads,
                contract_cols,
                preferred_element_type=jnp.float32,
            )
            for tap_index in range(tap_list)
        ],
        axis=0,
    )
    back_masks = np.stack(
        [
            ((rows_idx - a >= 0) & (rows_idx - a < MAP_HEIGHT) & (cols_idx - b >= 0) & (cols_idx - b < MAP_WIDTH))
            for a, b in tap_shifts
        ]
    ).astype(np.float32)
    summed, owned, back = dp_allreduce(
        local_grad.reshape(tap_list * input_channels_local, output_channels_total),
        total,
        jnp.transpose(weight, (1, 0, 2)),
        flat_grads,
        jnp.asarray(back_masks),
        tuple(a * MAP_WIDTH + b for a, b in tap_shifts),
        axis_names,
    )
    result = owned.reshape(1, cout_local, tap_locations)
    summed_grad = jnp.transpose(
        summed.reshape(tap_list, input_channels_local, output_channels_total), (1, 0, 2)
    )
    weight_grad = summed_grad / jnp.float32(lax.axis_size("dp"))
    input_grad = back.reshape(1, input_channels_local, tap_locations)
    return (result, input_grad, weight_grad)


def solution(mesh):
    placed = (P("dp", "chan", None), P("chan", None, None), P("dp", "chan", None))
    return jax.shard_map(
        functools.partial(on_device, tuple(mesh.axis_names)),
        mesh=mesh,
        in_specs=placed,
        out_specs=(P("dp", "chan", None), P("dp", "chan", None), P("chan", None, None)),
        check_vma=False,
    )
```

```python
import functools

import jax
import jax.numpy as jnp
import numpy as np
from jax import lax
from jax.experimental import pallas as pl
from jax.experimental.pallas import tpu as pltpu
from jax.sharding import PartitionSpec as P

DILATION_RATE = 12
MAP_HEIGHT = 16
MAP_WIDTH = 72
STREAMS = 3


def translated_input(receptive_field, row_shift, column_shift, reach):
    height, width = (receptive_field.shape[1], receptive_field.shape[2])
    bordered_input = jnp.pad(receptive_field, ((0, 0), (reach, reach), (reach, reach)))
    return bordered_input[
        :,
        reach + row_shift : reach + row_shift + height,
        reach + column_shift : reach + column_shift + width,
    ]


def _allreduce_kernel(axis_names, nz, nc, streams, shifts, a_ref, t_ref, w_ref, g_ref, m_ref,
                      o_ref, res_ref, ig_ref, rc, s1, f1, rx, rp, rm, ap, am, rs_buf, ig_acc,
                      send_sems, recv_sems, rs_send, rs_recv):
    rows, cols = a_ref.shape
    half = rows // 2
    chunk = half // nz
    lanes = cols // 2
    MESH = pl.DeviceIdType.MESH
    dp = lax.axis_index("dp")
    core = dp % 2
    xl = (dp // 2) % 2
    z = dp // 4
    nd = 4 * nz
    pc = dp + 1 - 2 * core
    px = dp + 2 - 4 * xl
    zr = (dp + 4) % nd
    zl = (dp + nd - 4) % nd

    me = lax.axis_index("chan")

    def dev(p):
        return tuple(p if n == "dp" else lax.axis_index(n) for n in axis_names)

    def cdev(p):
        return tuple(p if n == "chan" else lax.axis_index(n) for n in axis_names)

    barrier = pltpu.get_barrier_semaphore()
    for peer in (pc, px, zr, zl):
        pl.semaphore_signal(barrier, inc=1, device_id=dev(peer), device_id_type=MESH)
    for k in range(1, nc):
        pl.semaphore_signal(barrier, inc=1, device_id=cdev((me + k) % nc), device_id_type=MESH)
    pl.semaphore_wait(barrier, 4 + nc - 1)

    owned = res_ref.shape[0]
    rs_copies = []
    for k in range(1, nc):
        peer = (me + k) % nc
        c = pltpu.make_async_remote_copy(
            src_ref=t_ref.at[pl.ds(pl.multiple_of(peer * owned, 8), owned)],
            dst_ref=rs_buf.at[k], send_sem=rs_send.at[k], recv_sem=rs_recv.at[k],
            device_id=cdev(peer), device_id_type=MESH)
        c.start()
        rs_copies.append(c)

    sent = []
    counter = [0]

    def remote(src, dst, peer):
        k = counter[0]
        counter[0] += 1
        c = pltpu.make_async_remote_copy(
            src_ref=src, dst_ref=dst, send_sem=send_sems.at[k], recv_sem=recv_sems.at[k],
            device_id=dev(peer), device_id_type=MESH)
        c.start()
        sent.append(c)
        return c

    def rows_of(j):
        return pl.ds(pl.multiple_of(j * chunk, 8), chunk)

    done_taps = [0]
    size = g_ref.shape[1]

    def input_grad_tap():
        t = done_taps[0]
        if t < len(shifts):
            y = jnp.dot(w_ref[t], g_ref[...], preferred_element_type=jnp.float32)
            if shifts[t] % size:
                y = pltpu.roll(y, shifts[t] % size, 1)
            y = y * m_ref[pl.ds(t, 1), :]
            if t == 0:
                ig_acc[...] = y
            else:
                ig_acc[...] += y
            done_taps[0] += 1

    mine_c = core * half
    other_c = (1 - core) * half
    order = []
    for d in range(1, nz // 2 + 1):
        order.append((z + nz - d) % nz)
        if 2 * d != nz:
            order.append((z + d) % nz)
    order.append(z)
    core_in = []
    for j in order:
        src_rows = pl.ds(pl.multiple_of(other_c + j * chunk, 8), chunk)
        core_in.append((j, remote(a_ref.at[src_rows], rc.at[rows_of(j)], pc)))
    ready = [0]

    def ready_upto(n):
        while ready[0] < n:
            j, c = core_in[ready[0]]
            c.wait_recv()
            own_rows = pl.ds(pl.multiple_of(mine_c + j * chunk, 8), chunk)
            s1[rows_of(j), :] = a_ref[own_rows, :] + rc[rows_of(j), :]
            ready[0] += 1

    def needed(d):
        return min(len(order) - 1, 2 * d - (1 if 2 * d == nz else 0))

    lo = pl.ds(0, lanes)
    hi = pl.ds(lanes, lanes)
    sub = chunk // streams

    def srows(j, q):
        return pl.ds(pl.multiple_of(j * chunk + q * sub, 8), sub)

    blk = [pl.ds(q * sub, sub) for q in range(streams)]
    pending = [None] * streams
    for s in range(nz - 1):
        jp = (z + 2 * nz - 1 - s) % nz
        jm = (z + 1 + s) % nz
        if s + 1 <= nz // 2:
            ready_upto(needed(s + 1))
        for q in range(streams):
            if s == 0:
                src_p = s1.at[srows(jp, q), lo]
                src_m = s1.at[srows(jm, q), hi]
            else:
                pending[q][0].wait_recv()
                pending[q][1].wait_recv()
                ap[s, blk[q], :] = s1[srows(jp, q), lo] + rp[s - 1, blk[q], :]
                am[s, blk[q], :] = s1[srows(jm, q), hi] + rm[s - 1, blk[q], :]
                src_p = ap.at[s, blk[q]]
                src_m = am.at[s, blk[q]]
            pending[q] = (remote(src_p, rp.at[s, blk[q]], zr), remote(src_m, rm.at[s, blk[q]], zl))
    for q in range(streams):
        pending[q][0].wait_recv()
        pending[q][1].wait_recv()
    ready_upto(len(order))
    f1[:, lo] = s1[rows_of(z), lo] + rp[nz - 2]
    f1[:, hi] = s1[rows_of(z), hi] + rm[nz - 2]

    c = remote(f1, rx, px)
    c.wait_recv()
    own_chunk = pl.ds(pl.multiple_of(core * half + z * chunk, 8), chunk)
    o_ref[own_chunk, :] = f1[...] + rx[...]

    to_core = [remote(o_ref.at[own_chunk], o_ref.at[own_chunk], pc)]

    def grows(j, q):
        return pl.ds(pl.multiple_of(core * half + j * chunk + q * sub, 8), sub)

    def arrived(q, jp, jm):
        pending[q][0].wait_recv()
        pending[q][1].wait_recv()
        gp = grows((jp + nz - 1) % nz, q)
        gm = grows((jm + 1) % nz, q)
        to_core.append(remote(o_ref.at[gp, lo], o_ref.at[gp, lo], pc))
        to_core.append(remote(o_ref.at[gm, hi], o_ref.at[gm, hi], pc))

    for s in range(nz - 1):
        jp = (z + nz - s) % nz
        jm = (z + s) % nz
        for q in range(streams):
            if s > 0:
                arrived(q, (jp + 1) % nz, (jm + nz - 1) % nz)
            gp = grows(jp, q)
            gm = grows(jm, q)
            pending[q] = (remote(o_ref.at[gp, lo], o_ref.at[gp, lo], zr),
                          remote(o_ref.at[gm, hi], o_ref.at[gm, hi], zl))
        input_grad_tap()
        if s == nz - 2:
            while done_taps[0] < len(shifts):
                input_grad_tap()
    for q in range(streams):
        arrived(q, (z + 2) % nz, (z + nz - 2) % nz)
    for c in to_core:
        c.wait_recv()

    for c in rs_copies:
        c.wait_recv()
    acc = t_ref[pl.ds(pl.multiple_of(me * owned, 8), owned), :]
    for k in range(1, nc):
        acc = acc + rs_buf[k]
    res_ref[...] = acc.astype(res_ref.dtype)
    ig_ref[...] = ig_acc[...].astype(ig_ref.dtype)

    for c in sent + rs_copies:
        c.wait_send()


def dp_allreduce(a, t, w, g, masks, shifts, axis_names):
    rows, cols = a.shape
    nc = lax.axis_size("chan")
    owned = t.shape[0] // nc
    nz = lax.axis_size("dp") // 4
    half = rows // 2
    chunk = half // nz
    lanes = cols // 2
    n_copies = nz + 3 + 6 * (nz - 1) * STREAMS
    vmem = pltpu.VMEM
    return pl.pallas_call(
        functools.partial(_allreduce_kernel, axis_names, nz, nc, STREAMS, shifts),
        out_shape=(
            jax.ShapeDtypeStruct((rows, cols), a.dtype),
            jax.ShapeDtypeStruct((owned, t.shape[1]), jnp.bfloat16),
            jax.ShapeDtypeStruct((w.shape[1], g.shape[1]), jnp.bfloat16),
        ),
        in_specs=[pl.BlockSpec(memory_space=vmem)] * 5,
        out_specs=(pl.BlockSpec(memory_space=vmem),) * 3,
        scratch_shapes=[
            vmem((half, cols), a.dtype),
            vmem((half, cols), a.dtype),
            vmem((chunk, cols), a.dtype),
            vmem((chunk, cols), a.dtype),
            vmem((nz - 1, chunk, lanes), a.dtype),
            vmem((nz - 1, chunk, lanes), a.dtype),
            vmem((nz - 1, chunk, lanes), a.dtype),
            vmem((nz - 1, chunk, lanes), a.dtype),
            vmem((nc, owned, t.shape[1]), t.dtype),
            vmem((w.shape[1], g.shape[1]), jnp.float32),
            pltpu.SemaphoreType.DMA((n_copies,)),
            pltpu.SemaphoreType.DMA((n_copies,)),
            pltpu.SemaphoreType.DMA((nc,)),
            pltpu.SemaphoreType.DMA((nc,)),
        ],
        compiler_params=pltpu.CompilerParams(
            collective_id=0, has_side_effects=True, vmem_limit_bytes=48 * 1024 * 1024
        ),
    )(a, t, w, g, masks)


def _allgather_kernel(axis_names, n, shifts, x_ref, w_ref, f_ref, m_ref, o_ref, t_ref, wg_ref,
                      xs, send_sems, recv_sems):
    rows = x_ref.shape[0]
    MESH = pl.DeviceIdType.MESH
    me = lax.axis_index("chan")

    def dev(p):
        return tuple(p if a == "chan" else lax.axis_index(a) for a in axis_names)

    barrier = pltpu.get_barrier_semaphore()
    for k in range(1, n):
        pl.semaphore_signal(barrier, inc=1, device_id=dev((me + k) % n), device_id_type=MESH)
    pl.semaphore_wait(barrier, n - 1)

    mine = pl.ds(pl.multiple_of(me * rows, 16), rows)
    copies = []
    for k in range(1, n):
        peer = (me + k) % n
        c = pltpu.make_async_remote_copy(
            src_ref=x_ref, dst_ref=o_ref.at[mine], send_sem=send_sems.at[k],
            recv_sem=recv_sems.at[k], device_id=dev(peer), device_id_type=MESH)
        c.start()
        copies.append(c)
    o_ref[mine, :] = x_ref[...]
    size = f_ref.shape[1]
    for t, shift in enumerate(shifts):
        y = jnp.dot(w_ref[t], f_ref[...], preferred_element_type=jnp.float32)
        if shift % size:
            y = pltpu.roll(y, (-shift) % size, 1)
        y = y * m_ref[pl.ds(t, 1), :]
        if t == 0:
            t_ref[...] = y
        else:
            t_ref[...] += y
    wide = f_ref[...].astype(jnp.float32)
    for t, shift in enumerate(shifts):
        v = pltpu.roll(wide, (-shift) % size, 1) if shift % size else wide
        xs[t] = (v * m_ref[pl.ds(t, 1), :]).astype(xs.dtype)
    for k in range(1, n):
        src = (me + n - k) % n
        theirs = pl.ds(pl.multiple_of(src * rows, 16), rows)
        pltpu.make_async_remote_copy(
            src_ref=x_ref, dst_ref=o_ref.at[theirs], send_sem=send_sems.at[k],
            recv_sem=recv_sems.at[k], device_id=dev(src), device_id_type=MESH).wait_recv()
    cin = f_ref.shape[0]
    for t in range(len(shifts)):
        wg_ref[pl.ds(t * cin, cin), :] = lax.dot_general(
            xs[t], o_ref[...], (((1,), (1,)), ((), ())), preferred_element_type=jnp.float32)
    for c in copies:
        c.wait_send()


def chan_allgather(x, axis_names, w, f, masks, shifts):
    rows, cols = x.shape
    n = lax.axis_size("chan")
    vmem = pltpu.VMEM
    return pl.pallas_call(
        functools.partial(_allgather_kernel, axis_names, n, shifts),
        out_shape=(
            jax.ShapeDtypeStruct((rows * n, cols), x.dtype),
            jax.ShapeDtypeStruct((w.shape[1], f.shape[1]), jnp.float32),
            jax.ShapeDtypeStruct((len(shifts) * f.shape[0], rows * n), jnp.float32),
        ),
        in_specs=[pl.BlockSpec(memory_space=vmem)] * 4,
        out_specs=(pl.BlockSpec(memory_space=vmem),) * 3,
        scratch_shapes=[
            vmem((len(shifts),) + f.shape, f.dtype),
            pltpu.SemaphoreType.DMA((n,)),
            pltpu.SemaphoreType.DMA((n,)),
        ],
        compiler_params=pltpu.CompilerParams(
            collective_id=1, has_side_effects=True, vmem_limit_bytes=48 * 1024 * 1024
        ),
    )(x, w, f, masks)


def on_device(axis_names, inputs, weight, cotangent):
    input_channels_local = inputs.shape[1]
    cout_local = cotangent.shape[1]
    tap_locations = MAP_HEIGHT * MAP_WIDTH
    feature_map = inputs[0].reshape(input_channels_local, MAP_HEIGHT, MAP_WIDTH)
    tap_list = weight.shape[1]
    output_channels_total = weight.shape[2]
    tap_shifts = [
        (DILATION_RATE * (tap_index // 3 - 1), DILATION_RATE * (tap_index % 3 - 1))
        for tap_index in range(tap_list)
    ]
    rows_idx = np.arange(tap_locations) // MAP_WIDTH
    cols_idx = np.arange(tap_locations) % MAP_WIDTH
    masks = np.stack(
        [
            ((rows_idx + a >= 0) & (rows_idx + a < MAP_HEIGHT) & (cols_idx + b >= 0) & (cols_idx + b < MAP_WIDTH))
            for a, b in tap_shifts
        ]
    ).astype(np.float32)
    flat_grads, total, local_grad = chan_allgather(
        cotangent[0],
        axis_names,
        jnp.transpose(weight, (1, 2, 0)),
        inputs[0],
        jnp.asarray(masks),
        tuple(a * MAP_WIDTH + b for a, b in tap_shifts),
    )
    back_masks = np.stack(
        [
            ((rows_idx - a >= 0) & (rows_idx - a < MAP_HEIGHT) & (cols_idx - b >= 0) & (cols_idx - b < MAP_WIDTH))
            for a, b in tap_shifts
        ]
    ).astype(np.float32)
    summed, owned, back = dp_allreduce(
        local_grad,
        total,
        jnp.transpose(weight, (1, 0, 2)),
        flat_grads,
        jnp.asarray(back_masks),
        tuple(a * MAP_WIDTH + b for a, b in tap_shifts),
        axis_names,
    )
    result = owned.reshape(1, cout_local, tap_locations)
    summed_grad = jnp.transpose(
        summed.reshape(tap_list, input_channels_local, output_channels_total), (1, 0, 2)
    )
    weight_grad = summed_grad / jnp.float32(lax.axis_size("dp"))
    input_grad = back.reshape(1, input_channels_local, tap_locations)
    return (result, input_grad, weight_grad)


def solution(mesh):
    placed = (P("dp", "chan", None), P("chan", None, None), P("dp", "chan", None))
    return jax.shard_map(
        functools.partial(on_device, tuple(mesh.axis_names)),
        mesh=mesh,
        in_specs=placed,
        out_specs=(P("dp", "chan", None), P("dp", "chan", None), P("chan", None, None)),
        check_vma=False,
    )
```

```python
import functools

import jax
import jax.numpy as jnp
import numpy as np
from jax import lax
from jax.experimental import pallas as pl
from jax.experimental.pallas import tpu as pltpu
from jax.sharding import PartitionSpec as P

DILATION_RATE = 12
MAP_HEIGHT = 16
MAP_WIDTH = 72
STREAMS = 3


def translated_input(receptive_field, row_shift, column_shift, reach):
    height, width = (receptive_field.shape[1], receptive_field.shape[2])
    bordered_input = jnp.pad(receptive_field, ((0, 0), (reach, reach), (reach, reach)))
    return bordered_input[
        :,
        reach + row_shift : reach + row_shift + height,
        reach + column_shift : reach + column_shift + width,
    ]


def _allreduce_kernel(axis_names, nz, nc, streams, shifts, a_ref, t_ref, w_ref, g_ref, m_ref,
                      o_ref, res_ref, ig_ref, rc, s1, f1, rx, rp, rm, ap, am, rs_buf, ig_acc,
                      send_sems, recv_sems, rs_send, rs_recv, entry_barrier=True):
    rows, cols = a_ref.shape
    half = rows // 2
    chunk = half // nz
    lanes = cols // 2
    MESH = pl.DeviceIdType.MESH
    dp = lax.axis_index("dp")
    core = dp % 2
    xl = (dp // 2) % 2
    z = dp // 4
    nd = 4 * nz
    pc = dp + 1 - 2 * core
    px = dp + 2 - 4 * xl
    zr = (dp + 4) % nd
    zl = (dp + nd - 4) % nd

    me = lax.axis_index("chan")

    def dev(p):
        return tuple(p if n == "dp" else lax.axis_index(n) for n in axis_names)

    def cdev(p):
        return tuple(p if n == "chan" else lax.axis_index(n) for n in axis_names)

    if entry_barrier:
        barrier = pltpu.get_barrier_semaphore()
        for peer in (pc, px, zr, zl):
            pl.semaphore_signal(barrier, inc=1, device_id=dev(peer), device_id_type=MESH)
        for k in range(1, nc):
            pl.semaphore_signal(barrier, inc=1, device_id=cdev((me + k) % nc), device_id_type=MESH)
        pl.semaphore_wait(barrier, 4 + nc - 1)

    owned = res_ref.shape[0]
    rs_copies = []
    for k in range(1, nc):
        peer = (me + k) % nc
        c = pltpu.make_async_remote_copy(
            src_ref=t_ref.at[pl.ds(pl.multiple_of(peer * owned, 8), owned)],
            dst_ref=rs_buf.at[k], send_sem=rs_send.at[k], recv_sem=rs_recv.at[k],
            device_id=cdev(peer), device_id_type=MESH)
        c.start()
        rs_copies.append(c)

    sent = []
    counter = [0]

    def remote(src, dst, peer):
        k = counter[0]
        counter[0] += 1
        c = pltpu.make_async_remote_copy(
            src_ref=src, dst_ref=dst, send_sem=send_sems.at[k], recv_sem=recv_sems.at[k],
            device_id=dev(peer), device_id_type=MESH)
        c.start()
        sent.append(c)
        return c

    def rows_of(j):
        return pl.ds(pl.multiple_of(j * chunk, 8), chunk)

    done_taps = [0]
    size = g_ref.shape[1]

    def input_grad_tap():
        t = done_taps[0]
        if t < len(shifts):
            y = jnp.dot(w_ref[t], g_ref[...], preferred_element_type=jnp.float32)
            if shifts[t] % size:
                y = pltpu.roll(y, shifts[t] % size, 1)
            y = y * m_ref[pl.ds(t, 1), :]
            if t == 0:
                ig_acc[...] = y
            else:
                ig_acc[...] += y
            done_taps[0] += 1

    mine_c = core * half
    other_c = (1 - core) * half
    order = []
    for d in range(1, nz // 2 + 1):
        order.append((z + nz - d) % nz)
        if 2 * d != nz:
            order.append((z + d) % nz)
    order.append(z)
    core_in = []
    for j in order:
        src_rows = pl.ds(pl.multiple_of(other_c + j * chunk, 8), chunk)
        core_in.append((j, remote(a_ref.at[src_rows], rc.at[rows_of(j)], pc)))
    ready = [0]

    def ready_upto(n):
        while ready[0] < n:
            j, c = core_in[ready[0]]
            c.wait_recv()
            own_rows = pl.ds(pl.multiple_of(mine_c + j * chunk, 8), chunk)
            s1[rows_of(j), :] = a_ref[own_rows, :] + rc[rows_of(j), :]
            ready[0] += 1

    def needed(d):
        return min(len(order) - 1, 2 * d - (1 if 2 * d == nz else 0))

    lo = pl.ds(0, lanes)
    hi = pl.ds(lanes, lanes)
    sub = chunk // streams

    def srows(j, q):
        return pl.ds(pl.multiple_of(j * chunk + q * sub, 8), sub)

    blk = [pl.ds(q * sub, sub) for q in range(streams)]
    pending = [None] * streams
    for s in range(nz - 1):
        jp = (z + 2 * nz - 1 - s) % nz
        jm = (z + 1 + s) % nz
        if s + 1 <= nz // 2:
            ready_upto(needed(s + 1))
        for q in range(streams):
            if s == 0:
                src_p = s1.at[srows(jp, q), lo]
                src_m = s1.at[srows(jm, q), hi]
            else:
                pending[q][0].wait_recv()
                pending[q][1].wait_recv()
                ap[s, blk[q], :] = s1[srows(jp, q), lo] + rp[s - 1, blk[q], :]
                am[s, blk[q], :] = s1[srows(jm, q), hi] + rm[s - 1, blk[q], :]
                src_p = ap.at[s, blk[q]]
                src_m = am.at[s, blk[q]]
            pending[q] = (remote(src_p, rp.at[s, blk[q]], zr), remote(src_m, rm.at[s, blk[q]], zl))
    for q in range(streams):
        pending[q][0].wait_recv()
        pending[q][1].wait_recv()
    ready_upto(len(order))
    f1[:, lo] = s1[rows_of(z), lo] + rp[nz - 2]
    f1[:, hi] = s1[rows_of(z), hi] + rm[nz - 2]

    c = remote(f1, rx, px)
    c.wait_recv()
    own_chunk = pl.ds(pl.multiple_of(core * half + z * chunk, 8), chunk)
    o_ref[own_chunk, :] = f1[...] + rx[...]

    to_core = [remote(o_ref.at[own_chunk], o_ref.at[own_chunk], pc)]

    def grows(j, q):
        return pl.ds(pl.multiple_of(core * half + j * chunk + q * sub, 8), sub)

    def arrived(q, jp, jm):
        pending[q][0].wait_recv()
        pending[q][1].wait_recv()
        gp = grows((jp + nz - 1) % nz, q)
        gm = grows((jm + 1) % nz, q)
        to_core.append(remote(o_ref.at[gp, lo], o_ref.at[gp, lo], pc))
        to_core.append(remote(o_ref.at[gm, hi], o_ref.at[gm, hi], pc))

    for s in range(nz - 1):
        jp = (z + nz - s) % nz
        jm = (z + s) % nz
        for q in range(streams):
            if s > 0:
                arrived(q, (jp + 1) % nz, (jm + nz - 1) % nz)
            gp = grows(jp, q)
            gm = grows(jm, q)
            pending[q] = (remote(o_ref.at[gp, lo], o_ref.at[gp, lo], zr),
                          remote(o_ref.at[gm, hi], o_ref.at[gm, hi], zl))
        input_grad_tap()
        if s == nz - 2:
            while done_taps[0] < len(shifts):
                input_grad_tap()
    for q in range(streams):
        arrived(q, (z + 2) % nz, (z + nz - 2) % nz)
    for c in to_core:
        c.wait_recv()

    for c in rs_copies:
        c.wait_recv()
    acc = t_ref[pl.ds(pl.multiple_of(me * owned, 8), owned), :]
    for k in range(1, nc):
        acc = acc + rs_buf[k]
    res_ref[...] = acc.astype(res_ref.dtype)
    ig_ref[...] = ig_acc[...].astype(ig_ref.dtype)

    for c in sent + rs_copies:
        c.wait_send()


def dp_allreduce(a, t, w, g, masks, shifts, axis_names):
    rows, cols = a.shape
    nc = lax.axis_size("chan")
    owned = t.shape[0] // nc
    nz = lax.axis_size("dp") // 4
    half = rows // 2
    chunk = half // nz
    lanes = cols // 2
    n_copies = nz + 3 + 6 * (nz - 1) * STREAMS
    vmem = pltpu.VMEM
    return pl.pallas_call(
        functools.partial(_allreduce_kernel, axis_names, nz, nc, STREAMS, shifts),
        out_shape=(
            jax.ShapeDtypeStruct((rows, cols), a.dtype),
            jax.ShapeDtypeStruct((owned, t.shape[1]), jnp.bfloat16),
            jax.ShapeDtypeStruct((w.shape[1], g.shape[1]), jnp.bfloat16),
        ),
        in_specs=[pl.BlockSpec(memory_space=vmem)] * 5,
        out_specs=(pl.BlockSpec(memory_space=vmem),) * 3,
        scratch_shapes=[
            vmem((half, cols), a.dtype),
            vmem((half, cols), a.dtype),
            vmem((chunk, cols), a.dtype),
            vmem((chunk, cols), a.dtype),
            vmem((nz - 1, chunk, lanes), a.dtype),
            vmem((nz - 1, chunk, lanes), a.dtype),
            vmem((nz - 1, chunk, lanes), a.dtype),
            vmem((nz - 1, chunk, lanes), a.dtype),
            vmem((nc, owned, t.shape[1]), t.dtype),
            vmem((w.shape[1], g.shape[1]), jnp.float32),
            pltpu.SemaphoreType.DMA((n_copies,)),
            pltpu.SemaphoreType.DMA((n_copies,)),
            pltpu.SemaphoreType.DMA((nc,)),
            pltpu.SemaphoreType.DMA((nc,)),
        ],
        compiler_params=pltpu.CompilerParams(
            collective_id=0, has_side_effects=True, vmem_limit_bytes=48 * 1024 * 1024
        ),
    )(a, t, w, g, masks)


def _allgather_kernel(axis_names, n, shifts, x_ref, w_ref, f_ref, m_ref, o_ref, t_ref, wg_ref,
                      xs, send_sems, recv_sems, entry_barrier=True):
    rows = x_ref.shape[0]
    MESH = pl.DeviceIdType.MESH
    me = lax.axis_index("chan")

    def dev(p):
        return tuple(p if a == "chan" else lax.axis_index(a) for a in axis_names)

    if entry_barrier:
        barrier = pltpu.get_barrier_semaphore()
        for k in range(1, n):
            pl.semaphore_signal(barrier, inc=1, device_id=dev((me + k) % n), device_id_type=MESH)
        pl.semaphore_wait(barrier, n - 1)

    mine = pl.ds(pl.multiple_of(me * rows, 16), rows)
    copies = []
    for k in range(1, n):
        peer = (me + k) % n
        c = pltpu.make_async_remote_copy(
            src_ref=x_ref, dst_ref=o_ref.at[mine], send_sem=send_sems.at[k],
            recv_sem=recv_sems.at[k], device_id=dev(peer), device_id_type=MESH)
        c.start()
        copies.append(c)
    o_ref[mine, :] = x_ref[...]
    size = f_ref.shape[1]
    for t, shift in enumerate(shifts):
        y = jnp.dot(w_ref[t], f_ref[...], preferred_element_type=jnp.float32)
        if shift % size:
            y = pltpu.roll(y, (-shift) % size, 1)
        y = y * m_ref[pl.ds(t, 1), :]
        if t == 0:
            t_ref[...] = y
        else:
            t_ref[...] += y
    wide = f_ref[...].astype(jnp.float32)
    for t, shift in enumerate(shifts):
        v = pltpu.roll(wide, (-shift) % size, 1) if shift % size else wide
        xs[t] = (v * m_ref[pl.ds(t, 1), :]).astype(xs.dtype)
    for k in range(1, n):
        src = (me + n - k) % n
        theirs = pl.ds(pl.multiple_of(src * rows, 16), rows)
        pltpu.make_async_remote_copy(
            src_ref=x_ref, dst_ref=o_ref.at[theirs], send_sem=send_sems.at[k],
            recv_sem=recv_sems.at[k], device_id=dev(src), device_id_type=MESH).wait_recv()
    cin = f_ref.shape[0]
    for t in range(len(shifts)):
        wg_ref[pl.ds(t * cin, cin), :] = lax.dot_general(
            xs[t], o_ref[...], (((1,), (1,)), ((), ())), preferred_element_type=jnp.float32)
    for c in copies:
        c.wait_send()


def chan_allgather(x, axis_names, w, f, masks, shifts):
    rows, cols = x.shape
    n = lax.axis_size("chan")
    vmem = pltpu.VMEM
    return pl.pallas_call(
        functools.partial(_allgather_kernel, axis_names, n, shifts),
        out_shape=(
            jax.ShapeDtypeStruct((rows * n, cols), x.dtype),
            jax.ShapeDtypeStruct((w.shape[1], f.shape[1]), jnp.float32),
            jax.ShapeDtypeStruct((len(shifts) * f.shape[0], rows * n), jnp.float32),
        ),
        in_specs=[pl.BlockSpec(memory_space=vmem)] * 4,
        out_specs=(pl.BlockSpec(memory_space=vmem),) * 3,
        scratch_shapes=[
            vmem((len(shifts),) + f.shape, f.dtype),
            pltpu.SemaphoreType.DMA((n,)),
            pltpu.SemaphoreType.DMA((n,)),
        ],
        compiler_params=pltpu.CompilerParams(
            collective_id=1, has_side_effects=True, vmem_limit_bytes=48 * 1024 * 1024
        ),
    )(x, w, f, masks)


def _fused_kernel(axis_names, nz, nc, streams, shifts, x_ref, wf_ref, f_ref, mf_ref, wb_ref, mb_ref,
                  o_ref, res_ref, ig_ref, g_s, t_s, wg_s, xs, ag_send, ag_recv, *ar_scratch):
    MESH = pl.DeviceIdType.MESH
    dp = lax.axis_index("dp")
    me = lax.axis_index("chan")
    nd = 4 * nz
    core = dp % 2
    xl = (dp // 2) % 2
    peers = (dp + 1 - 2 * core, dp + 2 - 4 * xl, (dp + 4) % nd, (dp + nd - 4) % nd)
    barrier = pltpu.get_barrier_semaphore()
    for peer in peers:
        pl.semaphore_signal(barrier, inc=1, device_id=tuple(peer if a == "dp" else lax.axis_index(a) for a in axis_names), device_id_type=MESH)
    for k in range(1, nc):
        pl.semaphore_signal(barrier, inc=1, device_id=tuple((me + k) % nc if a == "chan" else lax.axis_index(a) for a in axis_names), device_id_type=MESH)
    pl.semaphore_wait(barrier, 4 + nc - 1)
    _allgather_kernel(axis_names, nc, shifts, x_ref, wf_ref, f_ref, mf_ref, g_s, t_s, wg_s, xs,
                      ag_send, ag_recv, entry_barrier=False)
    _allreduce_kernel(axis_names, nz, nc, streams, shifts, wg_s, t_s, wb_ref, g_s, mb_ref,
                      o_ref, res_ref, ig_ref, *ar_scratch, entry_barrier=False)


def fused_step(x, wf, f, mf, wb, mb, shifts, axis_names):
    nc = lax.axis_size("chan")
    nz = lax.axis_size("dp") // 4
    rows_x, cols = x.shape
    cin, taps = f.shape[0], len(shifts)
    cout = rows_x * nc
    rows, width = taps * cin, cout
    owned = cout // nc
    half = rows // 2
    chunk = half // nz
    lanes = width // 2
    n_copies = nz + 3 + 6 * (nz - 1) * STREAMS
    vmem = pltpu.VMEM
    f32 = jnp.float32
    return pl.pallas_call(
        functools.partial(_fused_kernel, axis_names, nz, nc, STREAMS, shifts),
        out_shape=(
            jax.ShapeDtypeStruct((rows, width), f32),
            jax.ShapeDtypeStruct((owned, cols), jnp.bfloat16),
            jax.ShapeDtypeStruct((cin, cols), jnp.bfloat16),
        ),
        in_specs=[pl.BlockSpec(memory_space=vmem)] * 6,
        out_specs=(pl.BlockSpec(memory_space=vmem),) * 3,
        scratch_shapes=[
            vmem((cout, cols), x.dtype),
            vmem((cout, cols), f32),
            vmem((rows, width), f32),
            vmem((taps,) + f.shape, f.dtype),
            pltpu.SemaphoreType.DMA((nc,)),
            pltpu.SemaphoreType.DMA((nc,)),
            vmem((half, width), f32),
            vmem((half, width), f32),
            vmem((chunk, width), f32),
            vmem((chunk, width), f32),
            vmem((nz - 1, chunk, lanes), f32),
            vmem((nz - 1, chunk, lanes), f32),
            vmem((nz - 1, chunk, lanes), f32),
            vmem((nz - 1, chunk, lanes), f32),
            vmem((nc, owned, cols), f32),
            vmem((cin, cols), f32),
            pltpu.SemaphoreType.DMA((n_copies,)),
            pltpu.SemaphoreType.DMA((n_copies,)),
            pltpu.SemaphoreType.DMA((nc,)),
            pltpu.SemaphoreType.DMA((nc,)),
        ],
        compiler_params=pltpu.CompilerParams(
            collective_id=0, has_side_effects=True, vmem_limit_bytes=56 * 1024 * 1024
        ),
    )(x, wf, f, mf, wb, mb)


def on_device(axis_names, inputs, weight, cotangent):
    input_channels_local = inputs.shape[1]
    cout_local = cotangent.shape[1]
    tap_locations = MAP_HEIGHT * MAP_WIDTH
    feature_map = inputs[0].reshape(input_channels_local, MAP_HEIGHT, MAP_WIDTH)
    tap_list = weight.shape[1]
    output_channels_total = weight.shape[2]
    tap_shifts = [
        (DILATION_RATE * (tap_index // 3 - 1), DILATION_RATE * (tap_index % 3 - 1))
        for tap_index in range(tap_list)
    ]
    rows_idx = np.arange(tap_locations) // MAP_WIDTH
    cols_idx = np.arange(tap_locations) % MAP_WIDTH
    masks = np.stack(
        [
            ((rows_idx + a >= 0) & (rows_idx + a < MAP_HEIGHT) & (cols_idx + b >= 0) & (cols_idx + b < MAP_WIDTH))
            for a, b in tap_shifts
        ]
    ).astype(np.float32)
    back_masks = np.stack(
        [
            ((rows_idx - a >= 0) & (rows_idx - a < MAP_HEIGHT) & (cols_idx - b >= 0) & (cols_idx - b < MAP_WIDTH))
            for a, b in tap_shifts
        ]
    ).astype(np.float32)
    summed, owned, back = fused_step(
        cotangent[0],
        jnp.transpose(weight, (1, 2, 0)),
        inputs[0],
        jnp.asarray(masks),
        jnp.transpose(weight, (1, 0, 2)),
        jnp.asarray(back_masks),
        tuple(a * MAP_WIDTH + b for a, b in tap_shifts),
        axis_names,
    )
    result = owned.reshape(1, cout_local, tap_locations)
    summed_grad = jnp.transpose(
        summed.reshape(tap_list, input_channels_local, output_channels_total), (1, 0, 2)
    )
    weight_grad = summed_grad / jnp.float32(lax.axis_size("dp"))
    input_grad = back.reshape(1, input_channels_local, tap_locations)
    return (result, input_grad, weight_grad)


def solution(mesh):
    placed = (P("dp", "chan", None), P("chan", None, None), P("dp", "chan", None))
    return jax.shard_map(
        functools.partial(on_device, tuple(mesh.axis_names)),
        mesh=mesh,
        in_specs=placed,
        out_specs=(P("dp", "chan", None), P("dp", "chan", None), P("chan", None, None)),
        check_vma=False,
    )
```

```python
import functools

import jax
import jax.numpy as jnp
import numpy as np
from jax import lax
from jax.experimental import pallas as pl
from jax.experimental.pallas import tpu as pltpu
from jax.sharding import PartitionSpec as P

DILATION_RATE = 12
MAP_HEIGHT = 16
MAP_WIDTH = 72
STREAMS = 3


def translated_input(receptive_field, row_shift, column_shift, reach):
    height, width = (receptive_field.shape[1], receptive_field.shape[2])
    bordered_input = jnp.pad(receptive_field, ((0, 0), (reach, reach), (reach, reach)))
    return bordered_input[
        :,
        reach + row_shift : reach + row_shift + height,
        reach + column_shift : reach + column_shift + width,
    ]


def start_chan_scatter(axis_names, nc, t_ref, rs_buf, rs_send, rs_recv, owned):
    me = lax.axis_index("chan")
    copies = []
    for k in range(1, nc):
        peer = (me + k) % nc
        c = pltpu.make_async_remote_copy(
            src_ref=t_ref.at[pl.ds(pl.multiple_of(peer * owned, 8), owned)],
            dst_ref=rs_buf.at[k], send_sem=rs_send.at[k], recv_sem=rs_recv.at[k],
            device_id=tuple(peer if a == "chan" else lax.axis_index(a) for a in axis_names),
            device_id_type=pl.DeviceIdType.MESH)
        c.start()
        copies.append(c)
    return copies


def _allreduce_kernel(axis_names, nz, nc, streams, shifts, a_ref, t_ref, w_ref, g_ref, m_ref,
                      o_ref, res_ref, ig_ref, rc, s1, f1, rx, rp, rm, ap, am, rs_buf, ig_acc,
                      send_sems, recv_sems, rs_send, rs_recv, entry_barrier=True, rs_started=None):
    rows, cols = a_ref.shape
    half = rows // 2
    chunk = half // nz
    lanes = cols // 2
    MESH = pl.DeviceIdType.MESH
    dp = lax.axis_index("dp")
    core = dp % 2
    xl = (dp // 2) % 2
    z = dp // 4
    nd = 4 * nz
    pc = dp + 1 - 2 * core
    px = dp + 2 - 4 * xl
    zr = (dp + 4) % nd
    zl = (dp + nd - 4) % nd

    me = lax.axis_index("chan")

    def dev(p):
        return tuple(p if n == "dp" else lax.axis_index(n) for n in axis_names)

    def cdev(p):
        return tuple(p if n == "chan" else lax.axis_index(n) for n in axis_names)

    if entry_barrier:
        barrier = pltpu.get_barrier_semaphore()
        for peer in (pc, px, zr, zl):
            pl.semaphore_signal(barrier, inc=1, device_id=dev(peer), device_id_type=MESH)
        for k in range(1, nc):
            pl.semaphore_signal(barrier, inc=1, device_id=cdev((me + k) % nc), device_id_type=MESH)
        pl.semaphore_wait(barrier, 4 + nc - 1)

    owned = res_ref.shape[0]
    if rs_started is None:
        rs_copies = start_chan_scatter(axis_names, nc, t_ref, rs_buf, rs_send, rs_recv, owned)
    else:
        rs_copies = rs_started

    sent = []
    counter = [0]

    def remote(src, dst, peer):
        k = counter[0]
        counter[0] += 1
        c = pltpu.make_async_remote_copy(
            src_ref=src, dst_ref=dst, send_sem=send_sems.at[k], recv_sem=recv_sems.at[k],
            device_id=dev(peer), device_id_type=MESH)
        c.start()
        sent.append(c)
        return c

    def rows_of(j):
        return pl.ds(pl.multiple_of(j * chunk, 8), chunk)

    done_taps = [0]
    size = g_ref.shape[1]

    def input_grad_tap():
        t = done_taps[0]
        if t < len(shifts):
            y = jnp.dot(w_ref[t], g_ref[...], preferred_element_type=jnp.float32)
            if shifts[t] % size:
                y = pltpu.roll(y, shifts[t] % size, 1)
            y = y * m_ref[pl.ds(t, 1), :]
            if t == 0:
                ig_acc[...] = y
            else:
                ig_acc[...] += y
            done_taps[0] += 1

    mine_c = core * half
    other_c = (1 - core) * half
    order = []
    for d in range(1, nz // 2 + 1):
        order.append((z + nz - d) % nz)
        if 2 * d != nz:
            order.append((z + d) % nz)
    order.append(z)
    core_in = []
    for j in order:
        src_rows = pl.ds(pl.multiple_of(other_c + j * chunk, 8), chunk)
        core_in.append((j, remote(a_ref.at[src_rows], rc.at[rows_of(j)], pc)))
    ready = [0]

    def ready_upto(n):
        while ready[0] < n:
            j, c = core_in[ready[0]]
            c.wait_recv()
            own_rows = pl.ds(pl.multiple_of(mine_c + j * chunk, 8), chunk)
            s1[rows_of(j), :] = a_ref[own_rows, :] + rc[rows_of(j), :]
            ready[0] += 1

    def needed(d):
        return min(len(order) - 1, 2 * d - (1 if 2 * d == nz else 0))

    lo = pl.ds(0, lanes)
    hi = pl.ds(lanes, lanes)
    sub = chunk // streams

    def srows(j, q):
        return pl.ds(pl.multiple_of(j * chunk + q * sub, 8), sub)

    blk = [pl.ds(q * sub, sub) for q in range(streams)]
    pending = [None] * streams
    for s in range(nz - 1):
        jp = (z + 2 * nz - 1 - s) % nz
        jm = (z + 1 + s) % nz
        if s + 1 <= nz // 2:
            ready_upto(needed(s + 1))
        for q in range(streams):
            if s == 0:
                src_p = s1.at[srows(jp, q), lo]
                src_m = s1.at[srows(jm, q), hi]
            else:
                pending[q][0].wait_recv()
                pending[q][1].wait_recv()
                ap[s, blk[q], :] = s1[srows(jp, q), lo] + rp[s - 1, blk[q], :]
                am[s, blk[q], :] = s1[srows(jm, q), hi] + rm[s - 1, blk[q], :]
                src_p = ap.at[s, blk[q]]
                src_m = am.at[s, blk[q]]
            pending[q] = (remote(src_p, rp.at[s, blk[q]], zr), remote(src_m, rm.at[s, blk[q]], zl))
    for q in range(streams):
        pending[q][0].wait_recv()
        pending[q][1].wait_recv()
    ready_upto(len(order))
    f1[:, lo] = s1[rows_of(z), lo] + rp[nz - 2]
    f1[:, hi] = s1[rows_of(z), hi] + rm[nz - 2]

    c = remote(f1, rx, px)
    c.wait_recv()
    own_chunk = pl.ds(pl.multiple_of(core * half + z * chunk, 8), chunk)
    o_ref[own_chunk, :] = f1[...] + rx[...]

    to_core = [remote(o_ref.at[own_chunk], o_ref.at[own_chunk], pc)]

    def grows(j, q):
        return pl.ds(pl.multiple_of(core * half + j * chunk + q * sub, 8), sub)

    def arrived(q, jp, jm):
        pending[q][0].wait_recv()
        pending[q][1].wait_recv()
        gp = grows((jp + nz - 1) % nz, q)
        gm = grows((jm + 1) % nz, q)
        to_core.append(remote(o_ref.at[gp, lo], o_ref.at[gp, lo], pc))
        to_core.append(remote(o_ref.at[gm, hi], o_ref.at[gm, hi], pc))

    for s in range(nz - 1):
        jp = (z + nz - s) % nz
        jm = (z + s) % nz
        for q in range(streams):
            if s > 0:
                arrived(q, (jp + 1) % nz, (jm + nz - 1) % nz)
            gp = grows(jp, q)
            gm = grows(jm, q)
            pending[q] = (remote(o_ref.at[gp, lo], o_ref.at[gp, lo], zr),
                          remote(o_ref.at[gm, hi], o_ref.at[gm, hi], zl))
        input_grad_tap()
        if s == nz - 2:
            while done_taps[0] < len(shifts):
                input_grad_tap()
    for q in range(streams):
        arrived(q, (z + 2) % nz, (z + nz - 2) % nz)
    for c in to_core:
        c.wait_recv()

    for c in rs_copies:
        c.wait_recv()
    acc = t_ref[pl.ds(pl.multiple_of(me * owned, 8), owned), :]
    for k in range(1, nc):
        acc = acc + rs_buf[k]
    res_ref[...] = acc.astype(res_ref.dtype)
    ig_ref[...] = ig_acc[...].astype(ig_ref.dtype)

    for c in sent + rs_copies:
        c.wait_send()


def dp_allreduce(a, t, w, g, masks, shifts, axis_names):
    rows, cols = a.shape
    nc = lax.axis_size("chan")
    owned = t.shape[0] // nc
    nz = lax.axis_size("dp") // 4
    half = rows // 2
    chunk = half // nz
    lanes = cols // 2
    n_copies = nz + 3 + 6 * (nz - 1) * STREAMS
    vmem = pltpu.VMEM
    return pl.pallas_call(
        functools.partial(_allreduce_kernel, axis_names, nz, nc, STREAMS, shifts),
        out_shape=(
            jax.ShapeDtypeStruct((rows, cols), a.dtype),
            jax.ShapeDtypeStruct((owned, t.shape[1]), jnp.bfloat16),
            jax.ShapeDtypeStruct((w.shape[1], g.shape[1]), jnp.bfloat16),
        ),
        in_specs=[pl.BlockSpec(memory_space=vmem)] * 5,
        out_specs=(pl.BlockSpec(memory_space=vmem),) * 3,
        scratch_shapes=[
            vmem((half, cols), a.dtype),
            vmem((half, cols), a.dtype),
            vmem((chunk, cols), a.dtype),
            vmem((chunk, cols), a.dtype),
            vmem((nz - 1, chunk, lanes), a.dtype),
            vmem((nz - 1, chunk, lanes), a.dtype),
            vmem((nz - 1, chunk, lanes), a.dtype),
            vmem((nz - 1, chunk, lanes), a.dtype),
            vmem((nc, owned, t.shape[1]), t.dtype),
            vmem((w.shape[1], g.shape[1]), jnp.float32),
            pltpu.SemaphoreType.DMA((n_copies,)),
            pltpu.SemaphoreType.DMA((n_copies,)),
            pltpu.SemaphoreType.DMA((nc,)),
            pltpu.SemaphoreType.DMA((nc,)),
        ],
        compiler_params=pltpu.CompilerParams(
            collective_id=0, has_side_effects=True, vmem_limit_bytes=48 * 1024 * 1024
        ),
    )(a, t, w, g, masks)


def _allgather_kernel(axis_names, n, shifts, x_ref, w_ref, f_ref, m_ref, o_ref, t_ref, wg_ref,
                      xs, send_sems, recv_sems, entry_barrier=True, before_wgrad=None):
    rows = x_ref.shape[0]
    MESH = pl.DeviceIdType.MESH
    me = lax.axis_index("chan")

    def dev(p):
        return tuple(p if a == "chan" else lax.axis_index(a) for a in axis_names)

    if entry_barrier:
        barrier = pltpu.get_barrier_semaphore()
        for k in range(1, n):
            pl.semaphore_signal(barrier, inc=1, device_id=dev((me + k) % n), device_id_type=MESH)
        pl.semaphore_wait(barrier, n - 1)

    mine = pl.ds(pl.multiple_of(me * rows, 16), rows)
    copies = []
    for k in range(1, n):
        peer = (me + k) % n
        c = pltpu.make_async_remote_copy(
            src_ref=x_ref, dst_ref=o_ref.at[mine], send_sem=send_sems.at[k],
            recv_sem=recv_sems.at[k], device_id=dev(peer), device_id_type=MESH)
        c.start()
        copies.append(c)
    o_ref[mine, :] = x_ref[...]
    size = f_ref.shape[1]
    for t, shift in enumerate(shifts):
        y = jnp.dot(w_ref[t], f_ref[...], preferred_element_type=jnp.float32)
        if shift % size:
            y = pltpu.roll(y, (-shift) % size, 1)
        y = y * m_ref[pl.ds(t, 1), :]
        if t == 0:
            t_ref[...] = y
        else:
            t_ref[...] += y
    wide = f_ref[...].astype(jnp.float32)
    for t, shift in enumerate(shifts):
        v = pltpu.roll(wide, (-shift) % size, 1) if shift % size else wide
        xs[t] = (v * m_ref[pl.ds(t, 1), :]).astype(xs.dtype)
    for k in range(1, n):
        src = (me + n - k) % n
        theirs = pl.ds(pl.multiple_of(src * rows, 16), rows)
        pltpu.make_async_remote_copy(
            src_ref=x_ref, dst_ref=o_ref.at[theirs], send_sem=send_sems.at[k],
            recv_sem=recv_sems.at[k], device_id=dev(src), device_id_type=MESH).wait_recv()
    started = before_wgrad() if before_wgrad is not None else None
    cin = f_ref.shape[0]
    for t in range(len(shifts)):
        wg_ref[pl.ds(t * cin, cin), :] = lax.dot_general(
            xs[t], o_ref[...], (((1,), (1,)), ((), ())), preferred_element_type=jnp.float32)
    for c in copies:
        c.wait_send()
    return started


def chan_allgather(x, axis_names, w, f, masks, shifts):
    rows, cols = x.shape
    n = lax.axis_size("chan")
    vmem = pltpu.VMEM
    return pl.pallas_call(
        functools.partial(_allgather_kernel, axis_names, n, shifts),
        out_shape=(
            jax.ShapeDtypeStruct((rows * n, cols), x.dtype),
            jax.ShapeDtypeStruct((w.shape[1], f.shape[1]), jnp.float32),
            jax.ShapeDtypeStruct((len(shifts) * f.shape[0], rows * n), jnp.float32),
        ),
        in_specs=[pl.BlockSpec(memory_space=vmem)] * 4,
        out_specs=(pl.BlockSpec(memory_space=vmem),) * 3,
        scratch_shapes=[
            vmem((len(shifts),) + f.shape, f.dtype),
            pltpu.SemaphoreType.DMA((n,)),
            pltpu.SemaphoreType.DMA((n,)),
        ],
        compiler_params=pltpu.CompilerParams(
            collective_id=1, has_side_effects=True, vmem_limit_bytes=48 * 1024 * 1024
        ),
    )(x, w, f, masks)


def _fused_kernel(axis_names, nz, nc, streams, shifts, x_ref, wf_ref, f_ref, mf_ref, wb_ref, mb_ref,
                  o_ref, res_ref, ig_ref, g_s, t_s, wg_s, xs, ag_send, ag_recv, *ar_scratch):
    MESH = pl.DeviceIdType.MESH
    dp = lax.axis_index("dp")
    me = lax.axis_index("chan")
    nd = 4 * nz
    core = dp % 2
    xl = (dp // 2) % 2
    peers = (dp + 1 - 2 * core, dp + 2 - 4 * xl, (dp + 4) % nd, (dp + nd - 4) % nd)
    barrier = pltpu.get_barrier_semaphore()
    for peer in peers:
        pl.semaphore_signal(barrier, inc=1, device_id=tuple(peer if a == "dp" else lax.axis_index(a) for a in axis_names), device_id_type=MESH)
    for k in range(1, nc):
        pl.semaphore_signal(barrier, inc=1, device_id=tuple((me + k) % nc if a == "chan" else lax.axis_index(a) for a in axis_names), device_id_type=MESH)
    pl.semaphore_wait(barrier, 4 + nc - 1)
    rs_buf, rs_send, rs_recv = ar_scratch[8], ar_scratch[12], ar_scratch[13]

    def scatter():
        return start_chan_scatter(axis_names, nc, t_s, rs_buf, rs_send, rs_recv, res_ref.shape[0])

    started = _allgather_kernel(axis_names, nc, shifts, x_ref, wf_ref, f_ref, mf_ref, g_s, t_s,
                                wg_s, xs, ag_send, ag_recv, entry_barrier=False,
                                before_wgrad=scatter)
    _allreduce_kernel(axis_names, nz, nc, streams, shifts, wg_s, t_s, wb_ref, g_s, mb_ref,
                      o_ref, res_ref, ig_ref, *ar_scratch, entry_barrier=False,
                      rs_started=started)


def fused_step(x, wf, f, mf, wb, mb, shifts, axis_names):
    nc = lax.axis_size("chan")
    nz = lax.axis_size("dp") // 4
    rows_x, cols = x.shape
    cin, taps = f.shape[0], len(shifts)
    cout = rows_x * nc
    rows, width = taps * cin, cout
    owned = cout // nc
    half = rows // 2
    chunk = half // nz
    lanes = width // 2
    n_copies = nz + 3 + 6 * (nz - 1) * STREAMS
    vmem = pltpu.VMEM
    f32 = jnp.float32
    return pl.pallas_call(
        functools.partial(_fused_kernel, axis_names, nz, nc, STREAMS, shifts),
        out_shape=(
            jax.ShapeDtypeStruct((rows, width), f32),
            jax.ShapeDtypeStruct((owned, cols), jnp.bfloat16),
            jax.ShapeDtypeStruct((cin, cols), jnp.bfloat16),
        ),
        in_specs=[pl.BlockSpec(memory_space=vmem)] * 6,
        out_specs=(pl.BlockSpec(memory_space=vmem),) * 3,
        scratch_shapes=[
            vmem((cout, cols), x.dtype),
            vmem((cout, cols), f32),
            vmem((rows, width), f32),
            vmem((taps,) + f.shape, f.dtype),
            pltpu.SemaphoreType.DMA((nc,)),
            pltpu.SemaphoreType.DMA((nc,)),
            vmem((half, width), f32),
            vmem((half, width), f32),
            vmem((chunk, width), f32),
            vmem((chunk, width), f32),
            vmem((nz - 1, chunk, lanes), f32),
            vmem((nz - 1, chunk, lanes), f32),
            vmem((nz - 1, chunk, lanes), f32),
            vmem((nz - 1, chunk, lanes), f32),
            vmem((nc, owned, cols), f32),
            vmem((cin, cols), f32),
            pltpu.SemaphoreType.DMA((n_copies,)),
            pltpu.SemaphoreType.DMA((n_copies,)),
            pltpu.SemaphoreType.DMA((nc,)),
            pltpu.SemaphoreType.DMA((nc,)),
        ],
        compiler_params=pltpu.CompilerParams(
            collective_id=0, has_side_effects=True, vmem_limit_bytes=56 * 1024 * 1024
        ),
    )(x, wf, f, mf, wb, mb)


def on_device(axis_names, inputs, weight, cotangent):
    input_channels_local = inputs.shape[1]
    cout_local = cotangent.shape[1]
    tap_locations = MAP_HEIGHT * MAP_WIDTH
    feature_map = inputs[0].reshape(input_channels_local, MAP_HEIGHT, MAP_WIDTH)
    tap_list = weight.shape[1]
    output_channels_total = weight.shape[2]
    tap_shifts = [
        (DILATION_RATE * (tap_index // 3 - 1), DILATION_RATE * (tap_index % 3 - 1))
        for tap_index in range(tap_list)
    ]
    rows_idx = np.arange(tap_locations) // MAP_WIDTH
    cols_idx = np.arange(tap_locations) % MAP_WIDTH
    masks = np.stack(
        [
            ((rows_idx + a >= 0) & (rows_idx + a < MAP_HEIGHT) & (cols_idx + b >= 0) & (cols_idx + b < MAP_WIDTH))
            for a, b in tap_shifts
        ]
    ).astype(np.float32)
    back_masks = np.stack(
        [
            ((rows_idx - a >= 0) & (rows_idx - a < MAP_HEIGHT) & (cols_idx - b >= 0) & (cols_idx - b < MAP_WIDTH))
            for a, b in tap_shifts
        ]
    ).astype(np.float32)
    summed, owned, back = fused_step(
        cotangent[0],
        jnp.transpose(weight, (1, 2, 0)),
        inputs[0],
        jnp.asarray(masks),
        jnp.transpose(weight, (1, 0, 2)),
        jnp.asarray(back_masks),
        tuple(a * MAP_WIDTH + b for a, b in tap_shifts),
        axis_names,
    )
    result = owned.reshape(1, cout_local, tap_locations)
    summed_grad = jnp.transpose(
        summed.reshape(tap_list, input_channels_local, output_channels_total), (1, 0, 2)
    )
    weight_grad = summed_grad / jnp.float32(lax.axis_size("dp"))
    input_grad = back.reshape(1, input_channels_local, tap_locations)
    return (result, input_grad, weight_grad)


def solution(mesh):
    placed = (P("dp", "chan", None), P("chan", None, None), P("dp", "chan", None))
    return jax.shard_map(
        functools.partial(on_device, tuple(mesh.axis_names)),
        mesh=mesh,
        in_specs=placed,
        out_specs=(P("dp", "chan", None), P("dp", "chan", None), P("chan", None, None)),
        check_vma=False,
    )
```

```python
import functools

import jax
import jax.numpy as jnp
import numpy as np
from jax import lax
from jax.experimental import pallas as pl
from jax.experimental.pallas import tpu as pltpu
from jax.sharding import PartitionSpec as P

DILATION_RATE = 12
MAP_HEIGHT = 16
MAP_WIDTH = 72
STREAMS = 3


def translated_input(receptive_field, row_shift, column_shift, reach):
    height, width = (receptive_field.shape[1], receptive_field.shape[2])
    bordered_input = jnp.pad(receptive_field, ((0, 0), (reach, reach), (reach, reach)))
    return bordered_input[
        :,
        reach + row_shift : reach + row_shift + height,
        reach + column_shift : reach + column_shift + width,
    ]


def _allreduce_kernel(axis_names, nz, nc, streams, shifts, a_ref, t_ref, w_ref, g_ref, m_ref,
                      o_ref, res_ref, ig_ref, rc, s1, f1, rx, rp, rm, ap, am, rs_buf, ig_acc,
                      send_sems, recv_sems, rs_send, rs_recv, entry_barrier=True):
    rows, cols = a_ref.shape
    half = rows // 2
    chunk = half // nz
    lanes = cols // 2
    MESH = pl.DeviceIdType.MESH
    dp = lax.axis_index("dp")
    core = dp % 2
    xl = (dp // 2) % 2
    z = dp // 4
    nd = 4 * nz
    pc = dp + 1 - 2 * core
    px = dp + 2 - 4 * xl
    zr = (dp + 4) % nd
    zl = (dp + nd - 4) % nd

    me = lax.axis_index("chan")

    def dev(p):
        return tuple(p if n == "dp" else lax.axis_index(n) for n in axis_names)

    def cdev(p):
        return tuple(p if n == "chan" else lax.axis_index(n) for n in axis_names)

    if entry_barrier:
        barrier = pltpu.get_barrier_semaphore()
        for peer in (pc, px, zr, zl):
            pl.semaphore_signal(barrier, inc=1, device_id=dev(peer), device_id_type=MESH)
        for k in range(1, nc):
            pl.semaphore_signal(barrier, inc=1, device_id=cdev((me + k) % nc), device_id_type=MESH)
        pl.semaphore_wait(barrier, 4 + nc - 1)

    owned = res_ref.shape[0]
    rs_copies = []
    for k in range(1, nc):
        peer = (me + k) % nc
        c = pltpu.make_async_remote_copy(
            src_ref=t_ref.at[pl.ds(pl.multiple_of(peer * owned, 8), owned)],
            dst_ref=rs_buf.at[k], send_sem=rs_send.at[k], recv_sem=rs_recv.at[k],
            device_id=cdev(peer), device_id_type=MESH)
        c.start()
        rs_copies.append(c)

    sent = []
    counter = [0]

    def remote(src, dst, peer):
        k = counter[0]
        counter[0] += 1
        c = pltpu.make_async_remote_copy(
            src_ref=src, dst_ref=dst, send_sem=send_sems.at[k], recv_sem=recv_sems.at[k],
            device_id=dev(peer), device_id_type=MESH)
        c.start()
        sent.append(c)
        return c

    def rows_of(j):
        return pl.ds(pl.multiple_of(j * chunk, 8), chunk)

    done_taps = [0]
    size = g_ref.shape[1]

    def input_grad_tap():
        t = done_taps[0]
        if t < len(shifts):
            y = jnp.dot(w_ref[t], g_ref[...], preferred_element_type=jnp.float32)
            if shifts[t] % size:
                y = pltpu.roll(y, shifts[t] % size, 1)
            y = y * m_ref[pl.ds(t, 1), :]
            if t == 0:
                ig_acc[...] = y
            else:
                ig_acc[...] += y
            done_taps[0] += 1

    mine_c = core * half
    other_c = (1 - core) * half
    order = []
    for d in range(1, nz // 2 + 1):
        order.append((z + nz - d) % nz)
        if 2 * d != nz:
            order.append((z + d) % nz)
    order.append(z)
    core_in = []
    for j in order:
        src_rows = pl.ds(pl.multiple_of(other_c + j * chunk, 8), chunk)
        core_in.append((j, remote(a_ref.at[src_rows], rc.at[rows_of(j)], pc)))
    ready = [0]

    def ready_upto(n):
        while ready[0] < n:
            j, c = core_in[ready[0]]
            c.wait_recv()
            own_rows = pl.ds(pl.multiple_of(mine_c + j * chunk, 8), chunk)
            s1[rows_of(j), :] = a_ref[own_rows, :] + rc[rows_of(j), :]
            ready[0] += 1

    def needed(d):
        return min(len(order) - 1, 2 * d - (1 if 2 * d == nz else 0))

    lo = pl.ds(0, lanes)
    hi = pl.ds(lanes, lanes)
    sub = chunk // streams

    def srows(j, q):
        return pl.ds(pl.multiple_of(j * chunk + q * sub, 8), sub)

    blk = [pl.ds(q * sub, sub) for q in range(streams)]
    pending = [None] * streams
    for s in range(nz - 1):
        jp = (z + 2 * nz - 1 - s) % nz
        jm = (z + 1 + s) % nz
        if s + 1 <= nz // 2:
            ready_upto(needed(s + 1))
        for q in range(streams):
            if s == 0:
                src_p = s1.at[srows(jp, q), lo]
                src_m = s1.at[srows(jm, q), hi]
            else:
                pending[q][0].wait_recv()
                pending[q][1].wait_recv()
                ap[s, blk[q], :] = s1[srows(jp, q), lo] + rp[s - 1, blk[q], :]
                am[s, blk[q], :] = s1[srows(jm, q), hi] + rm[s - 1, blk[q], :]
                src_p = ap.at[s, blk[q]]
                src_m = am.at[s, blk[q]]
            pending[q] = (remote(src_p, rp.at[s, blk[q]], zr), remote(src_m, rm.at[s, blk[q]], zl))
    for q in range(streams):
        pending[q][0].wait_recv()
        pending[q][1].wait_recv()
    ready_upto(len(order))
    f1[:, lo] = s1[rows_of(z), lo] + rp[nz - 2]
    f1[:, hi] = s1[rows_of(z), hi] + rm[nz - 2]

    c = remote(f1, rx, px)
    c.wait_recv()
    own_chunk = pl.ds(pl.multiple_of(core * half + z * chunk, 8), chunk)
    o_ref[own_chunk, :] = f1[...] + rx[...]

    to_core = [remote(o_ref.at[own_chunk], o_ref.at[own_chunk], pc)]

    def grows(j, q):
        return pl.ds(pl.multiple_of(core * half + j * chunk + q * sub, 8), sub)

    def arrived(q, jp, jm):
        pending[q][0].wait_recv()
        pending[q][1].wait_recv()
        gp = grows((jp + nz - 1) % nz, q)
        gm = grows((jm + 1) % nz, q)
        to_core.append(remote(o_ref.at[gp, lo], o_ref.at[gp, lo], pc))
        to_core.append(remote(o_ref.at[gm, hi], o_ref.at[gm, hi], pc))

    for s in range(nz - 1):
        jp = (z + nz - s) % nz
        jm = (z + s) % nz
        for q in range(streams):
            if s > 0:
                arrived(q, (jp + 1) % nz, (jm + nz - 1) % nz)
            gp = grows(jp, q)
            gm = grows(jm, q)
            pending[q] = (remote(o_ref.at[gp, lo], o_ref.at[gp, lo], zr),
                          remote(o_ref.at[gm, hi], o_ref.at[gm, hi], zl))
        input_grad_tap()
        if s == nz - 2:
            while done_taps[0] < len(shifts):
                input_grad_tap()
    for q in range(streams):
        arrived(q, (z + 2) % nz, (z + nz - 2) % nz)
    for c in to_core:
        c.wait_recv()

    for c in rs_copies:
        c.wait_recv()
    acc = t_ref[pl.ds(pl.multiple_of(me * owned, 8), owned), :]
    for k in range(1, nc):
        acc = acc + rs_buf[k]
    res_ref[...] = acc.astype(res_ref.dtype)
    ig_ref[...] = ig_acc[...].astype(ig_ref.dtype)

    for c in sent + rs_copies:
        c.wait_send()


def dp_allreduce(a, t, w, g, masks, shifts, axis_names):
    rows, cols = a.shape
    nc = lax.axis_size("chan")
    owned = t.shape[0] // nc
    nz = lax.axis_size("dp") // 4
    half = rows // 2
    chunk = half // nz
    lanes = cols // 2
    n_copies = nz + 3 + 6 * (nz - 1) * STREAMS
    vmem = pltpu.VMEM
    return pl.pallas_call(
        functools.partial(_allreduce_kernel, axis_names, nz, nc, STREAMS, shifts),
        out_shape=(
            jax.ShapeDtypeStruct((rows, cols), a.dtype),
            jax.ShapeDtypeStruct((owned, t.shape[1]), jnp.bfloat16),
            jax.ShapeDtypeStruct((w.shape[1], g.shape[1]), jnp.bfloat16),
        ),
        in_specs=[pl.BlockSpec(memory_space=vmem)] * 5,
        out_specs=(pl.BlockSpec(memory_space=vmem),) * 3,
        scratch_shapes=[
            vmem((half, cols), a.dtype),
            vmem((half, cols), a.dtype),
            vmem((chunk, cols), a.dtype),
            vmem((chunk, cols), a.dtype),
            vmem((nz - 1, chunk, lanes), a.dtype),
            vmem((nz - 1, chunk, lanes), a.dtype),
            vmem((nz - 1, chunk, lanes), a.dtype),
            vmem((nz - 1, chunk, lanes), a.dtype),
            vmem((nc, owned, t.shape[1]), t.dtype),
            vmem((w.shape[1], g.shape[1]), jnp.float32),
            pltpu.SemaphoreType.DMA((n_copies,)),
            pltpu.SemaphoreType.DMA((n_copies,)),
            pltpu.SemaphoreType.DMA((nc,)),
            pltpu.SemaphoreType.DMA((nc,)),
        ],
        compiler_params=pltpu.CompilerParams(
            collective_id=0, has_side_effects=True, vmem_limit_bytes=48 * 1024 * 1024
        ),
    )(a, t, w, g, masks)


def _allgather_kernel(axis_names, n, shifts, x_ref, w_ref, f_ref, m_ref, o_ref, t_ref, wg_ref,
                      xs, send_sems, recv_sems, entry_barrier=True):
    rows = x_ref.shape[0]
    MESH = pl.DeviceIdType.MESH
    me = lax.axis_index("chan")

    def dev(p):
        return tuple(p if a == "chan" else lax.axis_index(a) for a in axis_names)

    if entry_barrier:
        barrier = pltpu.get_barrier_semaphore()
        for k in range(1, n):
            pl.semaphore_signal(barrier, inc=1, device_id=dev((me + k) % n), device_id_type=MESH)
        pl.semaphore_wait(barrier, n - 1)

    mine = pl.ds(pl.multiple_of(me * rows, 16), rows)
    copies = []
    for k in range(1, n):
        peer = (me + k) % n
        c = pltpu.make_async_remote_copy(
            src_ref=x_ref, dst_ref=o_ref.at[mine], send_sem=send_sems.at[k],
            recv_sem=recv_sems.at[k], device_id=dev(peer), device_id_type=MESH)
        c.start()
        copies.append(c)
    o_ref[mine, :] = x_ref[...]
    size = f_ref.shape[1]
    for t, shift in enumerate(shifts):
        y = jnp.dot(w_ref[t], f_ref[...], preferred_element_type=jnp.float32)
        if shift % size:
            y = pltpu.roll(y, (-shift) % size, 1)
        y = y * m_ref[pl.ds(t, 1), :]
        if t == 0:
            t_ref[...] = y
        else:
            t_ref[...] += y
    wide = f_ref[...].astype(jnp.float32)
    for t, shift in enumerate(shifts):
        v = pltpu.roll(wide, (-shift) % size, 1) if shift % size else wide
        xs[t] = (v * m_ref[pl.ds(t, 1), :]).astype(xs.dtype)
    for k in range(1, n):
        src = (me + n - k) % n
        theirs = pl.ds(pl.multiple_of(src * rows, 16), rows)
        pltpu.make_async_remote_copy(
            src_ref=x_ref, dst_ref=o_ref.at[theirs], send_sem=send_sems.at[k],
            recv_sem=recv_sems.at[k], device_id=dev(src), device_id_type=MESH).wait_recv()
    cin = f_ref.shape[0]
    for t in range(len(shifts)):
        wg_ref[pl.ds(t * cin, cin), :] = lax.dot_general(
            xs[t], o_ref[...], (((1,), (1,)), ((), ())), preferred_element_type=jnp.float32)
    for c in copies:
        c.wait_send()


def chan_allgather(x, axis_names, w, f, masks, shifts):
    rows, cols = x.shape
    n = lax.axis_size("chan")
    vmem = pltpu.VMEM
    return pl.pallas_call(
        functools.partial(_allgather_kernel, axis_names, n, shifts),
        out_shape=(
            jax.ShapeDtypeStruct((rows * n, cols), x.dtype),
            jax.ShapeDtypeStruct((w.shape[1], f.shape[1]), jnp.float32),
            jax.ShapeDtypeStruct((len(shifts) * f.shape[0], rows * n), jnp.float32),
        ),
        in_specs=[pl.BlockSpec(memory_space=vmem)] * 4,
        out_specs=(pl.BlockSpec(memory_space=vmem),) * 3,
        scratch_shapes=[
            vmem((len(shifts),) + f.shape, f.dtype),
            pltpu.SemaphoreType.DMA((n,)),
            pltpu.SemaphoreType.DMA((n,)),
        ],
        compiler_params=pltpu.CompilerParams(
            collective_id=1, has_side_effects=True, vmem_limit_bytes=48 * 1024 * 1024
        ),
    )(x, w, f, masks)


def _fused_kernel(axis_names, nz, nc, streams, shifts, x_ref, wf_ref, f_ref, mf_ref, wb_ref, mb_ref,
                  o_ref, res_ref, ig_ref, g_s, t_s, wg_s, xs, ag_send, ag_recv, *ar_scratch):
    MESH = pl.DeviceIdType.MESH
    dp = lax.axis_index("dp")
    me = lax.axis_index("chan")
    nd = 4 * nz
    core = dp % 2
    xl = (dp // 2) % 2
    peers = (dp + 1 - 2 * core, dp + 2 - 4 * xl, (dp + 4) % nd, (dp + nd - 4) % nd)
    barrier = pltpu.get_barrier_semaphore()
    for peer in peers:
        pl.semaphore_signal(barrier, inc=1, device_id=tuple(peer if a == "dp" else lax.axis_index(a) for a in axis_names), device_id_type=MESH)
    for k in range(1, nc):
        pl.semaphore_signal(barrier, inc=1, device_id=tuple((me + k) % nc if a == "chan" else lax.axis_index(a) for a in axis_names), device_id_type=MESH)
    pl.semaphore_wait(barrier, 4 + nc - 1)
    _allgather_kernel(axis_names, nc, shifts, x_ref, wf_ref, f_ref, mf_ref, g_s, t_s, wg_s, xs,
                      ag_send, ag_recv, entry_barrier=False)
    o_s = ar_scratch[-1]
    _allreduce_kernel(axis_names, nz, nc, streams, shifts, wg_s, t_s, wb_ref, g_s, mb_ref,
                      o_s, res_ref, ig_ref, *ar_scratch[:-1], entry_barrier=False)
    cin = o_ref.shape[0]
    for t in range(o_ref.shape[1]):
        o_ref[:, t, :] = o_s[pl.ds(t * cin, cin), :] * (1.0 / (4 * nz))


def fused_step(x, wf, f, mf, wb, mb, shifts, axis_names):
    nc = lax.axis_size("chan")
    nz = lax.axis_size("dp") // 4
    rows_x, cols = x.shape
    cin, taps = f.shape[0], len(shifts)
    cout = rows_x * nc
    rows, width = taps * cin, cout
    owned = cout // nc
    half = rows // 2
    chunk = half // nz
    lanes = width // 2
    n_copies = nz + 3 + 6 * (nz - 1) * STREAMS
    vmem = pltpu.VMEM
    f32 = jnp.float32
    return pl.pallas_call(
        functools.partial(_fused_kernel, axis_names, nz, nc, STREAMS, shifts),
        out_shape=(
            jax.ShapeDtypeStruct((cin, taps, width), f32),
            jax.ShapeDtypeStruct((owned, cols), jnp.bfloat16),
            jax.ShapeDtypeStruct((cin, cols), jnp.bfloat16),
        ),
        in_specs=[pl.BlockSpec(memory_space=vmem)] * 6,
        out_specs=(pl.BlockSpec(memory_space=vmem),) * 3,
        scratch_shapes=[
            vmem((cout, cols), x.dtype),
            vmem((cout, cols), f32),
            vmem((rows, width), f32),
            vmem((taps,) + f.shape, f.dtype),
            pltpu.SemaphoreType.DMA((nc,)),
            pltpu.SemaphoreType.DMA((nc,)),
            vmem((half, width), f32),
            vmem((half, width), f32),
            vmem((chunk, width), f32),
            vmem((chunk, width), f32),
            vmem((nz - 1, chunk, lanes), f32),
            vmem((nz - 1, chunk, lanes), f32),
            vmem((nz - 1, chunk, lanes), f32),
            vmem((nz - 1, chunk, lanes), f32),
            vmem((nc, owned, cols), f32),
            vmem((cin, cols), f32),
            pltpu.SemaphoreType.DMA((n_copies,)),
            pltpu.SemaphoreType.DMA((n_copies,)),
            pltpu.SemaphoreType.DMA((nc,)),
            pltpu.SemaphoreType.DMA((nc,)),
            vmem((rows, width), f32),
        ],
        compiler_params=pltpu.CompilerParams(
            collective_id=0, has_side_effects=True, vmem_limit_bytes=56 * 1024 * 1024
        ),
    )(x, wf, f, mf, wb, mb)


def on_device(axis_names, inputs, weight, cotangent):
    input_channels_local = inputs.shape[1]
    cout_local = cotangent.shape[1]
    tap_locations = MAP_HEIGHT * MAP_WIDTH
    feature_map = inputs[0].reshape(input_channels_local, MAP_HEIGHT, MAP_WIDTH)
    tap_list = weight.shape[1]
    output_channels_total = weight.shape[2]
    tap_shifts = [
        (DILATION_RATE * (tap_index // 3 - 1), DILATION_RATE * (tap_index % 3 - 1))
        for tap_index in range(tap_list)
    ]
    rows_idx = np.arange(tap_locations) // MAP_WIDTH
    cols_idx = np.arange(tap_locations) % MAP_WIDTH
    masks = np.stack(
        [
            ((rows_idx + a >= 0) & (rows_idx + a < MAP_HEIGHT) & (cols_idx + b >= 0) & (cols_idx + b < MAP_WIDTH))
            for a, b in tap_shifts
        ]
    ).astype(np.float32)
    back_masks = np.stack(
        [
            ((rows_idx - a >= 0) & (rows_idx - a < MAP_HEIGHT) & (cols_idx - b >= 0) & (cols_idx - b < MAP_WIDTH))
            for a, b in tap_shifts
        ]
    ).astype(np.float32)
    summed, owned, back = fused_step(
        cotangent[0],
        jnp.transpose(weight, (1, 2, 0)),
        inputs[0],
        jnp.asarray(masks),
        jnp.transpose(weight, (1, 0, 2)),
        jnp.asarray(back_masks),
        tuple(a * MAP_WIDTH + b for a, b in tap_shifts),
        axis_names,
    )
    result = owned.reshape(1, cout_local, tap_locations)
    weight_grad = summed
    input_grad = back.reshape(1, input_channels_local, tap_locations)
    return (result, input_grad, weight_grad)


def solution(mesh):
    placed = (P("dp", "chan", None), P("chan", None, None), P("dp", "chan", None))
    return jax.shard_map(
        functools.partial(on_device, tuple(mesh.axis_names)),
        mesh=mesh,
        in_specs=placed,
        out_specs=(P("dp", "chan", None), P("dp", "chan", None), P("chan", None, None)),
        check_vma=False,
    )
```

```python
import functools

import jax
import jax.numpy as jnp
import numpy as np
from jax import lax
from jax.experimental import pallas as pl
from jax.experimental.pallas import tpu as pltpu
from jax.sharding import PartitionSpec as P

DILATION_RATE = 12
MAP_HEIGHT = 16
MAP_WIDTH = 72
STREAMS = 3


def translated_input(receptive_field, row_shift, column_shift, reach):
    height, width = (receptive_field.shape[1], receptive_field.shape[2])
    bordered_input = jnp.pad(receptive_field, ((0, 0), (reach, reach), (reach, reach)))
    return bordered_input[
        :,
        reach + row_shift : reach + row_shift + height,
        reach + column_shift : reach + column_shift + width,
    ]


def _allreduce_kernel(axis_names, nz, nc, streams, shifts, a_ref, t_ref, w_ref, g_ref, m_ref,
                      o_ref, res_ref, ig_ref, rc, s1, f1, rx, rp, rm, ap, am, rs_buf, ig_acc,
                      send_sems, recv_sems, rs_send, rs_recv, entry_barrier=True):
    rows, cols = a_ref.shape
    half = rows // 2
    chunk = half // nz
    lanes = cols // 2
    MESH = pl.DeviceIdType.MESH
    dp = lax.axis_index("dp")
    core = dp % 2
    xl = (dp // 2) % 2
    z = dp // 4
    nd = 4 * nz
    pc = dp + 1 - 2 * core
    px = dp + 2 - 4 * xl
    zr = (dp + 4) % nd
    zl = (dp + nd - 4) % nd

    me = lax.axis_index("chan")

    def dev(p):
        return tuple(p if n == "dp" else lax.axis_index(n) for n in axis_names)

    def cdev(p):
        return tuple(p if n == "chan" else lax.axis_index(n) for n in axis_names)

    if entry_barrier:
        barrier = pltpu.get_barrier_semaphore()
        for peer in (pc, px, zr, zl):
            pl.semaphore_signal(barrier, inc=1, device_id=dev(peer), device_id_type=MESH)
        for k in range(1, nc):
            pl.semaphore_signal(barrier, inc=1, device_id=cdev((me + k) % nc), device_id_type=MESH)
        pl.semaphore_wait(barrier, 4 + nc - 1)

    owned = res_ref.shape[0]
    rs_copies = []
    for k in range(1, nc):
        peer = (me + k) % nc
        c = pltpu.make_async_remote_copy(
            src_ref=t_ref.at[pl.ds(pl.multiple_of(peer * owned, 8), owned)],
            dst_ref=rs_buf.at[k], send_sem=rs_send.at[k], recv_sem=rs_recv.at[k],
            device_id=cdev(peer), device_id_type=MESH)
        c.start()
        rs_copies.append(c)

    sent = []
    counter = [0]

    def remote(src, dst, peer):
        k = counter[0]
        counter[0] += 1
        c = pltpu.make_async_remote_copy(
            src_ref=src, dst_ref=dst, send_sem=send_sems.at[k], recv_sem=recv_sems.at[k],
            device_id=dev(peer), device_id_type=MESH)
        c.start()
        sent.append(c)
        return c

    def rows_of(j):
        return pl.ds(pl.multiple_of(j * chunk, 8), chunk)

    done_taps = [0]
    size = g_ref.shape[1]

    def input_grad_tap():
        t = done_taps[0]
        if t < len(shifts):
            y = jnp.dot(w_ref[t], g_ref[...], preferred_element_type=jnp.float32)
            if shifts[t] % size:
                y = pltpu.roll(y, shifts[t] % size, 1)
            y = y * m_ref[pl.ds(t, 1), :]
            if t == 0:
                ig_acc[...] = y
            else:
                ig_acc[...] += y
            done_taps[0] += 1

    mine_c = core * half
    other_c = (1 - core) * half
    order = []
    for d in range(1, nz // 2 + 1):
        order.append((z + nz - d) % nz)
        if 2 * d != nz:
            order.append((z + d) % nz)
    order.append(z)
    core_in = []
    for j in order:
        src_rows = pl.ds(pl.multiple_of(other_c + j * chunk, 8), chunk)
        core_in.append((j, remote(a_ref.at[src_rows], rc.at[rows_of(j)], pc)))
    ready = [0]

    def ready_upto(n):
        while ready[0] < n:
            j, c = core_in[ready[0]]
            c.wait_recv()
            own_rows = pl.ds(pl.multiple_of(mine_c + j * chunk, 8), chunk)
            s1[rows_of(j), :] = a_ref[own_rows, :] + rc[rows_of(j), :]
            ready[0] += 1

    def needed(d):
        return min(len(order) - 1, 2 * d - (1 if 2 * d == nz else 0))

    lo = pl.ds(0, lanes)
    hi = pl.ds(lanes, lanes)
    sub = chunk // streams

    def srows(j, q):
        return pl.ds(pl.multiple_of(j * chunk + q * sub, 8), sub)

    blk = [pl.ds(q * sub, sub) for q in range(streams)]
    pending = [None] * streams
    for s in range(nz - 1):
        jp = (z + 2 * nz - 1 - s) % nz
        jm = (z + 1 + s) % nz
        if s + 1 <= nz // 2:
            ready_upto(needed(s + 1))
        for q in range(streams):
            if s == 0:
                src_p = s1.at[srows(jp, q), lo]
                src_m = s1.at[srows(jm, q), hi]
            else:
                pending[q][0].wait_recv()
                pending[q][1].wait_recv()
                ap[s, blk[q], :] = s1[srows(jp, q), lo] + rp[s - 1, blk[q], :]
                am[s, blk[q], :] = s1[srows(jm, q), hi] + rm[s - 1, blk[q], :]
                src_p = ap.at[s, blk[q]]
                src_m = am.at[s, blk[q]]
            pending[q] = (remote(src_p, rp.at[s, blk[q]], zr), remote(src_m, rm.at[s, blk[q]], zl))
        input_grad_tap()
    for q in range(streams):
        pending[q][0].wait_recv()
        pending[q][1].wait_recv()
    ready_upto(len(order))
    f1[:, lo] = s1[rows_of(z), lo] + rp[nz - 2]
    f1[:, hi] = s1[rows_of(z), hi] + rm[nz - 2]

    c = remote(f1, rx, px)
    c.wait_recv()
    own_chunk = pl.ds(pl.multiple_of(core * half + z * chunk, 8), chunk)
    o_ref[own_chunk, :] = f1[...] + rx[...]

    to_core = [remote(o_ref.at[own_chunk], o_ref.at[own_chunk], pc)]

    def grows(j, q):
        return pl.ds(pl.multiple_of(core * half + j * chunk + q * sub, 8), sub)

    def arrived(q, jp, jm):
        pending[q][0].wait_recv()
        pending[q][1].wait_recv()
        gp = grows((jp + nz - 1) % nz, q)
        gm = grows((jm + 1) % nz, q)
        to_core.append(remote(o_ref.at[gp, lo], o_ref.at[gp, lo], pc))
        to_core.append(remote(o_ref.at[gm, hi], o_ref.at[gm, hi], pc))

    for s in range(nz - 1):
        jp = (z + nz - s) % nz
        jm = (z + s) % nz
        for q in range(streams):
            if s > 0:
                arrived(q, (jp + 1) % nz, (jm + nz - 1) % nz)
            gp = grows(jp, q)
            gm = grows(jm, q)
            pending[q] = (remote(o_ref.at[gp, lo], o_ref.at[gp, lo], zr),
                          remote(o_ref.at[gm, hi], o_ref.at[gm, hi], zl))
        input_grad_tap()
        if s == nz - 2:
            while done_taps[0] < len(shifts):
                input_grad_tap()
    for q in range(streams):
        arrived(q, (z + 2) % nz, (z + nz - 2) % nz)
    for c in to_core:
        c.wait_recv()

    for c in rs_copies:
        c.wait_recv()
    acc = t_ref[pl.ds(pl.multiple_of(me * owned, 8), owned), :]
    for k in range(1, nc):
        acc = acc + rs_buf[k]
    res_ref[...] = acc.astype(res_ref.dtype)
    ig_ref[...] = ig_acc[...].astype(ig_ref.dtype)

    for c in sent + rs_copies:
        c.wait_send()


def dp_allreduce(a, t, w, g, masks, shifts, axis_names):
    rows, cols = a.shape
    nc = lax.axis_size("chan")
    owned = t.shape[0] // nc
    nz = lax.axis_size("dp") // 4
    half = rows // 2
    chunk = half // nz
    lanes = cols // 2
    n_copies = nz + 3 + 6 * (nz - 1) * STREAMS
    vmem = pltpu.VMEM
    return pl.pallas_call(
        functools.partial(_allreduce_kernel, axis_names, nz, nc, STREAMS, shifts),
        out_shape=(
            jax.ShapeDtypeStruct((rows, cols), a.dtype),
            jax.ShapeDtypeStruct((owned, t.shape[1]), jnp.bfloat16),
            jax.ShapeDtypeStruct((w.shape[1], g.shape[1]), jnp.bfloat16),
        ),
        in_specs=[pl.BlockSpec(memory_space=vmem)] * 5,
        out_specs=(pl.BlockSpec(memory_space=vmem),) * 3,
        scratch_shapes=[
            vmem((half, cols), a.dtype),
            vmem((half, cols), a.dtype),
            vmem((chunk, cols), a.dtype),
            vmem((chunk, cols), a.dtype),
            vmem((nz - 1, chunk, lanes), a.dtype),
            vmem((nz - 1, chunk, lanes), a.dtype),
            vmem((nz - 1, chunk, lanes), a.dtype),
            vmem((nz - 1, chunk, lanes), a.dtype),
            vmem((nc, owned, t.shape[1]), t.dtype),
            vmem((w.shape[1], g.shape[1]), jnp.float32),
            pltpu.SemaphoreType.DMA((n_copies,)),
            pltpu.SemaphoreType.DMA((n_copies,)),
            pltpu.SemaphoreType.DMA((nc,)),
            pltpu.SemaphoreType.DMA((nc,)),
        ],
        compiler_params=pltpu.CompilerParams(
            collective_id=0, has_side_effects=True, vmem_limit_bytes=48 * 1024 * 1024
        ),
    )(a, t, w, g, masks)


def _allgather_kernel(axis_names, n, shifts, x_ref, w_ref, f_ref, m_ref, o_ref, t_ref, wg_ref,
                      xs, send_sems, recv_sems, entry_barrier=True):
    rows = x_ref.shape[0]
    MESH = pl.DeviceIdType.MESH
    me = lax.axis_index("chan")

    def dev(p):
        return tuple(p if a == "chan" else lax.axis_index(a) for a in axis_names)

    if entry_barrier:
        barrier = pltpu.get_barrier_semaphore()
        for k in range(1, n):
            pl.semaphore_signal(barrier, inc=1, device_id=dev((me + k) % n), device_id_type=MESH)
        pl.semaphore_wait(barrier, n - 1)

    mine = pl.ds(pl.multiple_of(me * rows, 16), rows)
    copies = []
    for k in range(1, n):
        peer = (me + k) % n
        c = pltpu.make_async_remote_copy(
            src_ref=x_ref, dst_ref=o_ref.at[mine], send_sem=send_sems.at[k],
            recv_sem=recv_sems.at[k], device_id=dev(peer), device_id_type=MESH)
        c.start()
        copies.append(c)
    o_ref[mine, :] = x_ref[...]
    size = f_ref.shape[1]
    for t, shift in enumerate(shifts):
        y = jnp.dot(w_ref[t], f_ref[...], preferred_element_type=jnp.float32)
        if shift % size:
            y = pltpu.roll(y, (-shift) % size, 1)
        y = y * m_ref[pl.ds(t, 1), :]
        if t == 0:
            t_ref[...] = y
        else:
            t_ref[...] += y
    wide = f_ref[...].astype(jnp.float32)
    for t, shift in enumerate(shifts):
        v = pltpu.roll(wide, (-shift) % size, 1) if shift % size else wide
        xs[t] = (v * m_ref[pl.ds(t, 1), :]).astype(xs.dtype)
    for k in range(1, n):
        src = (me + n - k) % n
        theirs = pl.ds(pl.multiple_of(src * rows, 16), rows)
        pltpu.make_async_remote_copy(
            src_ref=x_ref, dst_ref=o_ref.at[theirs], send_sem=send_sems.at[k],
            recv_sem=recv_sems.at[k], device_id=dev(src), device_id_type=MESH).wait_recv()
    cin = f_ref.shape[0]
    for t in range(len(shifts)):
        wg_ref[pl.ds(t * cin, cin), :] = lax.dot_general(
            xs[t], o_ref[...], (((1,), (1,)), ((), ())), preferred_element_type=jnp.float32)
    for c in copies:
        c.wait_send()


def chan_allgather(x, axis_names, w, f, masks, shifts):
    rows, cols = x.shape
    n = lax.axis_size("chan")
    vmem = pltpu.VMEM
    return pl.pallas_call(
        functools.partial(_allgather_kernel, axis_names, n, shifts),
        out_shape=(
            jax.ShapeDtypeStruct((rows * n, cols), x.dtype),
            jax.ShapeDtypeStruct((w.shape[1], f.shape[1]), jnp.float32),
            jax.ShapeDtypeStruct((len(shifts) * f.shape[0], rows * n), jnp.float32),
        ),
        in_specs=[pl.BlockSpec(memory_space=vmem)] * 4,
        out_specs=(pl.BlockSpec(memory_space=vmem),) * 3,
        scratch_shapes=[
            vmem((len(shifts),) + f.shape, f.dtype),
            pltpu.SemaphoreType.DMA((n,)),
            pltpu.SemaphoreType.DMA((n,)),
        ],
        compiler_params=pltpu.CompilerParams(
            collective_id=1, has_side_effects=True, vmem_limit_bytes=48 * 1024 * 1024
        ),
    )(x, w, f, masks)


def _fused_kernel(axis_names, nz, nc, streams, shifts, x_ref, wf_ref, f_ref, mf_ref, wb_ref, mb_ref,
                  o_ref, res_ref, ig_ref, g_s, t_s, wg_s, xs, ag_send, ag_recv, *ar_scratch):
    MESH = pl.DeviceIdType.MESH
    dp = lax.axis_index("dp")
    me = lax.axis_index("chan")
    nd = 4 * nz
    core = dp % 2
    xl = (dp // 2) % 2
    peers = (dp + 1 - 2 * core, dp + 2 - 4 * xl, (dp + 4) % nd, (dp + nd - 4) % nd)
    barrier = pltpu.get_barrier_semaphore()
    for peer in peers:
        pl.semaphore_signal(barrier, inc=1, device_id=tuple(peer if a == "dp" else lax.axis_index(a) for a in axis_names), device_id_type=MESH)
    for k in range(1, nc):
        pl.semaphore_signal(barrier, inc=1, device_id=tuple((me + k) % nc if a == "chan" else lax.axis_index(a) for a in axis_names), device_id_type=MESH)
    pl.semaphore_wait(barrier, 4 + nc - 1)
    _allgather_kernel(axis_names, nc, shifts, x_ref, wf_ref, f_ref, mf_ref, g_s, t_s, wg_s, xs,
                      ag_send, ag_recv, entry_barrier=False)
    _allreduce_kernel(axis_names, nz, nc, streams, shifts, wg_s, t_s, wb_ref, g_s, mb_ref,
                      o_ref, res_ref, ig_ref, *ar_scratch, entry_barrier=False)


def fused_step(x, wf, f, mf, wb, mb, shifts, axis_names):
    nc = lax.axis_size("chan")
    nz = lax.axis_size("dp") // 4
    rows_x, cols = x.shape
    cin, taps = f.shape[0], len(shifts)
    cout = rows_x * nc
    rows, width = taps * cin, cout
    owned = cout // nc
    half = rows // 2
    chunk = half // nz
    lanes = width // 2
    n_copies = nz + 3 + 6 * (nz - 1) * STREAMS
    vmem = pltpu.VMEM
    f32 = jnp.float32
    return pl.pallas_call(
        functools.partial(_fused_kernel, axis_names, nz, nc, STREAMS, shifts),
        out_shape=(
            jax.ShapeDtypeStruct((rows, width), f32),
            jax.ShapeDtypeStruct((owned, cols), jnp.bfloat16),
            jax.ShapeDtypeStruct((cin, cols), jnp.bfloat16),
        ),
        in_specs=[pl.BlockSpec(memory_space=vmem)] * 6,
        out_specs=(pl.BlockSpec(memory_space=vmem),) * 3,
        scratch_shapes=[
            vmem((cout, cols), x.dtype),
            vmem((cout, cols), f32),
            vmem((rows, width), f32),
            vmem((taps,) + f.shape, f.dtype),
            pltpu.SemaphoreType.DMA((nc,)),
            pltpu.SemaphoreType.DMA((nc,)),
            vmem((half, width), f32),
            vmem((half, width), f32),
            vmem((chunk, width), f32),
            vmem((chunk, width), f32),
            vmem((nz - 1, chunk, lanes), f32),
            vmem((nz - 1, chunk, lanes), f32),
            vmem((nz - 1, chunk, lanes), f32),
            vmem((nz - 1, chunk, lanes), f32),
            vmem((nc, owned, cols), f32),
            vmem((cin, cols), f32),
            pltpu.SemaphoreType.DMA((n_copies,)),
            pltpu.SemaphoreType.DMA((n_copies,)),
            pltpu.SemaphoreType.DMA((nc,)),
            pltpu.SemaphoreType.DMA((nc,)),
        ],
        compiler_params=pltpu.CompilerParams(
            collective_id=0, has_side_effects=True, vmem_limit_bytes=56 * 1024 * 1024
        ),
    )(x, wf, f, mf, wb, mb)


def on_device(axis_names, inputs, weight, cotangent):
    input_channels_local = inputs.shape[1]
    cout_local = cotangent.shape[1]
    tap_locations = MAP_HEIGHT * MAP_WIDTH
    feature_map = inputs[0].reshape(input_channels_local, MAP_HEIGHT, MAP_WIDTH)
    tap_list = weight.shape[1]
    output_channels_total = weight.shape[2]
    tap_shifts = [
        (DILATION_RATE * (tap_index // 3 - 1), DILATION_RATE * (tap_index % 3 - 1))
        for tap_index in range(tap_list)
    ]
    rows_idx = np.arange(tap_locations) // MAP_WIDTH
    cols_idx = np.arange(tap_locations) % MAP_WIDTH
    masks = np.stack(
        [
            ((rows_idx + a >= 0) & (rows_idx + a < MAP_HEIGHT) & (cols_idx + b >= 0) & (cols_idx + b < MAP_WIDTH))
            for a, b in tap_shifts
        ]
    ).astype(np.float32)
    back_masks = np.stack(
        [
            ((rows_idx - a >= 0) & (rows_idx - a < MAP_HEIGHT) & (cols_idx - b >= 0) & (cols_idx - b < MAP_WIDTH))
            for a, b in tap_shifts
        ]
    ).astype(np.float32)
    summed, owned, back = fused_step(
        cotangent[0],
        jnp.transpose(weight, (1, 2, 0)),
        inputs[0],
        jnp.asarray(masks),
        jnp.transpose(weight, (1, 0, 2)),
        jnp.asarray(back_masks),
        tuple(a * MAP_WIDTH + b for a, b in tap_shifts),
        axis_names,
    )
    result = owned.reshape(1, cout_local, tap_locations)
    summed_grad = jnp.transpose(
        summed.reshape(tap_list, input_channels_local, output_channels_total), (1, 0, 2)
    )
    weight_grad = summed_grad / jnp.float32(lax.axis_size("dp"))
    input_grad = back.reshape(1, input_channels_local, tap_locations)
    return (result, input_grad, weight_grad)


def solution(mesh):
    placed = (P("dp", "chan", None), P("chan", None, None), P("dp", "chan", None))
    return jax.shard_map(
        functools.partial(on_device, tuple(mesh.axis_names)),
        mesh=mesh,
        in_specs=placed,
        out_specs=(P("dp", "chan", None), P("dp", "chan", None), P("chan", None, None)),
        check_vma=False,
    )
```

```python
import functools

import jax
import jax.numpy as jnp
import numpy as np
from jax import lax
from jax.experimental import pallas as pl
from jax.experimental.pallas import tpu as pltpu
from jax.sharding import PartitionSpec as P

DILATION_RATE = 12
MAP_HEIGHT = 16
MAP_WIDTH = 72
STREAMS = 3


def translated_input(receptive_field, row_shift, column_shift, reach):
    height, width = (receptive_field.shape[1], receptive_field.shape[2])
    bordered_input = jnp.pad(receptive_field, ((0, 0), (reach, reach), (reach, reach)))
    return bordered_input[
        :,
        reach + row_shift : reach + row_shift + height,
        reach + column_shift : reach + column_shift + width,
    ]


def _allreduce_kernel(axis_names, nz, nc, streams, shifts, a_ref, t_ref, w_ref, g_ref, m_ref,
                      o_ref, res_ref, ig_ref, rc, s1, f1, rx, rp, rm, ap, am, rs_buf, ig_acc,
                      send_sems, recv_sems, rs_send, rs_recv, entry_barrier=True):
    rows, cols = a_ref.shape
    half = rows // 2
    chunk = half // nz
    lanes = cols // 2
    MESH = pl.DeviceIdType.MESH
    dp = lax.axis_index("dp")
    core = dp % 2
    xl = (dp // 2) % 2
    z = dp // 4
    nd = 4 * nz
    pc = dp + 1 - 2 * core
    px = dp + 2 - 4 * xl
    zr = (dp + 4) % nd
    zl = (dp + nd - 4) % nd

    me = lax.axis_index("chan")

    def dev(p):
        return tuple(p if n == "dp" else lax.axis_index(n) for n in axis_names)

    def cdev(p):
        return tuple(p if n == "chan" else lax.axis_index(n) for n in axis_names)

    if entry_barrier:
        barrier = pltpu.get_barrier_semaphore()
        for peer in (pc, px, zr, zl):
            pl.semaphore_signal(barrier, inc=1, device_id=dev(peer), device_id_type=MESH)
        for k in range(1, nc):
            pl.semaphore_signal(barrier, inc=1, device_id=cdev((me + k) % nc), device_id_type=MESH)
        pl.semaphore_wait(barrier, 4 + nc - 1)

    owned = res_ref.shape[0]
    rs_copies = []
    for k in range(1, nc):
        peer = (me + k) % nc
        c = pltpu.make_async_remote_copy(
            src_ref=t_ref.at[pl.ds(pl.multiple_of(peer * owned, 8), owned)],
            dst_ref=rs_buf.at[k], send_sem=rs_send.at[k], recv_sem=rs_recv.at[k],
            device_id=cdev(peer), device_id_type=MESH)
        c.start()
        rs_copies.append(c)

    sent = []
    counter = [0]

    def remote(src, dst, peer):
        k = counter[0]
        counter[0] += 1
        c = pltpu.make_async_remote_copy(
            src_ref=src, dst_ref=dst, send_sem=send_sems.at[k], recv_sem=recv_sems.at[k],
            device_id=dev(peer), device_id_type=MESH)
        c.start()
        sent.append(c)
        return c

    def rows_of(j):
        return pl.ds(pl.multiple_of(j * chunk, 8), chunk)

    done_taps = [0]
    size = g_ref.shape[1]

    def input_grad_tap():
        t = done_taps[0]
        if t < len(shifts):
            y = jnp.dot(w_ref[t], g_ref[...], preferred_element_type=jnp.float32)
            if shifts[t] % size:
                y = pltpu.roll(y, shifts[t] % size, 1)
            y = y * m_ref[pl.ds(t, 1), :]
            if t == 0:
                ig_acc[...] = y
            elif t == len(shifts) - 1:
                ig_ref[...] = (ig_acc[...] + y).astype(ig_ref.dtype)
            else:
                ig_acc[...] += y
            done_taps[0] += 1

    mine_c = core * half
    other_c = (1 - core) * half
    order = []
    for d in range(1, nz // 2 + 1):
        order.append((z + nz - d) % nz)
        if 2 * d != nz:
            order.append((z + d) % nz)
    order.append(z)
    core_in = []
    for j in order:
        src_rows = pl.ds(pl.multiple_of(other_c + j * chunk, 8), chunk)
        core_in.append((j, remote(a_ref.at[src_rows], rc.at[rows_of(j)], pc)))
    ready = [0]

    def ready_upto(n):
        while ready[0] < n:
            j, c = core_in[ready[0]]
            c.wait_recv()
            own_rows = pl.ds(pl.multiple_of(mine_c + j * chunk, 8), chunk)
            s1[rows_of(j), :] = a_ref[own_rows, :] + rc[rows_of(j), :]
            ready[0] += 1

    def needed(d):
        return min(len(order) - 1, 2 * d - (1 if 2 * d == nz else 0))

    lo = pl.ds(0, lanes)
    hi = pl.ds(lanes, lanes)
    sub = chunk // streams

    def srows(j, q):
        return pl.ds(pl.multiple_of(j * chunk + q * sub, 8), sub)

    blk = [pl.ds(q * sub, sub) for q in range(streams)]
    pending = [None] * streams
    for s in range(nz - 1):
        jp = (z + 2 * nz - 1 - s) % nz
        jm = (z + 1 + s) % nz
        if s + 1 <= nz // 2:
            ready_upto(needed(s + 1))
        for q in range(streams):
            if s == 0:
                src_p = s1.at[srows(jp, q), lo]
                src_m = s1.at[srows(jm, q), hi]
            else:
                pending[q][0].wait_recv()
                pending[q][1].wait_recv()
                ap[s, blk[q], :] = s1[srows(jp, q), lo] + rp[s - 1, blk[q], :]
                am[s, blk[q], :] = s1[srows(jm, q), hi] + rm[s - 1, blk[q], :]
                src_p = ap.at[s, blk[q]]
                src_m = am.at[s, blk[q]]
            pending[q] = (remote(src_p, rp.at[s, blk[q]], zr), remote(src_m, rm.at[s, blk[q]], zl))
    for q in range(streams):
        pending[q][0].wait_recv()
        pending[q][1].wait_recv()
    ready_upto(len(order))
    f1[:, lo] = s1[rows_of(z), lo] + rp[nz - 2]
    f1[:, hi] = s1[rows_of(z), hi] + rm[nz - 2]

    c = remote(f1, rx, px)
    c.wait_recv()
    own_chunk = pl.ds(pl.multiple_of(core * half + z * chunk, 8), chunk)
    o_ref[own_chunk, :] = f1[...] + rx[...]

    to_core = [remote(o_ref.at[own_chunk], o_ref.at[own_chunk], pc)]

    def grows(j, q):
        return pl.ds(pl.multiple_of(core * half + j * chunk + q * sub, 8), sub)

    def arrived(q, jp, jm):
        pending[q][0].wait_recv()
        pending[q][1].wait_recv()
        gp = grows((jp + nz - 1) % nz, q)
        gm = grows((jm + 1) % nz, q)
        to_core.append(remote(o_ref.at[gp, lo], o_ref.at[gp, lo], pc))
        to_core.append(remote(o_ref.at[gm, hi], o_ref.at[gm, hi], pc))

    for s in range(nz - 1):
        jp = (z + nz - s) % nz
        jm = (z + s) % nz
        for q in range(streams):
            if s > 0:
                arrived(q, (jp + 1) % nz, (jm + nz - 1) % nz)
            gp = grows(jp, q)
            gm = grows(jm, q)
            pending[q] = (remote(o_ref.at[gp, lo], o_ref.at[gp, lo], zr),
                          remote(o_ref.at[gm, hi], o_ref.at[gm, hi], zl))
        input_grad_tap()
        if s == nz - 2:
            while done_taps[0] < len(shifts):
                input_grad_tap()
    for q in range(streams):
        arrived(q, (z + 2) % nz, (z + nz - 2) % nz)
    for c in to_core:
        c.wait_recv()

    for c in rs_copies:
        c.wait_recv()
    acc = t_ref[pl.ds(pl.multiple_of(me * owned, 8), owned), :]
    for k in range(1, nc):
        acc = acc + rs_buf[k]
    res_ref[...] = acc.astype(res_ref.dtype)

    for c in sent + rs_copies:
        c.wait_send()


def dp_allreduce(a, t, w, g, masks, shifts, axis_names):
    rows, cols = a.shape
    nc = lax.axis_size("chan")
    owned = t.shape[0] // nc
    nz = lax.axis_size("dp") // 4
    half = rows // 2
    chunk = half // nz
    lanes = cols // 2
    n_copies = nz + 3 + 6 * (nz - 1) * STREAMS
    vmem = pltpu.VMEM
    return pl.pallas_call(
        functools.partial(_allreduce_kernel, axis_names, nz, nc, STREAMS, shifts),
        out_shape=(
            jax.ShapeDtypeStruct((rows, cols), a.dtype),
            jax.ShapeDtypeStruct((owned, t.shape[1]), jnp.bfloat16),
            jax.ShapeDtypeStruct((w.shape[1], g.shape[1]), jnp.bfloat16),
        ),
        in_specs=[pl.BlockSpec(memory_space=vmem)] * 5,
        out_specs=(pl.BlockSpec(memory_space=vmem),) * 3,
        scratch_shapes=[
            vmem((half, cols), a.dtype),
            vmem((half, cols), a.dtype),
            vmem((chunk, cols), a.dtype),
            vmem((chunk, cols), a.dtype),
            vmem((nz - 1, chunk, lanes), a.dtype),
            vmem((nz - 1, chunk, lanes), a.dtype),
            vmem((nz - 1, chunk, lanes), a.dtype),
            vmem((nz - 1, chunk, lanes), a.dtype),
            vmem((nc, owned, t.shape[1]), t.dtype),
            vmem((w.shape[1], g.shape[1]), jnp.float32),
            pltpu.SemaphoreType.DMA((n_copies,)),
            pltpu.SemaphoreType.DMA((n_copies,)),
            pltpu.SemaphoreType.DMA((nc,)),
            pltpu.SemaphoreType.DMA((nc,)),
        ],
        compiler_params=pltpu.CompilerParams(
            collective_id=0, has_side_effects=True, vmem_limit_bytes=48 * 1024 * 1024
        ),
    )(a, t, w, g, masks)


def _allgather_kernel(axis_names, n, shifts, x_ref, w_ref, f_ref, m_ref, o_ref, t_ref, wg_ref,
                      xs, send_sems, recv_sems, entry_barrier=True):
    rows = x_ref.shape[0]
    MESH = pl.DeviceIdType.MESH
    me = lax.axis_index("chan")

    def dev(p):
        return tuple(p if a == "chan" else lax.axis_index(a) for a in axis_names)

    if entry_barrier:
        barrier = pltpu.get_barrier_semaphore()
        for k in range(1, n):
            pl.semaphore_signal(barrier, inc=1, device_id=dev((me + k) % n), device_id_type=MESH)
        pl.semaphore_wait(barrier, n - 1)

    mine = pl.ds(pl.multiple_of(me * rows, 16), rows)
    copies = []
    for k in range(1, n):
        peer = (me + k) % n
        c = pltpu.make_async_remote_copy(
            src_ref=x_ref, dst_ref=o_ref.at[mine], send_sem=send_sems.at[k],
            recv_sem=recv_sems.at[k], device_id=dev(peer), device_id_type=MESH)
        c.start()
        copies.append(c)
    o_ref[mine, :] = x_ref[...]
    size = f_ref.shape[1]
    for t, shift in enumerate(shifts):
        y = jnp.dot(w_ref[t], f_ref[...], preferred_element_type=jnp.float32)
        if shift % size:
            y = pltpu.roll(y, (-shift) % size, 1)
        y = y * m_ref[pl.ds(t, 1), :]
        if t == 0:
            t_ref[...] = y
        else:
            t_ref[...] += y
    wide = f_ref[...].astype(jnp.float32)
    for t, shift in enumerate(shifts):
        v = pltpu.roll(wide, (-shift) % size, 1) if shift % size else wide
        xs[t] = (v * m_ref[pl.ds(t, 1), :]).astype(xs.dtype)
    for k in range(1, n):
        src = (me + n - k) % n
        theirs = pl.ds(pl.multiple_of(src * rows, 16), rows)
        pltpu.make_async_remote_copy(
            src_ref=x_ref, dst_ref=o_ref.at[theirs], send_sem=send_sems.at[k],
            recv_sem=recv_sems.at[k], device_id=dev(src), device_id_type=MESH).wait_recv()
    cin = f_ref.shape[0]
    for t in range(len(shifts)):
        wg_ref[pl.ds(t * cin, cin), :] = lax.dot_general(
            xs[t], o_ref[...], (((1,), (1,)), ((), ())), preferred_element_type=jnp.float32)
    for c in copies:
        c.wait_send()


def chan_allgather(x, axis_names, w, f, masks, shifts):
    rows, cols = x.shape
    n = lax.axis_size("chan")
    vmem = pltpu.VMEM
    return pl.pallas_call(
        functools.partial(_allgather_kernel, axis_names, n, shifts),
        out_shape=(
            jax.ShapeDtypeStruct((rows * n, cols), x.dtype),
            jax.ShapeDtypeStruct((w.shape[1], f.shape[1]), jnp.float32),
            jax.ShapeDtypeStruct((len(shifts) * f.shape[0], rows * n), jnp.float32),
        ),
        in_specs=[pl.BlockSpec(memory_space=vmem)] * 4,
        out_specs=(pl.BlockSpec(memory_space=vmem),) * 3,
        scratch_shapes=[
            vmem((len(shifts),) + f.shape, f.dtype),
            pltpu.SemaphoreType.DMA((n,)),
            pltpu.SemaphoreType.DMA((n,)),
        ],
        compiler_params=pltpu.CompilerParams(
            collective_id=1, has_side_effects=True, vmem_limit_bytes=48 * 1024 * 1024
        ),
    )(x, w, f, masks)


def _fused_kernel(axis_names, nz, nc, streams, shifts, x_ref, wf_ref, f_ref, mf_ref, wb_ref, mb_ref,
                  o_ref, res_ref, ig_ref, g_s, t_s, wg_s, xs, ag_send, ag_recv, *ar_scratch):
    MESH = pl.DeviceIdType.MESH
    dp = lax.axis_index("dp")
    me = lax.axis_index("chan")
    nd = 4 * nz
    core = dp % 2
    xl = (dp // 2) % 2
    peers = (dp + 1 - 2 * core, dp + 2 - 4 * xl, (dp + 4) % nd, (dp + nd - 4) % nd)
    barrier = pltpu.get_barrier_semaphore()
    for peer in peers:
        pl.semaphore_signal(barrier, inc=1, device_id=tuple(peer if a == "dp" else lax.axis_index(a) for a in axis_names), device_id_type=MESH)
    for k in range(1, nc):
        pl.semaphore_signal(barrier, inc=1, device_id=tuple((me + k) % nc if a == "chan" else lax.axis_index(a) for a in axis_names), device_id_type=MESH)
    pl.semaphore_wait(barrier, 4 + nc - 1)
    _allgather_kernel(axis_names, nc, shifts, x_ref, wf_ref, f_ref, mf_ref, g_s, t_s, wg_s, xs,
                      ag_send, ag_recv, entry_barrier=False)
    _allreduce_kernel(axis_names, nz, nc, streams, shifts, wg_s, t_s, wb_ref, g_s, mb_ref,
                      o_ref, res_ref, ig_ref, *ar_scratch, entry_barrier=False)


def fused_step(x, wf, f, mf, wb, mb, shifts, axis_names):
    nc = lax.axis_size("chan")
    nz = lax.axis_size("dp") // 4
    rows_x, cols = x.shape
    cin, taps = f.shape[0], len(shifts)
    cout = rows_x * nc
    rows, width = taps * cin, cout
    owned = cout // nc
    half = rows // 2
    chunk = half // nz
    lanes = width // 2
    n_copies = nz + 3 + 6 * (nz - 1) * STREAMS
    vmem = pltpu.VMEM
    f32 = jnp.float32
    return pl.pallas_call(
        functools.partial(_fused_kernel, axis_names, nz, nc, STREAMS, shifts),
        out_shape=(
            jax.ShapeDtypeStruct((rows, width), f32),
            jax.ShapeDtypeStruct((owned, cols), jnp.bfloat16),
            jax.ShapeDtypeStruct((cin, cols), jnp.bfloat16),
        ),
        in_specs=[pl.BlockSpec(memory_space=vmem)] * 6,
        out_specs=(pl.BlockSpec(memory_space=vmem),) * 3,
        scratch_shapes=[
            vmem((cout, cols), x.dtype),
            vmem((cout, cols), f32),
            vmem((rows, width), f32),
            vmem((taps,) + f.shape, f.dtype),
            pltpu.SemaphoreType.DMA((nc,)),
            pltpu.SemaphoreType.DMA((nc,)),
            vmem((half, width), f32),
            vmem((half, width), f32),
            vmem((chunk, width), f32),
            vmem((chunk, width), f32),
            vmem((nz - 1, chunk, lanes), f32),
            vmem((nz - 1, chunk, lanes), f32),
            vmem((nz - 1, chunk, lanes), f32),
            vmem((nz - 1, chunk, lanes), f32),
            vmem((nc, owned, cols), f32),
            vmem((cin, cols), f32),
            pltpu.SemaphoreType.DMA((n_copies,)),
            pltpu.SemaphoreType.DMA((n_copies,)),
            pltpu.SemaphoreType.DMA((nc,)),
            pltpu.SemaphoreType.DMA((nc,)),
        ],
        compiler_params=pltpu.CompilerParams(
            collective_id=0, has_side_effects=True, vmem_limit_bytes=56 * 1024 * 1024
        ),
    )(x, wf, f, mf, wb, mb)


def on_device(axis_names, inputs, weight, cotangent):
    input_channels_local = inputs.shape[1]
    cout_local = cotangent.shape[1]
    tap_locations = MAP_HEIGHT * MAP_WIDTH
    feature_map = inputs[0].reshape(input_channels_local, MAP_HEIGHT, MAP_WIDTH)
    tap_list = weight.shape[1]
    output_channels_total = weight.shape[2]
    tap_shifts = [
        (DILATION_RATE * (tap_index // 3 - 1), DILATION_RATE * (tap_index % 3 - 1))
        for tap_index in range(tap_list)
    ]
    rows_idx = np.arange(tap_locations) // MAP_WIDTH
    cols_idx = np.arange(tap_locations) % MAP_WIDTH
    masks = np.stack(
        [
            ((rows_idx + a >= 0) & (rows_idx + a < MAP_HEIGHT) & (cols_idx + b >= 0) & (cols_idx + b < MAP_WIDTH))
            for a, b in tap_shifts
        ]
    ).astype(np.float32)
    back_masks = np.stack(
        [
            ((rows_idx - a >= 0) & (rows_idx - a < MAP_HEIGHT) & (cols_idx - b >= 0) & (cols_idx - b < MAP_WIDTH))
            for a, b in tap_shifts
        ]
    ).astype(np.float32)
    summed, owned, back = fused_step(
        cotangent[0],
        jnp.transpose(weight, (1, 2, 0)),
        inputs[0],
        jnp.asarray(masks),
        jnp.transpose(weight, (1, 0, 2)),
        jnp.asarray(back_masks),
        tuple(a * MAP_WIDTH + b for a, b in tap_shifts),
        axis_names,
    )
    result = owned.reshape(1, cout_local, tap_locations)
    summed_grad = jnp.transpose(
        summed.reshape(tap_list, input_channels_local, output_channels_total), (1, 0, 2)
    )
    weight_grad = summed_grad / jnp.float32(lax.axis_size("dp"))
    input_grad = back.reshape(1, input_channels_local, tap_locations)
    return (result, input_grad, weight_grad)


def solution(mesh):
    placed = (P("dp", "chan", None), P("chan", None, None), P("dp", "chan", None))
    return jax.shard_map(
        functools.partial(on_device, tuple(mesh.axis_names)),
        mesh=mesh,
        in_specs=placed,
        out_specs=(P("dp", "chan", None), P("dp", "chan", None), P("chan", None, None)),
        check_vma=False,
    )
```

```python
import functools

import jax
import jax.numpy as jnp
import numpy as np
from jax import lax
from jax.experimental import pallas as pl
from jax.experimental.pallas import tpu as pltpu
from jax.sharding import PartitionSpec as P

DILATION_RATE = 12
MAP_HEIGHT = 16
MAP_WIDTH = 72
STREAMS = 3


def translated_input(receptive_field, row_shift, column_shift, reach):
    height, width = (receptive_field.shape[1], receptive_field.shape[2])
    bordered_input = jnp.pad(receptive_field, ((0, 0), (reach, reach), (reach, reach)))
    return bordered_input[
        :,
        reach + row_shift : reach + row_shift + height,
        reach + column_shift : reach + column_shift + width,
    ]


def _allreduce_kernel(axis_names, nz, nc, streams, shifts, a_ref, t_ref, w_ref, g_ref, m_ref,
                      o_ref, res_ref, ig_ref, rc, s1, f1, rx, rp, rm, ap, am, rs_buf, ig_acc,
                      send_sems, recv_sems, rs_send, rs_recv, entry_barrier=True):
    rows, cols = a_ref.shape
    half = rows // 2
    chunk = half // nz
    lanes = cols // 2
    MESH = pl.DeviceIdType.MESH
    dp = lax.axis_index("dp")
    core = dp % 2
    xl = (dp // 2) % 2
    z = dp // 4
    nd = 4 * nz
    pc = dp + 1 - 2 * core
    px = dp + 2 - 4 * xl
    zr = (dp + 4) % nd
    zl = (dp + nd - 4) % nd

    me = lax.axis_index("chan")

    def dev(p):
        return tuple(p if n == "dp" else lax.axis_index(n) for n in axis_names)

    def cdev(p):
        return tuple(p if n == "chan" else lax.axis_index(n) for n in axis_names)

    if entry_barrier:
        barrier = pltpu.get_barrier_semaphore()
        for peer in (pc, px, zr, zl):
            pl.semaphore_signal(barrier, inc=1, device_id=dev(peer), device_id_type=MESH)
        for k in range(1, nc):
            pl.semaphore_signal(barrier, inc=1, device_id=cdev((me + k) % nc), device_id_type=MESH)
        pl.semaphore_wait(barrier, 4 + nc - 1)

    owned = res_ref.shape[0]
    rs_copies = []
    for k in range(1, nc):
        peer = (me + k) % nc
        c = pltpu.make_async_remote_copy(
            src_ref=t_ref.at[pl.ds(pl.multiple_of(peer * owned, 8), owned)],
            dst_ref=rs_buf.at[k], send_sem=rs_send.at[k], recv_sem=rs_recv.at[k],
            device_id=cdev(peer), device_id_type=MESH)
        c.start()
        rs_copies.append(c)

    sent = []
    counter = [0]

    def remote(src, dst, peer):
        k = counter[0]
        counter[0] += 1
        c = pltpu.make_async_remote_copy(
            src_ref=src, dst_ref=dst, send_sem=send_sems.at[k], recv_sem=recv_sems.at[k],
            device_id=dev(peer), device_id_type=MESH)
        c.start()
        sent.append(c)
        return c

    def rows_of(j):
        return pl.ds(pl.multiple_of(j * chunk, 8), chunk)

    done_taps = [0]
    size = g_ref.shape[1]

    def input_grad_tap():
        t = done_taps[0]
        if t < len(shifts):
            y = jnp.dot(w_ref[t], g_ref[...], preferred_element_type=jnp.float32)
            if shifts[t] % size:
                y = pltpu.roll(y, shifts[t] % size, 1)
            y = y * m_ref[pl.ds(t, 1), :]
            if t == 0:
                ig_acc[...] = y
            elif t == len(shifts) - 1:
                ig_ref[...] = (ig_acc[...] + y).astype(ig_ref.dtype)
            else:
                ig_acc[...] += y
            done_taps[0] += 1

    mine_c = core * half
    other_c = (1 - core) * half
    order = []
    for d in range(1, nz // 2 + 1):
        order.append((z + nz - d) % nz)
        if 2 * d != nz:
            order.append((z + d) % nz)
    order.append(z)
    core_in = []
    for j in order:
        src_rows = pl.ds(pl.multiple_of(other_c + j * chunk, 8), chunk)
        core_in.append((j, remote(a_ref.at[src_rows], rc.at[rows_of(j)], pc)))
    ready = [0]

    def ready_upto(n):
        while ready[0] < n:
            j, c = core_in[ready[0]]
            c.wait_recv()
            own_rows = pl.ds(pl.multiple_of(mine_c + j * chunk, 8), chunk)
            s1[rows_of(j), :] = a_ref[own_rows, :] + rc[rows_of(j), :]
            ready[0] += 1

    def needed(d):
        return min(len(order) - 1, 2 * d - (1 if 2 * d == nz else 0))

    lo = pl.ds(0, lanes)
    hi = pl.ds(lanes, lanes)
    sub = chunk // streams

    def srows(j, q):
        return pl.ds(pl.multiple_of(j * chunk + q * sub, 8), sub)

    blk = [pl.ds(q * sub, sub) for q in range(streams)]
    pending = [None] * streams
    for s in range(nz - 1):
        jp = (z + 2 * nz - 1 - s) % nz
        jm = (z + 1 + s) % nz
        if s + 1 <= nz // 2:
            ready_upto(needed(s + 1))
        for q in range(streams):
            if s == 0:
                src_p = s1.at[srows(jp, q), lo]
                src_m = s1.at[srows(jm, q), hi]
            else:
                pending[q][0].wait_recv()
                pending[q][1].wait_recv()
                ap[s, blk[q], :] = s1[srows(jp, q), lo] + rp[s - 1, blk[q], :]
                am[s, blk[q], :] = s1[srows(jm, q), hi] + rm[s - 1, blk[q], :]
                src_p = ap.at[s, blk[q]]
                src_m = am.at[s, blk[q]]
            pending[q] = (remote(src_p, rp.at[s, blk[q]], zr), remote(src_m, rm.at[s, blk[q]], zl))
    for q in range(streams):
        pending[q][0].wait_recv()
        pending[q][1].wait_recv()
    ready_upto(len(order))
    f1[:, lo] = s1[rows_of(z), lo] + rp[nz - 2]
    f1[:, hi] = s1[rows_of(z), hi] + rm[nz - 2]

    c = remote(f1, rx, px)
    c.wait_recv()
    own_chunk = pl.ds(pl.multiple_of(core * half + z * chunk, 8), chunk)
    o_ref[own_chunk, :] = f1[...] + rx[...]

    to_core = [remote(o_ref.at[own_chunk], o_ref.at[own_chunk], pc)]

    def grows(j, q):
        return pl.ds(pl.multiple_of(core * half + j * chunk + q * sub, 8), sub)

    def arrived(q, jp, jm):
        pending[q][0].wait_recv()
        pending[q][1].wait_recv()
        gp = grows((jp + nz - 1) % nz, q)
        gm = grows((jm + 1) % nz, q)
        to_core.append(remote(o_ref.at[gp, lo], o_ref.at[gp, lo], pc))
        to_core.append(remote(o_ref.at[gm, hi], o_ref.at[gm, hi], pc))

    for s in range(nz - 1):
        jp = (z + nz - s) % nz
        jm = (z + s) % nz
        for q in range(streams):
            if s > 0:
                arrived(q, (jp + 1) % nz, (jm + nz - 1) % nz)
            gp = grows(jp, q)
            gm = grows(jm, q)
            pending[q] = (remote(o_ref.at[gp, lo], o_ref.at[gp, lo], zr),
                          remote(o_ref.at[gm, hi], o_ref.at[gm, hi], zl))
        input_grad_tap()
        if s == 0:
            for c in rs_copies:
                c.wait_recv()
            acc = t_ref[pl.ds(pl.multiple_of(me * owned, 8), owned), :]
            for k in range(1, nc):
                acc = acc + rs_buf[k]
            res_ref[...] = acc.astype(res_ref.dtype)
        if s == nz - 2:
            while done_taps[0] < len(shifts):
                input_grad_tap()
    for q in range(streams):
        arrived(q, (z + 2) % nz, (z + nz - 2) % nz)
    for c in to_core:
        c.wait_recv()


    for c in sent + rs_copies:
        c.wait_send()


def dp_allreduce(a, t, w, g, masks, shifts, axis_names):
    rows, cols = a.shape
    nc = lax.axis_size("chan")
    owned = t.shape[0] // nc
    nz = lax.axis_size("dp") // 4
    half = rows // 2
    chunk = half // nz
    lanes = cols // 2
    n_copies = nz + 3 + 6 * (nz - 1) * STREAMS
    vmem = pltpu.VMEM
    return pl.pallas_call(
        functools.partial(_allreduce_kernel, axis_names, nz, nc, STREAMS, shifts),
        out_shape=(
            jax.ShapeDtypeStruct((rows, cols), a.dtype),
            jax.ShapeDtypeStruct((owned, t.shape[1]), jnp.bfloat16),
            jax.ShapeDtypeStruct((w.shape[1], g.shape[1]), jnp.bfloat16),
        ),
        in_specs=[pl.BlockSpec(memory_space=vmem)] * 5,
        out_specs=(pl.BlockSpec(memory_space=vmem),) * 3,
        scratch_shapes=[
            vmem((half, cols), a.dtype),
            vmem((half, cols), a.dtype),
            vmem((chunk, cols), a.dtype),
            vmem((chunk, cols), a.dtype),
            vmem((nz - 1, chunk, lanes), a.dtype),
            vmem((nz - 1, chunk, lanes), a.dtype),
            vmem((nz - 1, chunk, lanes), a.dtype),
            vmem((nz - 1, chunk, lanes), a.dtype),
            vmem((nc, owned, t.shape[1]), t.dtype),
            vmem((w.shape[1], g.shape[1]), jnp.float32),
            pltpu.SemaphoreType.DMA((n_copies,)),
            pltpu.SemaphoreType.DMA((n_copies,)),
            pltpu.SemaphoreType.DMA((nc,)),
            pltpu.SemaphoreType.DMA((nc,)),
        ],
        compiler_params=pltpu.CompilerParams(
            collective_id=0, has_side_effects=True, vmem_limit_bytes=48 * 1024 * 1024
        ),
    )(a, t, w, g, masks)


def _allgather_kernel(axis_names, n, shifts, x_ref, w_ref, f_ref, m_ref, o_ref, t_ref, wg_ref,
                      xs, send_sems, recv_sems, entry_barrier=True):
    rows = x_ref.shape[0]
    MESH = pl.DeviceIdType.MESH
    me = lax.axis_index("chan")

    def dev(p):
        return tuple(p if a == "chan" else lax.axis_index(a) for a in axis_names)

    if entry_barrier:
        barrier = pltpu.get_barrier_semaphore()
        for k in range(1, n):
            pl.semaphore_signal(barrier, inc=1, device_id=dev((me + k) % n), device_id_type=MESH)
        pl.semaphore_wait(barrier, n - 1)

    mine = pl.ds(pl.multiple_of(me * rows, 16), rows)
    copies = []
    for k in range(1, n):
        peer = (me + k) % n
        c = pltpu.make_async_remote_copy(
            src_ref=x_ref, dst_ref=o_ref.at[mine], send_sem=send_sems.at[k],
            recv_sem=recv_sems.at[k], device_id=dev(peer), device_id_type=MESH)
        c.start()
        copies.append(c)
    o_ref[mine, :] = x_ref[...]
    size = f_ref.shape[1]
    for t, shift in enumerate(shifts):
        y = jnp.dot(w_ref[t], f_ref[...], preferred_element_type=jnp.float32)
        if shift % size:
            y = pltpu.roll(y, (-shift) % size, 1)
        y = y * m_ref[pl.ds(t, 1), :]
        if t == 0:
            t_ref[...] = y
        else:
            t_ref[...] += y
    wide = f_ref[...].astype(jnp.float32)
    for t, shift in enumerate(shifts):
        v = pltpu.roll(wide, (-shift) % size, 1) if shift % size else wide
        xs[t] = (v * m_ref[pl.ds(t, 1), :]).astype(xs.dtype)
    for k in range(1, n):
        src = (me + n - k) % n
        theirs = pl.ds(pl.multiple_of(src * rows, 16), rows)
        pltpu.make_async_remote_copy(
            src_ref=x_ref, dst_ref=o_ref.at[theirs], send_sem=send_sems.at[k],
            recv_sem=recv_sems.at[k], device_id=dev(src), device_id_type=MESH).wait_recv()
    cin = f_ref.shape[0]
    for t in range(len(shifts)):
        wg_ref[pl.ds(t * cin, cin), :] = lax.dot_general(
            xs[t], o_ref[...], (((1,), (1,)), ((), ())), preferred_element_type=jnp.float32)
    for c in copies:
        c.wait_send()


def chan_allgather(x, axis_names, w, f, masks, shifts):
    rows, cols = x.shape
    n = lax.axis_size("chan")
    vmem = pltpu.VMEM
    return pl.pallas_call(
        functools.partial(_allgather_kernel, axis_names, n, shifts),
        out_shape=(
            jax.ShapeDtypeStruct((rows * n, cols), x.dtype),
            jax.ShapeDtypeStruct((w.shape[1], f.shape[1]), jnp.float32),
            jax.ShapeDtypeStruct((len(shifts) * f.shape[0], rows * n), jnp.float32),
        ),
        in_specs=[pl.BlockSpec(memory_space=vmem)] * 4,
        out_specs=(pl.BlockSpec(memory_space=vmem),) * 3,
        scratch_shapes=[
            vmem((len(shifts),) + f.shape, f.dtype),
            pltpu.SemaphoreType.DMA((n,)),
            pltpu.SemaphoreType.DMA((n,)),
        ],
        compiler_params=pltpu.CompilerParams(
            collective_id=1, has_side_effects=True, vmem_limit_bytes=48 * 1024 * 1024
        ),
    )(x, w, f, masks)


def _fused_kernel(axis_names, nz, nc, streams, shifts, x_ref, wf_ref, f_ref, mf_ref, wb_ref, mb_ref,
                  o_ref, res_ref, ig_ref, g_s, t_s, wg_s, xs, ag_send, ag_recv, *ar_scratch):
    MESH = pl.DeviceIdType.MESH
    dp = lax.axis_index("dp")
    me = lax.axis_index("chan")
    nd = 4 * nz
    core = dp % 2
    xl = (dp // 2) % 2
    peers = (dp + 1 - 2 * core, dp + 2 - 4 * xl, (dp + 4) % nd, (dp + nd - 4) % nd)
    barrier = pltpu.get_barrier_semaphore()
    for peer in peers:
        pl.semaphore_signal(barrier, inc=1, device_id=tuple(peer if a == "dp" else lax.axis_index(a) for a in axis_names), device_id_type=MESH)
    for k in range(1, nc):
        pl.semaphore_signal(barrier, inc=1, device_id=tuple((me + k) % nc if a == "chan" else lax.axis_index(a) for a in axis_names), device_id_type=MESH)
    pl.semaphore_wait(barrier, 4 + nc - 1)
    _allgather_kernel(axis_names, nc, shifts, x_ref, wf_ref, f_ref, mf_ref, g_s, t_s, wg_s, xs,
                      ag_send, ag_recv, entry_barrier=False)
    _allreduce_kernel(axis_names, nz, nc, streams, shifts, wg_s, t_s, wb_ref, g_s, mb_ref,
                      o_ref, res_ref, ig_ref, *ar_scratch, entry_barrier=False)


def fused_step(x, wf, f, mf, wb, mb, shifts, axis_names):
    nc = lax.axis_size("chan")
    nz = lax.axis_size("dp") // 4
    rows_x, cols = x.shape
    cin, taps = f.shape[0], len(shifts)
    cout = rows_x * nc
    rows, width = taps * cin, cout
    owned = cout // nc
    half = rows // 2
    chunk = half // nz
    lanes = width // 2
    n_copies = nz + 3 + 6 * (nz - 1) * STREAMS
    vmem = pltpu.VMEM
    f32 = jnp.float32
    return pl.pallas_call(
        functools.partial(_fused_kernel, axis_names, nz, nc, STREAMS, shifts),
        out_shape=(
            jax.ShapeDtypeStruct((rows, width), f32),
            jax.ShapeDtypeStruct((owned, cols), jnp.bfloat16),
            jax.ShapeDtypeStruct((cin, cols), jnp.bfloat16),
        ),
        in_specs=[pl.BlockSpec(memory_space=vmem)] * 6,
        out_specs=(pl.BlockSpec(memory_space=vmem),) * 3,
        scratch_shapes=[
            vmem((cout, cols), x.dtype),
            vmem((cout, cols), f32),
            vmem((rows, width), f32),
            vmem((taps,) + f.shape, f.dtype),
            pltpu.SemaphoreType.DMA((nc,)),
            pltpu.SemaphoreType.DMA((nc,)),
            vmem((half, width), f32),
            vmem((half, width), f32),
            vmem((chunk, width), f32),
            vmem((chunk, width), f32),
            vmem((nz - 1, chunk, lanes), f32),
            vmem((nz - 1, chunk, lanes), f32),
            vmem((nz - 1, chunk, lanes), f32),
            vmem((nz - 1, chunk, lanes), f32),
            vmem((nc, owned, cols), f32),
            vmem((cin, cols), f32),
            pltpu.SemaphoreType.DMA((n_copies,)),
            pltpu.SemaphoreType.DMA((n_copies,)),
            pltpu.SemaphoreType.DMA((nc,)),
            pltpu.SemaphoreType.DMA((nc,)),
        ],
        compiler_params=pltpu.CompilerParams(
            collective_id=0, has_side_effects=True, vmem_limit_bytes=56 * 1024 * 1024
        ),
    )(x, wf, f, mf, wb, mb)


def on_device(axis_names, inputs, weight, cotangent):
    input_channels_local = inputs.shape[1]
    cout_local = cotangent.shape[1]
    tap_locations = MAP_HEIGHT * MAP_WIDTH
    feature_map = inputs[0].reshape(input_channels_local, MAP_HEIGHT, MAP_WIDTH)
    tap_list = weight.shape[1]
    output_channels_total = weight.shape[2]
    tap_shifts = [
        (DILATION_RATE * (tap_index // 3 - 1), DILATION_RATE * (tap_index % 3 - 1))
        for tap_index in range(tap_list)
    ]
    rows_idx = np.arange(tap_locations) // MAP_WIDTH
    cols_idx = np.arange(tap_locations) % MAP_WIDTH
    masks = np.stack(
        [
            ((rows_idx + a >= 0) & (rows_idx + a < MAP_HEIGHT) & (cols_idx + b >= 0) & (cols_idx + b < MAP_WIDTH))
            for a, b in tap_shifts
        ]
    ).astype(np.float32)
    back_masks = np.stack(
        [
            ((rows_idx - a >= 0) & (rows_idx - a < MAP_HEIGHT) & (cols_idx - b >= 0) & (cols_idx - b < MAP_WIDTH))
            for a, b in tap_shifts
        ]
    ).astype(np.float32)
    summed, owned, back = fused_step(
        cotangent[0],
        jnp.transpose(weight, (1, 2, 0)),
        inputs[0],
        jnp.asarray(masks),
        jnp.transpose(weight, (1, 0, 2)),
        jnp.asarray(back_masks),
        tuple(a * MAP_WIDTH + b for a, b in tap_shifts),
        axis_names,
    )
    result = owned.reshape(1, cout_local, tap_locations)
    summed_grad = jnp.transpose(
        summed.reshape(tap_list, input_channels_local, output_channels_total), (1, 0, 2)
    )
    weight_grad = summed_grad / jnp.float32(lax.axis_size("dp"))
    input_grad = back.reshape(1, input_channels_local, tap_locations)
    return (result, input_grad, weight_grad)


def solution(mesh):
    placed = (P("dp", "chan", None), P("chan", None, None), P("dp", "chan", None))
    return jax.shard_map(
        functools.partial(on_device, tuple(mesh.axis_names)),
        mesh=mesh,
        in_specs=placed,
        out_specs=(P("dp", "chan", None), P("dp", "chan", None), P("chan", None, None)),
        check_vma=False,
    )
```
